32 devices in a mesh: section: 2 (over x), dp: 4 (over z), mp: 4 (over y, core).
Axes of the slice: x: 2, y: 2, z: 4, core: 2. Of those that a mesh axis runs over, the one named last changes fastest.
Arguments:
- image: bfloat16 [16, 576, 768], P('dp', 'mp'), may hold values from -6 to 6
- text: bfloat16 [16, 800, 768], P('dp', 'mp'), may hold values from -6 to 6
- lengths: int32 [16], P('dp'), may hold values from 5 to 800, as said below
- image_cot: bfloat16 [16, 576, 768], P('dp', 'mp'), may hold values from -6 to 6
- text_cot: bfloat16 [16, 800, 768], P('dp', 'mp'), may hold values from -6 to 6
- qkv_image: bfloat16 [2, 768, 3, 768], P('section', None, None, 'mp'), may hold values from -0.21875 to 0.21875
- out_image: bfloat16 [2, 768, 768], P('section', 'mp'), may hold values from -0.875 to 0.875
- qkv_text: bfloat16 [2, 768, 3, 768], P('section', None, None, 'mp'), may hold values from -0.21875 to 0.21875
- out_text: bfloat16 [2, 768, 768], P('section', 'mp'), may hold values from -0.875 to 0.875
- query_cross: bfloat16 [2, 768, 768], P('section', None, 'mp'), may hold values from -0.21875 to 0.21875
- kv_cross: bfloat16 [2, 768, 2, 768], P('section', None, None, 'mp'), may hold values from -0.21875 to 0.21875
- out_cross: bfloat16 [2, 768, 768], P('section', 'mp'), may hold values from -0.875 to 0.875
- up_proj: bfloat16 [2, 768, 3072], P('section', None, 'mp'), may hold values from -0.21875 to 0.21875
- down_proj: bfloat16 [2, 3072, 768], P('section', 'mp'), may hold values from -0.21875 to 0.21875
- norm_gain: float32 [2, 2, 768], P('section'), may hold values from 0.1 to 1.9
- norm_bias: float32 [2, 2, 768], P('section'), may hold values from -2.4 to 2.4
Outputs:
- image_out: bfloat16 [2, 16, 576, 768], P('section', 'dp', 'mp')
- text_out: bfloat16 [2, 16, 800, 768], P('section', 'dp', 'mp')
- image_grad: float32 [2, 16, 576, 768], P('section', 'dp', 'mp')
- text_grad: float32 [2, 16, 800, 768], P('section', 'dp', 'mp')
- qkv_image_grad: float32 [2, 768, 3, 768], P('section', 'dp', None, 'mp')
- out_image_grad: float32 [2, 768, 768], P('section', ('mp', 'dp'))
- qkv_text_grad: float32 [2, 768, 3, 768], P('section', 'dp', None, 'mp')
- out_text_grad: float32 [2, 768, 768], P('section', ('mp', 'dp'))
- query_cross_grad: float32 [2, 768, 768], P('section', 'dp', 'mp')
- kv_cross_grad: float32 [2, 768, 2, 768], P('section', 'dp', None, 'mp')
- out_cross_grad: float32 [2, 768, 768], P('section', ('mp', 'dp'))
- up_proj_grad: float32 [2, 768, 3072], P('section', 'dp', 'mp')
- down_proj_grad: float32 [2, 3072, 768], P('section', ('mp', 'dp'))
- norm_gain_grad: float32 [2, 2, 768], P('section', None, ('dp', 'mp'))
- norm_bias_grad: float32 [2, 2, 768], P('section', None, ('dp', 'mp'))
The draws below stay inside these ranges and needn't reach their ends.
Inputs may be any that keep to these rules, and one draw needn't show every extreme that they name: `lengths`: the answer length of each sample; the longest equals 800 in every draw.
All inputs are finite; a program needn't handle non-finite values.
Results may differ from the reference program's by a relative error of at most 0.033.
Values may be sent and summed in bfloat16 or wider, within the bound.
No kernel may reach another device: no remote copies, remote signals or barrier semaphores. Data moves between devices by JAX's collectives and lax.ppermute only.
A program may use at most 448 MiB of HBM per device.

```python
import jax
import jax.numpy as jnp
from jax import lax

D = 768
HEAD_DIM = 64
FF = 3072
WIN = 12
PATCH_ROWS = 24
PATCH_COLS = 24
ANSWER_MAX = 800
PATCHES = 576
SAMPLES = 16


def draw_lengths(key, part):
    first_key, second_key = jax.random.split(key)
    draw_values = jax.random.randint(first_key, (SAMPLES,), 5, ANSWER_MAX + 1)
    longest = jax.random.randint(second_key, (), 0, SAMPLES)
    return jnp.where(jnp.arange(SAMPLES) == longest, ANSWER_MAX, draw_values).astype(jnp.int32)


def shard_levels(own_key, extent, cuts, least, top_value):
    factor_of = 1.0
    for axis_at, parts in cuts:
        draws = jax.random.uniform(jax.random.fold_in(jax.random.fold_in(own_key, 6), axis_at), (parts,), jnp.float32, least / len(cuts), top_value / len(cuts))
        factor_of = factor_of * jnp.repeat(jnp.exp(draws), extent[axis_at] // parts).reshape((-1,) + (1,) * (len(extent) - 1 - axis_at))
    return factor_of


def scatter_about(stream_key, extent, scale, most, cuts=(), held_as=jnp.bfloat16):
    values = jax.random.normal(stream_key, extent, jnp.float32) * scale
    if len(cuts) > 0:
        values = shard_levels(stream_key, extent, cuts, -0.22, 0.18) * values
    return jnp.clip(values, min=-most, max=most).astype(held_as)


def setup_inputs(seed: int = 0) -> dict:
    keys = jax.random.split(jax.random.key(seed), 17)
    image = scatter_about(keys[0], (SAMPLES, PATCHES, D), 1.0, 6.0, ((0, 4), (1, 4)))
    text = scatter_about(keys[1], (SAMPLES, ANSWER_MAX, D), 1.0, 6.0, ((0, 4), (1, 4)))
    lengths = draw_lengths(jax.random.fold_in(keys[16], 71), 0)
    image_cot = scatter_about(keys[3], (SAMPLES, PATCHES, D), 1.0, 6.0, ((0, 4), (1, 4)))
    text_cot = scatter_about(keys[4], (SAMPLES, ANSWER_MAX, D), 1.0, 6.0, ((0, 4), (1, 4)))
    qkv_image = scatter_about(keys[5], (2, D, 3, D), D ** -0.5, 0.21875, ((0, 2), (3, 4)))
    out_image = scatter_about(keys[6], (2, D, D), (D // 16) ** -0.5, 0.875, ((0, 2), (1, 4)))
    qkv_text = scatter_about(keys[7], (2, D, 3, D), D ** -0.5, 0.21875, ((0, 2), (3, 4)))
    out_text = scatter_about(keys[8], (2, D, D), (D // 16) ** -0.5, 0.875, ((0, 2), (1, 4)))
    query_cross = scatter_about(keys[9], (2, D, D), D ** -0.5, 0.21875, ((0, 2), (2, 4)))
    kv_cross = scatter_about(keys[10], (2, D, 2, D), D ** -0.5, 0.21875, ((0, 2), (3, 4)))
    out_cross = scatter_about(keys[11], (2, D, D), (D // 16) ** -0.5, 0.875, ((0, 2), (1, 4)))
    up_proj = scatter_about(keys[12], (2, D, FF), D ** -0.5, 0.21875, ((0, 2), (2, 4)))
    down_proj = scatter_about(keys[13], (2, FF, D), (FF // 4) ** -0.5, 0.21875, ((0, 2), (1, 4)))
    norm_gain = jnp.clip(1.0 + 0.18 * jax.random.normal(keys[14], (2, 2, D), jnp.float32), 0.1, 1.9)
    norm_bias = scatter_about(keys[15], (2, 2, D), 0.4, 2.4, ((0, 2),), jnp.float32)
    return dict(image=image, text=text, lengths=lengths, image_cot=image_cot, text_cot=text_cot, qkv_image=qkv_image, out_image=out_image, qkv_text=qkv_text, out_text=out_text, query_cross=query_cross, kv_cross=kv_cross, out_cross=out_cross, up_proj=up_proj, down_proj=down_proj, norm_gain=norm_gain, norm_bias=norm_bias)


EPSILON = 1e-05
MASKED_SCORE = -1000000000.0
HIGHEST = lax.Precision.HIGHEST

@jax.custom_vjp
def low(v):
    return lax.optimization_barrier(v.astype(jnp.bfloat16)).astype(jnp.float32)

@jax.custom_vjp
def low_back(v):
    return v

def low_keep(v):
    return (low(v), None)

def low_pass(kept, grad):
    return (grad,)

def back_keep(v):
    return (v, None)

def back_low(kept, grad):
    return (low(grad),)
low.defvjp(low_keep, low_pass)
low_back.defvjp(back_keep, back_low)

def rounded_both(values):
    return low_back(low(values))

def layer_norm(values, norm_gains, norm_biases):
    average = lax.optimization_barrier(jnp.mean(values, axis=-1, keepdims=True))
    centered = values - average
    variance = lax.optimization_barrier(jnp.mean(centered * centered, axis=-1, keepdims=True))
    return centered * lax.rsqrt(variance + EPSILON) * norm_gains + norm_biases

def to_windows(row_data, shift_by):
    channels = row_data.shape[-1]
    patch_grid = row_data.reshape(PATCH_ROWS, PATCH_COLS, channels)
    patch_grid = jnp.roll(jnp.roll(patch_grid, -shift_by, axis=0), -shift_by, axis=1)
    patch_grid = patch_grid.reshape(PATCH_ROWS // WIN, WIN, PATCH_COLS // WIN, WIN, channels)
    return patch_grid.transpose(0, 2, 1, 3, 4).reshape(-1, WIN * WIN, channels)

def from_windows(windowed, shift_by):
    channels = windowed.shape[-1]
    patch_grid = windowed.reshape(PATCH_ROWS // WIN, PATCH_COLS // WIN, WIN, WIN, channels)
    patch_grid = patch_grid.transpose(0, 2, 1, 3, 4).reshape(PATCH_ROWS, PATCH_COLS, channels)
    patch_grid = jnp.roll(jnp.roll(patch_grid, shift_by, axis=0), shift_by, axis=1)
    return patch_grid.reshape(PATCH_ROWS * PATCH_COLS, channels)

def window_allowed(shift_by):
    row_index = jnp.arange(PATCH_ROWS)
    col_index = jnp.arange(PATCH_COLS)
    row_region = (row_index >= PATCH_ROWS - WIN).astype(jnp.int32) + (row_index >= PATCH_ROWS - shift_by).astype(jnp.int32)
    col_region = (col_index >= PATCH_COLS - WIN).astype(jnp.int32) + (col_index >= PATCH_COLS - shift_by).astype(jnp.int32)
    region_ids = (row_region[:, None] * 3 + col_region[None, :]).reshape(PATCH_ROWS * PATCH_COLS, 1)
    window_ids = to_windows(region_ids, 0)[:, :, 0]
    return window_ids[:, :, None] == window_ids[:, None, :]

def text_allowed(length, answer):
    positions = jnp.arange(answer)
    return (positions[None, :] <= positions[:, None]) & (positions[None, :] < length)

def attend(query_rows, key_rows, value_rows, allowed):
    scale_factor = HEAD_DIM ** (-0.5)
    scores = jnp.einsum('bnhe,bmhe->bhnm', query_rows, key_rows, precision=HIGHEST) * scale_factor
    if allowed is not None:
        scores = jnp.where(allowed[:, None], scores, MASKED_SCORE)
    scores = low_back(scores)
    log_total = jax.scipy.special.logsumexp(scores, axis=-1, keepdims=True)
    weights = jnp.exp(scores - log_total)
    result = jnp.einsum('bhnm,bmhe->bnhe', low(weights), value_rows, precision=HIGHEST)
    return rounded_both(result)

def layer(image_rows, text_rows, length, params, shift_by):
    qkv_image, out_image, qkv_text, out_text, query_cross, kv_cross, out_cross, up_proj, down_proj, norm_gain, norm_bias = params
    heads_total = D // HEAD_DIM
    patch_count = image_rows.shape[0]
    answer = text_rows.shape[0]
    normed_image = low(layer_norm(image_rows, norm_gain[0], norm_bias[0]))
    normed_text = low(layer_norm(text_rows, norm_gain[0], norm_bias[0]))
    image_qkv = rounded_both(jnp.einsum('rd,dtk->rtk', normed_image, qkv_image, precision=HIGHEST))
    windowed = to_windows(image_qkv.reshape(patch_count, 3 * D), shift_by).reshape(-1, WIN * WIN, 3, heads_total, HEAD_DIM)
    image_att = attend(windowed[:, :, 0], windowed[:, :, 1], windowed[:, :, 2], window_allowed(shift_by))
    image_att = from_windows(image_att.reshape(-1, WIN * WIN, D), shift_by)
    image_branch = low_back(jnp.dot(image_att, out_image, precision=HIGHEST))
    text_qkv = rounded_both(jnp.einsum('rd,dtk->rtk', normed_text, qkv_text, precision=HIGHEST))
    text_qkv = text_qkv.reshape(1, answer, 3, heads_total, HEAD_DIM)
    self_att = attend(text_qkv[:, :, 0], text_qkv[:, :, 1], text_qkv[:, :, 2], text_allowed(length, answer)[None])
    cross_query = rounded_both(jnp.dot(normed_text, query_cross, precision=HIGHEST)).reshape(1, answer, heads_total, HEAD_DIM)
    cross_kv = rounded_both(jnp.einsum('rd,dtk->rtk', normed_image, kv_cross, precision=HIGHEST))
    cross_kv = cross_kv.reshape(1, patch_count, 2, heads_total, HEAD_DIM)
    cross_att = attend(cross_query, cross_kv[:, :, 0], cross_kv[:, :, 1], None)
    text_branch = low_back(jnp.dot(self_att.reshape(answer, D), out_text, precision=HIGHEST) + jnp.dot(cross_att.reshape(answer, D), out_cross, precision=HIGHEST))
    mid_rows = jnp.concatenate((image_rows + image_branch, text_rows + text_branch), axis=0)
    normed_mid = low(layer_norm(mid_rows, norm_gain[1], norm_bias[1]))
    hidden_pre = low_back(jnp.dot(normed_mid, up_proj, precision=HIGHEST))
    hidden_act = low(jax.nn.gelu(hidden_pre))
    mlp_branch = low_back(jnp.dot(hidden_act, down_proj, precision=HIGHEST))
    out_rows = mid_rows + mlp_branch
    return (out_rows[:patch_count], out_rows[patch_count:])

def reference(image, text, lengths, image_cot, text_cot, qkv_image, out_image, qkv_text, out_text, query_cross, kv_cross, out_cross, up_proj, down_proj, norm_gain, norm_bias):
    params = tuple((member.astype(jnp.float32) for member in (qkv_image, out_image, qkv_text, out_text, query_cross, kv_cross, out_cross, up_proj, down_proj, norm_gain, norm_bias)))
    image_in = image.astype(jnp.float32)
    text_in = text.astype(jnp.float32)
    extra_image_zero = jnp.zeros(image.shape, jnp.float32)
    extra_text_zero = jnp.zeros(text.shape, jnp.float32)

    def forward(weights, image_rows_all, text_rows_all, extra_image_all, extra_text_all):

        def per_sample(items):
            image_rows, text_rows, extra_image, extra_text, length = items
            first_params = tuple((member[0] for member in weights))
            second_params = tuple((member[1] for member in weights))
            one_image, one_text = layer(image_rows, text_rows, length, first_params, 0)
            sent_image = rounded_both(one_image) + extra_image
            sent_text = rounded_both(one_text) + extra_text
            two_image, two_text = layer(sent_image, sent_text, length, second_params, WIN // 2)
            return (low(one_image), low(one_text), low(two_image), low(two_text))
        return lax.map(jax.checkpoint(per_sample), (image_rows_all, text_rows_all, extra_image_all, extra_text_all, lengths))
    outputs, pullback = jax.vjp(forward, params, image_in, text_in, extra_image_zero, extra_text_zero)
    keep_rows = (jnp.arange(ANSWER_MAX)[None, :] < lengths[:, None]).astype(jnp.float32)
    text_top = text_cot.astype(jnp.float32) * keep_rows[:, :, None]
    cotangents = (jnp.zeros_like(outputs[0]), jnp.zeros_like(outputs[1]), image_cot.astype(jnp.float32), text_top)
    param_grads, image_in_grad, text_in_grad, extra_image_grad, extra_text_grad = pullback(cotangents)
    image_result = jnp.stack((outputs[0], outputs[2])).astype(jnp.bfloat16)
    text_result = jnp.stack((outputs[1], outputs[3])).astype(jnp.bfloat16)
    image_grads = jnp.stack((image_in_grad, extra_image_grad))
    text_grads = jnp.stack((text_in_grad, extra_text_grad))
    return (image_result, text_result, image_grads, text_grads, param_grads[0], param_grads[1], param_grads[2], param_grads[3], param_grads[4], param_grads[5], param_grads[6], param_grads[7], param_grads[8], param_grads[9], param_grads[10])
```

```python
import functools

import jax
import jax.numpy as jnp
from jax import lax
from jax.experimental import pallas as pl
from jax.experimental.pallas import tpu as pltpu
from jax.sharding import PartitionSpec as P

HEAD_DIM = 64
WIN = 12
PATCH_ROWS = 24
PATCH_COLS = 24
SHIFT = WIN // 2

EPSILON = 1e-05
MASKED_SCORE = -1000000000.0
SCALE = HEAD_DIM**-0.5
GELU_C = 0.7978845608028654
GELU_A = 0.044715

VMEM_MIB = 56
FF_BLOCK = 256
SKEW = 2

F32 = jnp.float32
BF16 = jnp.bfloat16

FLIPS = (0, 2, 1, 3)
AT_SLOT, AT_BLOCK, AT_SECTION, AT_MP, AT_LENGTH, AT_VALID = 0, 4, 8, 9, 16, 32


def dot(left, right):
    return lax.dot_general(left, right, (((1,), (0,)), ((), ())), preferred_element_type=F32)


def dot_nt(left, right):
    return lax.dot_general(left, right, (((1,), (1,)), ((), ())), preferred_element_type=F32)


def dot_tn(left, right):
    return lax.dot_general(left, right, (((0,), (0,)), ((), ())), preferred_element_type=F32)


def head_mask(head, width, scale):
    lane = lax.broadcasted_iota(jnp.int32, (1, width), 1)
    inside = (lane >= head * HEAD_DIM) & (lane < (head + 1) * HEAD_DIM)
    return jnp.where(inside, F32(scale), F32(0.0)).astype(BF16)


def normalized(values):
    average = jnp.mean(values, axis=-1, keepdims=True)
    centered = values - average
    variance = jnp.mean(centered * centered, axis=-1, keepdims=True)
    inverse = lax.rsqrt(variance + EPSILON)
    return centered * inverse, inverse


def norm_pull(grad, values, gain):
    unit, inverse = normalized(values)
    scaled = grad * gain
    first = jnp.mean(scaled, axis=-1, keepdims=True)
    second = jnp.mean(scaled * unit, axis=-1, keepdims=True)
    pulled = inverse * (scaled - first - unit * second)
    gain_sum = jnp.sum(grad * unit, axis=0, keepdims=True)
    bias_sum = jnp.sum(grad, axis=0, keepdims=True)
    return pulled, gain_sum, bias_sum


SMEM_SPEC = pl.BlockSpec(memory_space=pltpu.SMEM)
ANY_SPEC = pl.BlockSpec(memory_space=pl.ANY)


def whole(*extent):
    zeros = (0,) * len(extent)
    return pl.BlockSpec(extent, lambda *at: zeros, pipeline_mode=pl.Buffered(1))


def params(mib=VMEM_MIB):
    return pltpu.CompilerParams(vmem_limit_bytes=mib << 20)


def cost(flops, moved, exps=0):
    return pl.CostEstimate(flops=int(flops), bytes_accessed=int(moved), transcendentals=int(exps))


def shape_of(extent, dtype):
    return jax.ShapeDtypeStruct(extent, dtype)


def entry_kernel(tick, info, image, text, got_image, got_text, gain, bias, xi, xt, hi, ht):
    first = info[AT_SECTION] == 0
    for own, got, rows, normed in ((image, got_image, xi, hi), (text, got_text, xt, ht)):
        values = jnp.where(first, own[0].astype(F32), got[...].astype(F32))
        rows[...] = values.astype(BF16)
        unit, _ = normalized(values)
        normed[...] = (unit * gain[0:1, :] + bias[0:1, :]).astype(BF16)


def entry(tick, info, source, image, text, got_image, got_text, gain, bias):
    ni, d = got_image.shape
    nt = got_text.shape[0]
    return pl.pallas_call(
        entry_kernel,
        grid=(1,),
        out_shape=(
            shape_of((ni, d), BF16),
            shape_of((nt, d), BF16),
            shape_of((ni, d), BF16),
            shape_of((nt, d), BF16),
        ),
        in_specs=[
            SMEM_SPEC,
            SMEM_SPEC,
            pl.BlockSpec((1, ni, d), lambda i: (source, 0, 0)),
            pl.BlockSpec((1, nt, d), lambda i: (source, 0, 0)),
            whole(ni, d),
            whole(nt, d),
            whole(*gain.shape),
            whole(*bias.shape),
        ],
        out_specs=(whole(ni, d), whole(nt, d), whole(ni, d), whole(nt, d)),
        compiler_params=params(),
        cost_estimate=cost(10 * (ni + nt) * d, 8 * (ni + nt) * d),
        name="entry_norm",
    )(tick, info, image, text, got_image, got_text, gain, bias)


def image_forward_kernel(
    info, p0, p1, p2, p3, w, wo, gidc, gidr, hx, qkv, ot, tt, r0, r1, r2, r3, o_rows, v_tall
):
    shard = p0.shape[0]
    band = ot.shape[2]
    width = wo.shape[0]
    heads = width // HEAD_DIM
    offs = [pl.multiple_of(info[AT_SLOT + i] * shard, 16) for i in range(4)]
    for off, piece in zip(offs, (p0, p1, p2, p3)):
        rows = piece[...]
        hx[pl.ds(off, shard), :] = rows
        for j in range(5):
            qkv[j, pl.ds(off, shard), :] = dot(rows, w[j]).astype(BF16)
    for b in range(ot.shape[0]):
        span = slice(b * band, (b + 1) * band)
        bias = jnp.where(gidc[span, :] == gidr[0:1, span], F32(0.0), F32(MASKED_SCORE))
        v_tall[...] = qkv[4, span, :].astype(F32).T.astype(BF16)

        def one_head(head, carry):
            query = qkv[2, span, :] * head_mask(head, width, SCALE)
            scores = dot_nt(qkv[3, span, :], query) + bias
            largest = jnp.max(scores, axis=0, keepdims=True)
            weights = jnp.exp(scores - largest)
            total = jnp.sum(weights, axis=0, keepdims=True)
            tt[b * heads + head] = largest + jnp.log(total)
            at = pl.multiple_of(head * HEAD_DIM, HEAD_DIM)
            mixed = dot(v_tall[pl.ds(at, HEAD_DIM), :], weights.astype(BF16))
            ot[b, pl.ds(at, HEAD_DIM), :] = mixed * (1.0 / total)
            return carry

        lax.fori_loop(0, heads, one_head, 0)
        o_rows[span, :] = ot[b].T.astype(BF16)
    for off, piece in zip(offs, (r0, r1, r2, r3)):
        piece[...] = dot(o_rows[pl.ds(off, shard), :], wo[...]).astype(BF16)


def image_forward(info, pieces, w, wo, gidc, gidr):
    shard, d = pieces[0].shape
    rows = 4 * shard
    width = wo.shape[0]
    band = rows // 2
    heads = width // HEAD_DIM
    return pl.pallas_call(
        image_forward_kernel,
        out_shape=(
            shape_of((rows, d), BF16),
            shape_of((5, rows, width), BF16),
            shape_of((2, width, band), F32),
            shape_of((2 * heads, 1, band), F32),
        )
        + (shape_of((shard, d), BF16),) * 4,
        grid=(1,),
        in_specs=[SMEM_SPEC]
        + [whole(shard, d)] * 4
        + [whole(*a.shape) for a in (w, wo, gidc, gidr)],
        out_specs=(
            whole(rows, d),
            whole(5, rows, width),
            whole(2, width, band),
            whole(2 * heads, 1, band),
        )
        + (whole(shard, d),) * 4,
        scratch_shapes=[
            pltpu.VMEM((rows, width), BF16),
            pltpu.VMEM((width, band), BF16),
        ],
        compiler_params=params(),
        cost_estimate=cost(
            2 * rows * d * width * 6 + 8 * heads * band * band * 256,
            2 * rows * d * 3 + 12 * rows * width + 12 * d * width,
            2 * heads * band * band,
        ),
        name="image_forward",
    )(info, *pieces, w, wo, gidc, gidr)


def store_chunks(grads, chunks, w_parts, wo_parts):
    width, d = w_parts[0].shape
    rows, at = d // chunks, d // chunks
    for j, part in enumerate(w_parts):
        turned = part.T.astype(BF16)
        for z in range(chunks):
            grads[z, 0:rows, j * width : (j + 1) * width] = turned[z * rows : (z + 1) * rows, :]
    for part in wo_parts:
        rows = width // chunks
        narrow = part.astype(BF16)
        for z in range(chunks):
            grads[z, at : at + rows, 0:d] = narrow[z * rows : (z + 1) * rows, :]
            if grads.shape[2] > d:
                grads[z, at : at + rows, d:] = jnp.zeros((rows, grads.shape[2] - d), BF16)
        at += rows


def image_backward_kernel(
    first, last, tick, info, p0, p1, p2, p3, w, wo, gidc, gidr, hx, qkv, ot, tt, dkv, *refs
):
    olds, refs = ([], refs) if first else (refs[:2], refs[2:])
    (r0, r1, r2, r3), refs = refs[:4], refs[4:]
    news, refs = (refs[:1], refs[1:]) if last else (refs[:2], refs[2:])
    da_rows, do_rows, d_rows, dq_tall, k_tall, do_tall, dk_sum, dv_sum = refs
    shard = p0.shape[0]
    band = ot.shape[2]
    width = wo.shape[0]
    heads = width // HEAD_DIM
    valid = info[AT_VALID + tick[0]].astype(F32)
    offs = [pl.multiple_of(info[AT_SLOT + i] * shard, 16) for i in range(4)]
    for off, piece in zip(offs, (p0, p1, p2, p3)):
        rows = piece[...]
        da_rows[pl.ds(off, shard), :] = rows
        do_rows[pl.ds(off, shard), :] = dot_nt(rows, wo[...]).astype(BF16)
    total_wo = jnp.zeros(wo.shape, F32)
    for b in range(ot.shape[0]):
        span = slice(b * band, (b + 1) * band)
        total_wo = total_wo + dot(ot[b].astype(BF16), da_rows[span, :])
        bias = jnp.where(gidc[span, :] == gidr[0:1, span], F32(0.0), F32(MASKED_SCORE))
        k_tall[...] = qkv[3, span, :].astype(F32).T.astype(BF16)
        do_tall[...] = do_rows[span, :].astype(F32).T
        dk_sum[...] = jnp.zeros_like(dk_sum)
        dv_sum[...] = jnp.zeros_like(dv_sum)

        def one_head(head, carry):
            at = pl.multiple_of(head * HEAD_DIM, HEAD_DIM)
            query = qkv[2, span, :] * head_mask(head, width, SCALE)
            grad = do_rows[span, :] * head_mask(head, width, 1.0)
            scores = dot_nt(qkv[3, span, :], query) + bias
            weights = jnp.exp(scores - tt[b * heads + head])
            pulled = dot_nt(qkv[4, span, :], grad)
            mixed = ot[b, pl.ds(at, HEAD_DIM), :]
            delta = jnp.sum(do_tall[pl.ds(at, HEAD_DIM), :] * mixed, axis=0, keepdims=True)
            score_grad = (weights * (pulled - delta)).astype(BF16)
            dv_sum[...] += dot(weights.astype(BF16), grad)
            dk_sum[...] += dot(score_grad, query)
            dq_tall[pl.ds(at, HEAD_DIM), :] = dot(k_tall[pl.ds(at, HEAD_DIM), :], score_grad) * SCALE
            return carry

        lax.fori_loop(0, heads, one_head, 0)
        d_rows[0, span, :] = dq_tall[...].T.astype(BF16)
        d_rows[1, span, :] = dk_sum[...].astype(BF16)
        d_rows[2, span, :] = dv_sum[...].astype(BF16)
    for off, piece in zip(offs, (r0, r1, r2, r3)):
        part = dot_nt(dkv[0, pl.ds(off, shard), :], w[0]) + dot_nt(dkv[1, pl.ds(off, shard), :], w[1])
        for j in range(3):
            part = part + dot_nt(d_rows[j, pl.ds(off, shard), :], w[2 + j])
        piece[...] = part.astype(BF16)
    w_parts = [dot_tn(dkv[j] if j < 2 else d_rows[j - 2], hx[...]) * valid for j in range(5)]
    wo_part = total_wo * valid
    if not first:
        w_parts = [olds[0][j] + part for j, part in enumerate(w_parts)]
        wo_part = olds[1][...] + wo_part
    if last:
        store_chunks(news[0], news[0].shape[0], w_parts, [wo_part])
    else:
        for j, part in enumerate(w_parts):
            news[0][j] = part
        news[1][...] = wo_part


def image_backward(tick, info, pieces, w, wo, gidc, gidr, hx, qkv, ot, tt, dkv, accs, chunks):
    first, last = not accs, chunks > 0
    shard, d = pieces[0].shape
    rows = 4 * shard
    width = wo.shape[0]
    band = rows // 2
    heads = width // HEAD_DIM
    if last:
        news = (shape_of((chunks, (d + width) // chunks, max(5 * width, d)), BF16),)
    else:
        news = (shape_of((5, width, d), F32), shape_of((width, d), F32))
    arrays = (w, wo, gidc, gidr, hx, qkv, ot, tt, dkv) + tuple(accs)
    out = pl.pallas_call(
        functools.partial(image_backward_kernel, first, last),
        grid=(1,),
        out_shape=(shape_of((shard, d), BF16),) * 4 + news,
        in_specs=[SMEM_SPEC] * 2 + [whole(shard, d)] * 4 + [whole(*a.shape) for a in arrays],
        out_specs=(whole(shard, d),) * 4 + tuple(whole(*a.shape) for a in news),
        input_output_aliases={} if first or last else {15: 4, 16: 5},
        scratch_shapes=[
            pltpu.VMEM((rows, d), BF16),
            pltpu.VMEM((rows, width), BF16),
            pltpu.VMEM((3, rows, width), BF16),
            pltpu.VMEM((width, band), F32),
            pltpu.VMEM((width, band), BF16),
            pltpu.VMEM((width, band), F32),
            pltpu.VMEM((band, width), F32),
            pltpu.VMEM((band, width), F32),
        ],
        compiler_params=params(),
        cost_estimate=cost(
            2 * rows * d * width * 12 + 20 * heads * band * band * 256,
            2 * rows * d * 3 + 20 * rows * width + 60 * d * width,
            2 * heads * band * band,
        ),
        name="image_backward",
    )(tick, info, *pieces, *arrays)
    return out[:4], out[4:]


QUERY_BLOCK = 256


def query_blocks(rows):
    return [(at, min(QUERY_BLOCK, rows - at)) for at in range(0, rows, QUERY_BLOCK)]


def text_forward_kernel(
    tick, info, p0, p1, p2, p3, w, wo, kv, hy, qkv, ot, tt, r0, r1, r2, r3, stage, o_rows, v_tall
):
    shard, d = p0.shape
    rows = 4 * shard
    patches = kv.shape[1]
    width = wo.shape[1]
    heads = width // HEAD_DIM
    last_key = info[AT_LENGTH + tick[0]] - 1
    offs = [pl.multiple_of(info[AT_BLOCK + i] * shard, 8) for i in range(4)]
    for off, piece in zip(offs, (p0, p1, p2, p3)):
        stage[pl.ds(off, shard), :] = piece[...].astype(F32)
    hy[...] = stage[...].astype(BF16)
    for j in range(4):
        qkv[j] = dot(hy[...], w[j]).astype(BF16)
    for kind in range(2):
        span = rows if kind == 0 else patches
        values = qkv[2] if kind == 0 else kv[1]
        v_tall[:, 0:span] = values.astype(F32).T.astype(BF16)

        def one_head(head, carry):
            at = pl.multiple_of(head * HEAD_DIM, HEAD_DIM)
            out_at = pl.multiple_of(kind * width + head * HEAD_DIM, HEAD_DIM)
            mask = head_mask(head, width, SCALE)
            for start, size in query_blocks(rows):
                seen = start + size if kind == 0 else patches
                query = qkv[0 if kind == 0 else 3, start : start + size, :] * mask
                keys = qkv[1, 0:seen, :] if kind == 0 else kv[0]
                scores = dot_nt(keys, query)
                if kind == 0:
                    key_at = lax.broadcasted_iota(jnp.int32, (seen, size), 0)
                    query_at = lax.broadcasted_iota(jnp.int32, (1, size), 1) + start
                    limit = jnp.minimum(query_at, last_key)
                    scores = jnp.where(key_at <= limit, scores, F32(MASKED_SCORE))
                largest = jnp.max(scores, axis=0, keepdims=True)
                weights = jnp.exp(scores - largest)
                total = jnp.sum(weights, axis=0, keepdims=True)
                tt[kind * heads + head, :, start : start + size] = largest + jnp.log(total)
                mixed = dot(v_tall[pl.ds(at, HEAD_DIM), 0:seen], weights.astype(BF16))
                mixed = mixed * (1.0 / total)
                ot[pl.ds(out_at, HEAD_DIM), start : start + size] = mixed
            return carry

        lax.fori_loop(0, heads, one_head, 0)
    o_rows[...] = ot[...].T
    for off, piece in zip(offs, (r0, r1, r2, r3)):
        mixed = o_rows[pl.ds(off, shard), :].astype(BF16)
        piece[...] = (dot(mixed[:, 0:width], wo[0]) + dot(mixed[:, width:], wo[1])).astype(BF16)


def text_forward(tick, info, pieces, w, wo, kv):
    shard, d = pieces[0].shape
    rows = 4 * shard
    width = wo.shape[1]
    heads = width // HEAD_DIM
    patches = kv.shape[1]
    return pl.pallas_call(
        text_forward_kernel,
        grid=(1,),
        out_shape=(
            shape_of((rows, d), BF16),
            shape_of((4, rows, width), BF16),
            shape_of((2 * width, rows), F32),
            shape_of((2 * heads, 1, rows), F32),
        )
        + (shape_of((shard, d), BF16),) * 4,
        in_specs=[SMEM_SPEC] * 2
        + [whole(shard, d)] * 4
        + [whole(*w.shape), whole(*wo.shape), whole(2, patches, width)],
        out_specs=(whole(rows, d), whole(4, rows, width), whole(2 * width, rows), whole(2 * heads, 1, rows))
        + (whole(shard, d),) * 4,
        scratch_shapes=[
            pltpu.VMEM((rows, d), F32),
            pltpu.VMEM((rows, 2 * width), F32),
            pltpu.VMEM((width, rows), BF16),
        ],
        compiler_params=params(),
        cost_estimate=cost(
            2 * rows * d * width * 6 + 4 * heads * rows * (rows * 0.6 + patches) * 256,
            2 * rows * d * 3 + 12 * rows * width + 12 * d * width,
            heads * rows * (rows * 0.6 + patches),
        ),
        name="text_forward",
    )(tick, info, *pieces, w, wo, kv)


def text_backward_kernel(first, last, tick, info, p0, p1, p2, p3, w, wo, kv, hy, qkv, ot, tt, *refs):
    olds, refs = ([], refs) if first else (refs[:2], refs[2:])
    (r0, r1, r2, r3, dkv), refs = refs[:5], refs[5:]
    news, refs = (refs[:1], refs[1:]) if last else (refs[:2], refs[2:])
    stage, da_rows, do_rows, dq_tall, k_tall, do_tall, dk_sum, dv_sum, d_rows = refs
    shard, d = p0.shape
    rows = 4 * shard
    patches = kv.shape[1]
    width = wo.shape[1]
    heads = width // HEAD_DIM
    valid = info[AT_VALID + tick[0]].astype(F32)
    last_key = info[AT_LENGTH + tick[0]] - 1
    offs = [pl.multiple_of(info[AT_BLOCK + i] * shard, 8) for i in range(4)]
    for off, piece in zip(offs, (p0, p1, p2, p3)):
        stage[pl.ds(off, shard), :] = piece[...].astype(F32)
    da_rows[...] = stage[...].astype(BF16)
    wo_parts = []
    for kind in range(2):
        span = rows if kind == 0 else patches
        grads = dot_nt(da_rows[...], wo[kind]).astype(BF16)
        do_rows[...] = grads
        do_tall[...] = grads.astype(F32).T
        wo_parts.append(dot(ot[kind * width : (kind + 1) * width, :].astype(BF16), da_rows[...]) * valid)
        whole_keys = qkv[1] if kind == 0 else kv[0]
        k_tall[:, 0:span] = whole_keys.astype(F32).T.astype(BF16)
        dk_sum[...] = jnp.zeros_like(dk_sum)
        dv_sum[...] = jnp.zeros_like(dv_sum)

        def one_head(head, carry):
            at = pl.multiple_of(head * HEAD_DIM, HEAD_DIM)
            out_at = pl.multiple_of(kind * width + head * HEAD_DIM, HEAD_DIM)
            query_mask = head_mask(head, width, SCALE)
            grad_mask = head_mask(head, width, 1.0)
            for start, size in query_blocks(rows):
                seen = start + size if kind == 0 else patches
                block = slice(start, start + size)
                query = qkv[0 if kind == 0 else 3, block, :] * query_mask
                grad = do_rows[block, :] * grad_mask
                keys = qkv[1, 0:seen, :] if kind == 0 else kv[0]
                values = qkv[2, 0:seen, :] if kind == 0 else kv[1]
                scores = dot_nt(keys, query)
                if kind == 0:
                    key_at = lax.broadcasted_iota(jnp.int32, (seen, size), 0)
                    query_at = lax.broadcasted_iota(jnp.int32, (1, size), 1) + start
                    limit = jnp.minimum(query_at, last_key)
                    scores = jnp.where(key_at <= limit, scores, F32(MASKED_SCORE))
                weights = jnp.exp(scores - tt[kind * heads + head, :, block])
                pulled = dot_nt(values, grad)
                mixed = ot[pl.ds(out_at, HEAD_DIM), block]
                delta = jnp.sum(do_tall[pl.ds(at, HEAD_DIM), block] * mixed, axis=0, keepdims=True)
                score_grad = (weights * (pulled - delta)).astype(BF16)
                dv_sum[0:seen, :] += dot(weights.astype(BF16), grad)
                dk_sum[0:seen, :] += dot(score_grad, query)
                dq_tall[pl.ds(at, HEAD_DIM), block] = (
                    dot(k_tall[pl.ds(at, HEAD_DIM), 0:seen], score_grad) * SCALE
                )
            return carry

        lax.fori_loop(0, heads, one_head, 0)
        if kind == 0:
            d_rows[0] = dq_tall[...].T.astype(BF16)
            d_rows[1] = dk_sum[...].astype(BF16)
            d_rows[2] = dv_sum[...].astype(BF16)
        else:
            d_rows[3] = dq_tall[...].T.astype(BF16)
            dkv[0] = dk_sum[0:patches, :].astype(BF16)
            dkv[1] = dv_sum[0:patches, :].astype(BF16)
    part = dot_nt(d_rows[0], w[0])
    for j in range(1, 4):
        part = part + dot_nt(d_rows[j], w[j])
    stage[...] = part
    for off, piece in zip(offs, (r0, r1, r2, r3)):
        piece[...] = stage[pl.ds(off, shard), :].astype(BF16)
    w_parts = [dot_tn(d_rows[j], hy[...]) * valid for j in range(4)]
    if not first:
        w_parts = [olds[0][j] + part for j, part in enumerate(w_parts)]
        wo_parts = [olds[1][j] + part for j, part in enumerate(wo_parts)]
    if last:
        store_chunks(news[0], news[0].shape[0], w_parts, wo_parts)
    else:
        for j, part in enumerate(w_parts):
            news[0][j] = part
        for j, part in enumerate(wo_parts):
            news[1][j] = part


def text_backward(tick, info, pieces, w, wo, kv, hy, qkv, ot, tt, accs, chunks):
    first, last = not accs, chunks > 0
    shard, d = pieces[0].shape
    rows = 4 * shard
    width = wo.shape[1]
    heads = width // HEAD_DIM
    patches = kv.shape[1]
    if last:
        news = (shape_of((chunks, (d + 2 * width) // chunks, max(4 * width, d)), BF16),)
    else:
        news = (shape_of((4, width, d), F32), shape_of((2, width, d), F32))
    arrays = (hy, qkv, ot, tt) + tuple(accs)
    out = pl.pallas_call(
        functools.partial(text_backward_kernel, first, last),
        grid=(1,),
        out_shape=(shape_of((shard, d), BF16),) * 4 + (shape_of((2, patches, width), BF16),) + news,
        in_specs=[SMEM_SPEC] * 2
        + [whole(shard, d)] * 4
        + [whole(*w.shape), whole(*wo.shape), whole(2, patches, width)]
        + [whole(*a.shape) for a in arrays],
        out_specs=(whole(shard, d),) * 4
        + (whole(2, patches, width),)
        + tuple(whole(*a.shape) for a in news),
        input_output_aliases={} if first or last else {13: 5, 14: 6},
        scratch_shapes=[
            pltpu.VMEM((rows, d), F32),
            pltpu.VMEM((rows, d), BF16),
            pltpu.VMEM((rows, width), BF16),
            pltpu.VMEM((width, rows), F32),
            pltpu.VMEM((width, rows), BF16),
            pltpu.VMEM((width, rows), F32),
            pltpu.VMEM((rows, width), F32),
            pltpu.VMEM((rows, width), F32),
            pltpu.VMEM((4, rows, width), BF16),
        ],
        compiler_params=params(),
        cost_estimate=cost(
            2 * rows * d * width * 12 + 10 * heads * rows * (rows * 0.6 + patches) * 256,
            2 * rows * d * 3 + 20 * rows * width + 60 * d * width,
            heads * rows * (rows * 0.6 + patches),
        ),
        name="text_backward",
    )(tick, info, *pieces, w, wo, kv, *arrays)
    return out[:4], out[4], out[5:]


def ff_forward_kernel(stacked, xi, ai, bi, ci, xt, at, bt, ct, gain, bias, up, down, *refs):
    refs = refs[2:] if stacked else refs
    mid, h2_tall, g, gp, zi, zt, h2, acc = refs
    step = pl.program_id(0)
    ni = xi.shape[0]

    @pl.when(step == 0)
    def _():
        for x, a, b, c, span in (
            (xi, ai, bi, ci, slice(0, ni)),
            (xt, at, bt, ct, slice(ni, mid.shape[0])),
        ):
            branch = a[...].astype(F32) + b[...].astype(F32) + c[...].astype(F32)
            values = x[...].astype(F32) + branch
            mid[span, :] = values
            acc[span, :] = values
        unit, _ = normalized(mid[...])
        rows = unit * gain[1:2, :] + bias[1:2, :]
        h2[...] = rows.astype(BF16)
        h2_tall[0] = rows.T.astype(BF16)

    hidden = up.shape[2]
    total = acc[...]
    for at_unit in range(0, hidden, FF_BLOCK):
        block = slice(at_unit, at_unit + FF_BLOCK)
        u = dot(h2[...], up[0, :, block])
        square = u * u
        bent = jnp.tanh(u * (GELU_C + (GELU_C * GELU_A) * square))
        half = 0.5 * (1.0 + bent)
        act = (u * half).astype(BF16)
        g[0, :, block] = act
        slope = half + (0.5 * u) * (1.0 - bent * bent) * (GELU_C + (3.0 * GELU_C * GELU_A) * square)
        gp[:, block] = slope.astype(BF16)
        total = total + dot(act, down[0, block, :])
    acc[...] = total

    @pl.when(step == pl.num_programs(0) - 1)
    def _():
        zi[...] = acc[0:ni, :].astype(BF16)
        zt[...] = acc[ni:, :].astype(BF16)


def ff_forward(t, ticks, stacks, xi, image_parts, xt, text_parts, gain, bias, up, down):
    ni, d = xi.shape
    nt = xt.shape[0]
    n = ni + nt
    blocks, _, hidden = up.shape
    stacked = len(stacks) > 0
    return pl.pallas_call(
        functools.partial(ff_forward_kernel, stacked),
        grid=(blocks,),
        out_shape=(
            shape_of((n, d), F32),
            shape_of((ticks, d, n), BF16),
            shape_of((ticks, n, blocks * hidden), BF16),
            shape_of((n, blocks * hidden), BF16),
            shape_of((ni, d), BF16),
            shape_of((nt, d), BF16),
        ),
        in_specs=[whole(ni, d)] * 4
        + [whole(nt, d)] * 4
        + [whole(*gain.shape), whole(*bias.shape)]
        + [
            pl.BlockSpec((1, d, hidden), lambda i: (i, 0, 0)),
            pl.BlockSpec((1, hidden, d), lambda i: (i, 0, 0)),
        ]
        + [ANY_SPEC] * len(stacks),
        out_specs=(
            whole(n, d),
            pl.BlockSpec((1, d, n), lambda i: (t, 0, 0)),
            pl.BlockSpec((1, n, hidden), lambda i: (t, 0, i)),
            pl.BlockSpec((n, hidden), lambda i: (0, i)),
            whole(ni, d),
            whole(nt, d),
        ),
        input_output_aliases={12: 1, 13: 2} if stacked else {},
        scratch_shapes=[pltpu.VMEM((n, d), BF16), pltpu.VMEM((n, d), F32)],
        compiler_params=params(),
        cost_estimate=cost(
            4 * n * d * hidden * blocks,
            4 * d * hidden * blocks + 4 * n * hidden * blocks + 16 * n * d,
            n * hidden * blocks,
        ),
        name="ff_forward",
    )(xi, *image_parts, xt, *text_parts, gain, bias, up, down, *stacks)


def ff_backward_kernel(
    stacked, tick, info, coti, cott, backi, backt, gp, mid, gain, up, down, *refs
):
    refs = refs[2:] if stacked else refs
    dm_tall, du, dmid, dai, dat, sums, rows, dm, acc = refs
    step = pl.program_id(0)
    ni = backi.shape[0]
    nt = backt.shape[0]
    valid = info[AT_VALID + tick[0]].astype(F32)

    @pl.when(step == 0)
    def _():
        first = info[AT_SECTION] == 0
        place = lax.broadcasted_iota(jnp.int32, (nt, 1), 0) + info[AT_MP] * nt
        kept = (place < info[AT_LENGTH + tick[0]]).astype(F32)
        rows[0:ni, :] = jnp.where(first, backi[...].astype(F32), coti[0].astype(F32)) * valid
        rows[ni:, :] = jnp.where(first, backt[...].astype(F32), cott[0].astype(F32) * kept) * valid
        dm[...] = rows[...].astype(BF16)
        dm_tall[0] = rows[...].T.astype(BF16)
        acc[...] = jnp.zeros_like(acc)

    hidden = up.shape[2]
    total = acc[...]
    for at_unit in range(0, hidden, FF_BLOCK):
        block = slice(at_unit, at_unit + FF_BLOCK)
        act_grad = dot_nt(dm[...], down[0, block, :])
        pre_grad = (gp[:, block].astype(F32) * act_grad).astype(BF16)
        du[0, :, block] = pre_grad
        total = total + dot_nt(pre_grad, up[0, :, block])
    acc[...] = total

    @pl.when(step == pl.num_programs(0) - 1)
    def _():
        pulled, gain_sum, bias_sum = norm_pull(acc[...], mid[...], gain[1:2, :])
        total = rows[...] + pulled
        dmid[...] = total
        dai[...] = total[0:ni, :].astype(BF16)
        dat[...] = total[ni:, :].astype(BF16)
        sums[0:1, :] = gain_sum
        sums[1:2, :] = bias_sum


def ff_backward(
    tick, info, source, t, ticks, stacks, coti, cott, backi, backt, gp, mid, gain, up, down
):
    ni, d = backi.shape
    nt = backt.shape[0]
    n = ni + nt
    blocks, _, hidden = up.shape
    stacked = len(stacks) > 0
    return pl.pallas_call(
        functools.partial(ff_backward_kernel, stacked),
        grid=(blocks,),
        out_shape=(
            shape_of((ticks, d, n), BF16),
            shape_of((ticks, n, blocks * hidden), BF16),
            shape_of((n, d), F32),
            shape_of((ni, d), BF16),
            shape_of((nt, d), BF16),
            shape_of((2, d), F32),
        ),
        in_specs=[
            SMEM_SPEC,
            SMEM_SPEC,
            pl.BlockSpec((1, ni, d), lambda i: (source, 0, 0)),
            pl.BlockSpec((1, nt, d), lambda i: (source, 0, 0)),
            whole(ni, d),
            whole(nt, d),
            pl.BlockSpec((n, hidden), lambda i: (0, i)),
            whole(n, d),
            whole(*gain.shape),
            pl.BlockSpec((1, d, hidden), lambda i: (i, 0, 0)),
            pl.BlockSpec((1, hidden, d), lambda i: (i, 0, 0)),
        ]
        + [ANY_SPEC] * len(stacks),
        out_specs=(
            pl.BlockSpec((1, d, n), lambda i: (t, 0, 0)),
            pl.BlockSpec((1, n, hidden), lambda i: (t, 0, i)),
            whole(n, d),
            whole(ni, d),
            whole(nt, d),
            whole(2, d),
        ),
        input_output_aliases={11: 0, 12: 1} if stacked else {},
        scratch_shapes=[
            pltpu.VMEM((n, d), F32),
            pltpu.VMEM((n, d), BF16),
            pltpu.VMEM((n, d), F32),
        ],
        compiler_params=params(),
        cost_estimate=cost(
            4 * n * d * hidden * blocks,
            4 * d * hidden * blocks + 4 * n * hidden * blocks + 16 * n * d,
        ),
        name="ff_backward",
    )(tick, info, coti, cott, backi, backt, gp, mid, gain, up, down, *stacks)


def ff_weights_kernel(h2_tall, dm_tall, du, g, one, two, up_sum, down_sum):
    piece, t = pl.program_id(0), pl.program_id(1)
    up_part = dot(h2_tall[t], du[0])
    down_part = dot(dm_tall[t], g[0])

    @pl.when(t == 0)
    def _():
        up_sum[...] = up_part
        down_sum[...] = down_part

    @pl.when(t > 0)
    def _():
        up_sum[...] += up_part
        down_sum[...] += down_part

    for index, out in enumerate((one, two)):

        @pl.when((t == pl.num_programs(1) - 1) & (piece == index))
        def _():
            chunks, rows = out.shape[0], out.shape[1] // 2
            turned = down_sum[...].T
            for z in range(chunks):
                span = slice(z * rows, (z + 1) * rows)
                out[z, 0:rows, :] = up_sum[span, :].astype(BF16)
                out[z, rows:, :] = turned[span, :].astype(BF16)


def ff_weights(pieces, h2_tall, dm_tall, du, g, chunks):
    ticks, d, n = h2_tall.shape
    hidden = du.shape[2] // 4
    one, two = pieces
    part = (chunks, 2 * d // chunks, hidden)
    column = lambda i: one + (two - one) * i
    return pl.pallas_call(
        ff_weights_kernel,
        grid=(2, ticks),
        out_shape=(shape_of(part, BF16),) * 2,
        in_specs=[
            whole(ticks, d, n),
            whole(ticks, d, n),
            pl.BlockSpec((1, n, hidden), lambda i, t: (t, 0, column(i))),
            pl.BlockSpec((1, n, hidden), lambda i, t: (t, 0, column(i))),
        ],
        out_specs=(whole(*part), whole(*part)),
        scratch_shapes=[pltpu.VMEM((d, hidden), F32), pltpu.VMEM((hidden, d), F32)],
        compiler_params=params(),
        cost_estimate=cost(
            8 * ticks * n * d * hidden, 4 * ticks * d * n + 8 * ticks * n * hidden + 8 * d * hidden
        ),
        name="ff_weights",
    )(h2_tall, dm_tall, du, g)


def close_kernel(
    tick, info, xi, ai, bi, ci, xt, at, bt, ct, dmid, gain, gi, gt, backi, backt, sums
):
    ni = xi.shape[0]
    n = dmid.shape[0]
    gain_total = jnp.zeros((1, xi.shape[1]), F32)
    bias_total = jnp.zeros((1, xi.shape[1]), F32)
    for x, a, b, c, span, out, back in (
        (xi, ai, bi, ci, slice(0, ni), gi, backi),
        (xt, at, bt, ct, slice(ni, n), gt, backt),
    ):
        grad = a[...].astype(F32) + b[...].astype(F32) + c[...].astype(F32)
        pulled, gain_sum, bias_sum = norm_pull(grad, x[...].astype(F32), gain[0:1, :])
        total = dmid[span, :] + pulled
        out[...] = total
        back[...] = total.astype(BF16)
        gain_total = gain_total + gain_sum
        bias_total = bias_total + bias_sum
    valid = info[AT_VALID + tick[0]].astype(F32)
    sums[0:1, :] = gain_total * valid
    sums[1:2, :] = bias_total * valid


def close(tick, info, xi, image_parts, xt, text_parts, dmid, gain):
    ni, d = xi.shape
    nt = xt.shape[0]
    return pl.pallas_call(
        close_kernel,
        out_shape=(
            shape_of((ni, d), F32),
            shape_of((nt, d), F32),
            shape_of((ni, d), BF16),
            shape_of((nt, d), BF16),
            shape_of((2, d), F32),
        ),
        grid=(1,),
        in_specs=[SMEM_SPEC] * 2
        + [whole(ni, d)] * 4
        + [whole(nt, d)] * 4
        + [whole(*dmid.shape), whole(*gain.shape)],
        out_specs=(whole(ni, d), whole(nt, d), whole(ni, d), whole(nt, d), whole(2, d)),
        compiler_params=params(),
        cost_estimate=cost(20 * (ni + nt) * d, 18 * (ni + nt) * d),
        name="input_grad",
    )(tick, info, xi, *image_parts, xt, *text_parts, dmid, gain)


def over_y(array):
    return lax.ppermute(array, "mp", [(m, m ^ 2) for m in range(4)])


def over_core(array):
    return lax.ppermute(array, "mp", [(m, m ^ 1) for m in range(4)])


def gathered(own):
    across = over_y(own)
    return (own, across, over_core(own), over_core(across))


def scattered(r0, r1, r2, r3):
    across = (r1.astype(F32) + over_core(r3).astype(F32)).astype(BF16)
    return (r0, over_core(r2), over_y(across))


def shifted(array, by):
    length = lax.axis_size("section")
    return lax.ppermute(array, "section", [(i, i + by) for i in range(length) if 0 <= i + by < length])


def shards(
    image, text, lengths, image_cot, text_cot, qkv_image, out_image, qkv_text, out_text,
    query_cross, kv_cross, out_cross, up_proj, down_proj, norm_gain, norm_bias,
):
    section = lax.axis_index("section")
    me = lax.axis_index("mp")
    groups = lax.axis_size("dp")
    micro = image.shape[0]
    ticks = micro + SKEW
    ni, d = image.shape[1:]
    nt = text.shape[1]
    gain, bias = norm_gain[0], norm_bias[0]
    wo_image = out_image[0]
    wo_text = jnp.stack((out_text[0], out_cross[0]))
    w_image = jnp.concatenate((kv_cross[0].transpose(1, 0, 2), qkv_image[0].transpose(1, 0, 2)), axis=0)
    w_text = jnp.concatenate((qkv_text[0].transpose(1, 0, 2), query_cross[0][None]), axis=0)
    width = wo_image.shape[0]

    flips = jnp.array(FLIPS, jnp.int32)
    turn = jnp.arange(ticks) - section * SKEW
    valid = ((turn >= 0) & (turn < micro)).astype(jnp.int32)
    info = jnp.concatenate(
        (
            ((me ^ flips) - section) % 4,
            me ^ flips,
            jnp.stack((section, me)).astype(jnp.int32),
            jnp.zeros((AT_LENGTH - 10,), jnp.int32),
            lengths[jnp.clip(turn, 0, micro - 1)],
            jnp.zeros((AT_VALID - AT_LENGTH - ticks,), jnp.int32),
            valid,
        )
    ).astype(jnp.int32)
    place = jnp.arange(4 * ni)
    turned = (place % PATCH_COLS - section * SHIFT) % PATCH_COLS
    edge = PATCH_ROWS - section * SHIFT
    row_region = (place // PATCH_COLS >= PATCH_ROWS - WIN).astype(jnp.int32) + (
        place // PATCH_COLS >= edge
    ).astype(jnp.int32)
    col_region = (turned >= PATCH_COLS - WIN).astype(jnp.int32) + (turned >= edge).astype(jnp.int32)
    region = row_region * 3 + col_region
    gidc = region[:, None]
    gidr = region[None, :]

    tick_at = [jnp.full((1,), t, jnp.int32) for t in range(ticks)]
    none_image = jnp.zeros((ni, d), BF16)
    none_text = jnp.zeros((nt, d), BF16)
    kept = []
    sent = []
    relayed = []
    up = down = None
    stacks = ()
    for t in range(ticks):
        got_image, got_text = relayed[t - SKEW] if t >= SKEW else (none_image, none_text)
        xi, xt, hi, ht = entry(
            tick_at[t], info, min(t, micro - 1), image, text, got_image, got_text, gain, bias
        )
        image_pieces = gathered(hi)
        text_pieces = gathered(ht)
        if up is None:
            up_own, down_own, _ = lax.optimization_barrier((up_proj[0], down_proj[0], text_pieces[1]))
            up = jnp.stack(gathered(up_own))
            down = jnp.stack(gathered(down_own))
        hx, qkvi, oti, tti, *image_parts = image_forward(info, image_pieces, w_image, wo_image, gidc, gidr)
        hy, qkvt, ott, ttt, *text_parts = text_forward(tick_at[t], info, text_pieces, w_text, wo_text, qkvi)
        mid, h2_tall, g, gp, zi, zt = ff_forward(
            t, ticks, stacks, xi, scattered(*image_parts), xt, scattered(*text_parts),
            gain, bias, up, down,
        )
        stacks = (h2_tall, g)
        kept.append((xi, xt, hx, qkvi, oti, tti, hy, qkvt, ott, ttt, mid, gp))
        sent.append((zi, zt))
        if t + SKEW < ticks:
            relayed.append((shifted(zi, 1), shifted(zt, 1)))

    accs_image = accs_text = back_stacks = ()
    sums_one = sums_two = jnp.zeros((2, d), F32)
    grads = []
    relayed = []
    for k in range(ticks):
        t = ticks - 1 - k
        last = groups if k == ticks - 1 else 0
        xi, xt, hx, qkvi, oti, tti, hy, qkvt, ott, ttt, mid, gp = kept[t]
        back_image, back_text = relayed[k - SKEW] if k >= SKEW else (none_image, none_text)
        dm_tall, du, dmid, dai, dat, sums = ff_backward(
            tick_at[t], info, max(t - SKEW, 0), t, ticks, back_stacks, image_cot, text_cot,
            back_image, back_text, gp, mid, gain, up, down,
        )
        back_stacks = (dm_tall, du)
        sums_two = sums_two + sums
        text_pieces = gathered(dat)
        image_pieces = gathered(dai)
        if last:
            far, y_part = ff_weights((3, 1), stacks[0], dm_tall, du, stacks[1], groups)
            near, core_part = ff_weights((0, 2), stacks[0], dm_tall, du, stacks[1], groups)
            ff_parts = scattered(near, y_part, core_part, far)
        text_parts, dkv, accs_text = text_backward(
            tick_at[t], info, text_pieces, w_text, wo_text, qkvi, hy, qkvt, ott, ttt, accs_text, last
        )
        image_parts, accs_image = image_backward(
            tick_at[t], info, image_pieces, w_image, wo_image, gidc, gidr, hx, qkvi, oti, tti,
            dkv, accs_image, last,
        )
        gi, gt, back_image, back_text, sums = close(
            tick_at[t], info, xi, scattered(*image_parts), xt, scattered(*text_parts), dmid, gain
        )
        sums_one = sums_one + sums
        grads.append((gi, gt))
        if k + SKEW < ticks:
            relayed.append((shifted(back_image, -1), shifted(back_text, -1)))

    def over_dp(array):
        return lax.psum_scatter(array, "dp", scatter_dimension=0, tiled=True)[0].astype(F32)

    a, b, c = ff_parts
    ff_grad = over_dp((a.astype(F32) + b.astype(F32) + c.astype(F32)).astype(BF16))
    text_grad = over_dp(accs_text[0])
    image_grad = over_dp(accs_image[0])
    rows, wo_rows = d // groups, width // groups
    up_grad, down_grad = ff_grad[:rows], ff_grad[rows:]
    gain_grad, bias_grad = (
        lax.psum_scatter(
            jnp.stack((sums_one[i], sums_two[i])), ("dp", "mp"), scatter_dimension=1, tiled=True
        )
        for i in range(2)
    )
    head = section == 0
    image_result, text_result = (
        jnp.stack([jnp.where(head, sent[b][i], sent[b + SKEW][i]) for b in range(micro)])
        for i in range(2)
    )
    by_tick = grads[::-1]
    image_grads, text_grads = (
        jnp.stack([jnp.where(head, by_tick[b][i], by_tick[b + SKEW][i]) for b in range(micro)])
        for i in range(2)
    )
    return (
        image_result[None],
        text_result[None],
        image_grads[None],
        text_grads[None],
        image_grad[:rows, 2 * width :].reshape(1, rows, 3, width),
        image_grad[rows:, :d][None],
        text_grad[:rows, : 3 * width].reshape(1, rows, 3, width),
        text_grad[rows : rows + wo_rows, :d][None],
        text_grad[:rows, 3 * width :][None],
        image_grad[:rows, : 2 * width].reshape(1, rows, 2, width),
        text_grad[rows + wo_rows :, :d][None],
        up_grad[None],
        down_grad[None],
        gain_grad[None],
        bias_grad[None],
    )


def solution(mesh):
    return jax.shard_map(
        shards,
        mesh=mesh,
        in_specs=(
            P("dp", "mp", None),
            P("dp", "mp", None),
            P("dp"),
            P("dp", "mp", None),
            P("dp", "mp", None),
            P("section", None, None, "mp"),
            P("section", "mp", None),
            P("section", None, None, "mp"),
            P("section", "mp", None),
            P("section", None, "mp"),
            P("section", None, None, "mp"),
            P("section", "mp", None),
            P("section", None, "mp"),
            P("section", "mp", None),
            P("section", None, None),
            P("section", None, None),
        ),
        out_specs=(
            P("section", "dp", "mp", None),
            P("section", "dp", "mp", None),
            P("section", "dp", "mp", None),
            P("section", "dp", "mp", None),
            P("section", "dp", None, "mp"),
            P("section", ("mp", "dp"), None),
            P("section", "dp", None, "mp"),
            P("section", ("mp", "dp"), None),
            P("section", "dp", "mp"),
            P("section", "dp", None, "mp"),
            P("section", ("mp", "dp"), None),
            P("section", "dp", "mp"),
            P("section", ("mp", "dp"), None),
            P("section", None, ("dp", "mp")),
            P("section", None, ("dp", "mp")),
        ),
        check_vma=False,
    )
```

```python
import functools

import jax
import jax.numpy as jnp
from jax import lax
from jax.experimental import pallas as pl
from jax.experimental.pallas import tpu as pltpu
from jax.sharding import PartitionSpec as P

HEAD_DIM = 64
WIN = 12
PATCH_ROWS = 24
PATCH_COLS = 24
SHIFT = WIN // 2

EPSILON = 1e-05
MASKED_SCORE = -1000000000.0
SCALE = HEAD_DIM**-0.5
GELU_C = 0.7978845608028654
GELU_A = 0.044715

VMEM_MIB = 56
SKEW = 2
SELF_BLOCK = 256
CROSS_BLOCK = 1024

F32 = jnp.float32
BF16 = jnp.bfloat16

FLIPS = (0, 2, 1, 3)
AT_SLOT, AT_BLOCK, AT_SECTION, AT_MP, AT_LENGTH, AT_VALID, AT_STACK = 0, 4, 8, 9, 16, 32, 48


def dot(left, right):
    return lax.dot_general(left, right, (((1,), (0,)), ((), ())), preferred_element_type=F32)


def dot_nt(left, right):
    return lax.dot_general(left, right, (((1,), (1,)), ((), ())), preferred_element_type=F32)


def dot_tn(left, right):
    return lax.dot_general(left, right, (((0,), (0,)), ((), ())), preferred_element_type=F32)


def head_mask(head, width, scale):
    lane = lax.broadcasted_iota(jnp.int32, (1, width), 1)
    inside = (lane >= head * HEAD_DIM) & (lane < (head + 1) * HEAD_DIM)
    return jnp.where(inside, F32(scale), F32(0.0)).astype(BF16)


def normalized(values):
    average = jnp.mean(values, axis=-1, keepdims=True)
    centered = values - average
    variance = jnp.mean(centered * centered, axis=-1, keepdims=True)
    inverse = lax.rsqrt(variance + EPSILON)
    return centered * inverse, inverse


def norm_pull(grad, values, gain):
    unit, inverse = normalized(values)
    scaled = grad * gain
    first = jnp.mean(scaled, axis=-1, keepdims=True)
    second = jnp.mean(scaled * unit, axis=-1, keepdims=True)
    pulled = inverse * (scaled - first - unit * second)
    gain_sum = jnp.sum(grad * unit, axis=0, keepdims=True)
    bias_sum = jnp.sum(grad, axis=0, keepdims=True)
    return pulled, gain_sum, bias_sum


SMEM_SPEC = pl.BlockSpec(memory_space=pltpu.SMEM)
ANY_SPEC = pl.BlockSpec(memory_space=pl.ANY)


def whole(*extent):
    zeros = (0,) * len(extent)
    return pl.BlockSpec(extent, lambda *at: zeros, pipeline_mode=pl.Buffered(1))


def params():
    return pltpu.CompilerParams(vmem_limit_bytes=VMEM_MIB << 20)


def cost(flops, moved, exps=0):
    return pl.CostEstimate(flops=int(flops), bytes_accessed=int(moved), transcendentals=int(exps))


def shape_of(extent, dtype):
    return jax.ShapeDtypeStruct(extent, dtype)


class Copies:
    def __init__(self, sems):
        self.sems = sems
        self.used = 0
        self.going = []

    def start(self, source, target):
        copy = pltpu.make_async_copy(source, target, self.sems.at[self.used])
        self.used += 1
        copy.start()
        self.going.append(copy)
        return copy

    def wait(self, *copies):
        for copy in copies:
            copy.wait()
            self.going = [other for other in self.going if other is not copy]

    def finish(self):
        for copy in self.going:
            copy.wait()
        self.going = []


def run(kernel, name, estimate, scalars, arrays, outs, scratch, sems, aliases=()):
    lead = len(scalars)
    return pl.pallas_call(
        kernel,
        out_shape=tuple(outs),
        in_specs=[SMEM_SPEC] * lead + [ANY_SPEC] * len(arrays),
        out_specs=(ANY_SPEC,) * len(outs),
        scratch_shapes=list(scratch) + [pltpu.SemaphoreType.DMA((sems,))],
        input_output_aliases={lead + a: b for a, b in aliases},
        compiler_params=params(),
        cost_estimate=estimate,
        name=name,
    )(*scalars, *arrays)


def entry_kernel(source, tick, info, image, text, got, gain, bias, x, h, own, got_v, norm, xv, hv, sems):
    copies = Copies(sems)
    ni = image.shape[1]
    loads = [
        copies.start(image.at[source], own.at[0:ni]),
        copies.start(text.at[source], own.at[ni:]),
        copies.start(got, got_v),
        copies.start(gain, norm.at[0]),
        copies.start(bias, norm.at[1]),
    ]
    copies.wait(*loads)
    first = info[AT_SECTION] == 0
    values = jnp.where(first, own[...].astype(F32), got_v[...].astype(F32))
    xv[...] = values.astype(BF16)
    unit, _ = normalized(values)
    hv[...] = (unit * norm[0, 0:1, :] + norm[1, 0:1, :]).astype(BF16)
    copies.start(hv, h)
    copies.start(xv, x)
    copies.finish()


def entry(tick, info, source, image, text, got, gain, bias):
    n, d = got.shape
    return run(
        functools.partial(entry_kernel, source),
        "entry_norm",
        cost(10 * n * d, 8 * n * d),
        (tick, info),
        (image, text, got, gain, bias),
        (shape_of((n, d), BF16),) * 2,
        [pltpu.VMEM((n, d), BF16), pltpu.VMEM((n, d), BF16), pltpu.VMEM((2, 2, d), F32)]
        + [pltpu.VMEM((n, d), BF16)] * 2,
        7,
    )


def image_forward_kernel(
    tick, info, p0, p1, p2, p3, w, wo, gidc, gidr, *refs
):
    refs = refs[-(8 + 12) :]
    r0, r1, r23, qkv, ot, tt, hx, o = refs[:8]
    hx_v, w_v, wo_v, gidc_v, gidr_v, qkv_v, ot_v, tt_v, o_v, part, v_tall, sems = refs[8:]
    copies = Copies(sems)
    rows, d = hx_v.shape
    shard = rows // 4
    band = ot_v.shape[2]
    width = wo_v.shape[0]
    heads = width // HEAD_DIM
    slot = info[AT_STACK + tick[0]]
    offs = [pl.multiple_of(info[AT_SLOT + i] * shard, 16) for i in range(4)]
    loads = [
        copies.start(piece.at[0:shard], hx_v.at[pl.ds(off, shard)])
        for off, piece in zip(offs, (p0, p1, p2, p3))
    ] + [copies.start(w, w_v)]
    more = [copies.start(a, b) for a, b in ((gidc, gidc_v), (gidr, gidr_v), (wo, wo_v))]
    copies.wait(*loads)
    projected = dot(hx_v[...], w_v[...])
    for j in range(5):
        qkv_v[j] = projected[:, j * width : (j + 1) * width].astype(BF16)
    copies.start(hx_v, hx.at[slot])
    copies.start(qkv_v, qkv)
    copies.wait(*more)
    for b in range(2):
        span = slice(b * band, (b + 1) * band)
        bias = jnp.where(gidc_v[span, :] == gidr_v[0:1, span], F32(0.0), F32(MASKED_SCORE))
        v_tall[...] = qkv_v[4, span, :].astype(F32).T.astype(BF16)
        for head in range(heads):
            query = qkv_v[2, span, :] * head_mask(head, width, SCALE)
            scores = dot_nt(qkv_v[3, span, :], query) + bias
            largest = jnp.max(scores, axis=0, keepdims=True)
            weights = jnp.exp(scores - largest)
            total = jnp.sum(weights, axis=0, keepdims=True)
            tt_v[b * heads + head] = largest + jnp.log(total)
            at = head * HEAD_DIM
            mixed = dot(v_tall[at : at + HEAD_DIM, :], weights.astype(BF16))
            ot_v[b, at : at + HEAD_DIM, :] = mixed * (1.0 / total)
        o_v[span, :] = ot_v[b].T.astype(BF16)
    copies.start(ot_v, ot)
    copies.start(tt_v, tt)
    copies.start(o_v, o.at[slot])
    part[...] = dot(o_v[...], wo_v[...]).astype(BF16)
    for off, piece in zip(offs, (r0, r1, r23.at[0], r23.at[1])):
        copies.start(part.at[pl.ds(off, shard)], piece.at[0:shard])
    copies.finish()


def image_forward(tick, info, shard, micro, pieces, w, wo, gidc, gidr, stacks):
    n, d = pieces[0].shape
    rows = 4 * shard
    width = wo.shape[0]
    band = rows // 2
    heads = width // HEAD_DIM
    return run(
        image_forward_kernel,
        "image_forward",
        cost(
            2 * rows * d * width * 6 + 8 * heads * band * band * 256,
            2 * rows * d * 3 + 12 * rows * width + 12 * d * width,
            2 * heads * band * band,
        ),
        (tick, info),
        (*pieces, w, wo, gidc, gidr, *stacks),
        (
            shape_of((n, d), BF16),
            shape_of((n, d), BF16),
            shape_of((2, n, d), BF16),
            shape_of((5, rows, width), BF16),
            shape_of((2, width, band), F32),
            shape_of((2 * heads, 1, band), F32),
            shape_of((micro + 1, rows, d), BF16),
            shape_of((micro + 1, rows, width), BF16),
        ),
        [
            pltpu.VMEM((rows, d), BF16),
            pltpu.VMEM(w.shape, BF16),
            pltpu.VMEM(wo.shape, BF16),
            pltpu.VMEM(gidc.shape, jnp.int32),
            pltpu.VMEM(gidr.shape, jnp.int32),
            pltpu.VMEM((5, rows, width), BF16),
            pltpu.VMEM((2, width, band), F32),
            pltpu.VMEM((2 * heads, 1, band), F32),
            pltpu.VMEM((rows, width), BF16),
            pltpu.VMEM((rows, d), BF16),
            pltpu.VMEM((width, band), BF16),
        ],
        18,
        ((8, 6), (9, 7)) if stacks else (),
    )


def image_backward_kernel(tick, info, p0, p1, p2, p3, w, wo, gidc, gidr, qkv, ot, tt, dkv, *refs):
    refs = refs[-(5 + 18) :]
    r0, r1, r23, da, dd = refs[:5]
    (
        da_v, w_v, wo_v, gidc_v, gidr_v, qkv_v, ot_v, tt_v, dkv_v, do_v, d_v, part,
        dq_tall, k_tall, do_tall, dk_sum, dv_sum, sems,
    ) = refs[5:]
    copies = Copies(sems)
    rows, d = da_v.shape
    shard = rows // 4
    band = ot_v.shape[2]
    width = wo_v.shape[0]
    heads = width // HEAD_DIM
    slot = info[AT_STACK + tick[0]]
    offs = [pl.multiple_of(info[AT_SLOT + i] * shard, 16) for i in range(4)]
    loads = [
        copies.start(piece.at[0:shard], da_v.at[pl.ds(off, shard)])
        for off, piece in zip(offs, (p0, p1, p2, p3))
    ] + [copies.start(wo, wo_v)]
    more = [
        copies.start(a, b)
        for a, b in ((qkv, qkv_v), (gidc, gidc_v), (gidr, gidr_v), (tt, tt_v), (ot, ot_v))
    ]
    rest = [copies.start(a, b) for a, b in ((dkv, dkv_v), (w, w_v))]
    copies.wait(*loads)
    copies.start(da_v, da.at[slot])
    do_v[...] = dot_nt(da_v[...], wo_v[...]).astype(BF16)
    copies.wait(*more)
    for b in range(2):
        span = slice(b * band, (b + 1) * band)
        bias = jnp.where(gidc_v[span, :] == gidr_v[0:1, span], F32(0.0), F32(MASKED_SCORE))
        k_tall[...] = qkv_v[3, span, :].astype(F32).T.astype(BF16)
        do_tall[...] = do_v[span, :].astype(F32).T
        dk_sum[...] = jnp.zeros_like(dk_sum)
        dv_sum[...] = jnp.zeros_like(dv_sum)
        for head in range(heads):
            at = head * HEAD_DIM
            own = slice(at, at + HEAD_DIM)
            query = qkv_v[2, span, :] * head_mask(head, width, SCALE)
            grad = do_v[span, :] * head_mask(head, width, 1.0)
            scores = dot_nt(qkv_v[3, span, :], query) + bias
            weights = jnp.exp(scores - tt_v[b * heads + head])
            pulled = dot_nt(qkv_v[4, span, :], grad)
            delta = jnp.sum(do_tall[own, :] * ot_v[b, own, :], axis=0, keepdims=True)
            score_grad = (weights * (pulled - delta)).astype(BF16)
            dv_sum[...] += dot(weights.astype(BF16), grad)
            dk_sum[...] += dot(score_grad, query)
            dq_tall[own, :] = dot(k_tall[own, :], score_grad) * SCALE
        d_v[span, 2 * width : 3 * width] = dq_tall[...].T.astype(BF16)
        d_v[span, 3 * width : 4 * width] = dk_sum[...].astype(BF16)
        d_v[span, 4 * width :] = dv_sum[...].astype(BF16)
    copies.wait(*rest)
    d_v[:, 0:width] = dkv_v[0]
    d_v[:, width : 2 * width] = dkv_v[1]
    copies.start(d_v, dd.at[slot])
    part[...] = dot_nt(d_v[...], w_v[...]).astype(BF16)
    for off, piece in zip(offs, (r0, r1, r23.at[0], r23.at[1])):
        copies.start(part.at[pl.ds(off, shard)], piece.at[0:shard])
    copies.finish()


def image_backward(tick, info, shard, micro, pieces, w, wo, gidc, gidr, qkv, ot, tt, dkv, parts, stacks):
    n, d = pieces[0].shape
    rows = 4 * shard
    width = wo.shape[0]
    band = rows // 2
    heads = width // HEAD_DIM
    return run(
        image_backward_kernel,
        "image_backward",
        cost(
            2 * rows * d * width * 6 + 20 * heads * band * band * 256,
            2 * rows * d * 3 + 20 * rows * width + 12 * d * width,
            2 * heads * band * band,
        ),
        (tick, info),
        (*pieces, w, wo, gidc, gidr, qkv, ot, tt, dkv, *parts, *stacks),
        (
            shape_of((n, d), BF16),
            shape_of((n, d), BF16),
            shape_of((2, n, d), BF16),
            shape_of((micro + 1, rows, d), BF16),
            shape_of((micro + 1, rows, 5 * width), BF16),
        ),
        [
            pltpu.VMEM((rows, d), BF16),
            pltpu.VMEM(w.shape, BF16),
            pltpu.VMEM(wo.shape, BF16),
            pltpu.VMEM(gidc.shape, jnp.int32),
            pltpu.VMEM(gidr.shape, jnp.int32),
            pltpu.VMEM((5, rows, width), BF16),
            pltpu.VMEM((2, width, band), F32),
            pltpu.VMEM((2 * heads, 1, band), F32),
            pltpu.VMEM((2, rows, width), BF16),
            pltpu.VMEM((rows, width), BF16),
            pltpu.VMEM((rows, 5 * width), BF16),
            pltpu.VMEM((rows, d), BF16),
            pltpu.VMEM((width, band), F32),
            pltpu.VMEM((width, band), BF16),
            pltpu.VMEM((width, band), F32),
            pltpu.VMEM((band, width), F32),
            pltpu.VMEM((band, width), F32),
        ],
        18,
        ((12, 0), (13, 1), (14, 2)) + (((15, 3), (16, 4)) if stacks else ()),
    )


def query_blocks(rows, size):
    return [(at, min(size, rows - at)) for at in range(0, rows, size)]


def causal(scores, start, last_key):
    key_at = lax.broadcasted_iota(jnp.int32, scores.shape, 0)
    query_at = lax.broadcasted_iota(jnp.int32, (1, scores.shape[1]), 1) + start
    return jnp.where(key_at <= jnp.minimum(query_at, last_key), scores, F32(MASKED_SCORE))


def text_forward_kernel(skip, tick, info, p0, p1, p2, p3, w, wo, kv, *refs):
    refs = refs[-(8 + 11) :]
    r0, r1, r23, qkv, ot, tt, hy, o = refs[:8]
    hy_v, w_v, wo_v, kv_v, qkv_v, ot_v, tt_v, o_v, part, piece_v, sems = refs[8:]
    copies = Copies(sems)
    rows, d = hy_v.shape
    shard = rows // 4
    patches = kv_v.shape[1]
    width = kv_v.shape[2]
    heads = width // HEAD_DIM
    slot = info[AT_STACK + tick[0]]
    last_key = info[AT_LENGTH + tick[0]] - 1
    offs = [pl.multiple_of(info[AT_BLOCK + i] * shard, 8) for i in range(4)]
    loads = [
        copies.start(piece.at[skip:], piece_v.at[i]) for i, piece in enumerate((p0, p1, p2, p3))
    ] + [copies.start(w, w_v)]
    more = [copies.start(kv.at[0:2], kv_v)]
    rest = [copies.start(wo, wo_v)]
    copies.wait(*loads)
    for i, off in enumerate(offs):
        part[pl.ds(off, shard), :] = piece_v[i].astype(F32)
    hy_v[...] = part[...].astype(BF16)
    projected = dot(hy_v[...], w_v[...])
    for j in range(4):
        qkv_v[j] = projected[:, j * width : (j + 1) * width].astype(BF16)
    copies.start(hy_v, hy.at[slot])
    copies.start(qkv_v, qkv)
    copies.wait(*more)
    for kind in range(2):
        values = qkv_v[2] if kind == 0 else kv_v[1]
        v_tall = values.astype(F32).T.astype(BF16)
        for start, size in query_blocks(rows, CROSS_BLOCK if kind else SELF_BLOCK):
            seen = start + size if kind == 0 else patches
            for head in range(heads):
                at = head * HEAD_DIM
                mask = head_mask(head, width, SCALE)
                query = qkv_v[3 if kind else 0, start : start + size, :] * mask
                keys = kv_v[0] if kind else qkv_v[1, 0:seen, :]
                scores = dot_nt(keys, query)
                if kind == 0:
                    scores = causal(scores, start, last_key)
                largest = jnp.max(scores, axis=0, keepdims=True)
                weights = jnp.exp(scores - largest)
                total = jnp.sum(weights, axis=0, keepdims=True)
                tt_v[kind * heads + head, :, start : start + size] = largest + jnp.log(total)
                mixed = dot(v_tall[at : at + HEAD_DIM, 0:seen], weights.astype(BF16))
                out_at = kind * width + at
                ot_v[out_at : out_at + HEAD_DIM, start : start + size] = mixed * (1.0 / total)
    copies.start(ot_v, ot)
    copies.start(tt_v, tt)
    o_v[...] = ot_v[...].T.astype(BF16)
    copies.start(o_v, o.at[slot])
    copies.wait(*rest)
    part[...] = dot(o_v[...], wo_v[...])
    for i, (off, piece) in enumerate(zip(offs, (r0, r1, r23.at[0], r23.at[1]))):
        piece_v[i] = part[pl.ds(off, shard), :].astype(BF16)
        copies.start(piece_v.at[i], piece.at[skip:])
    copies.finish()


def text_forward(tick, info, shard, micro, pieces, w, wo, kv, parts, stacks):
    n, d = pieces[0].shape
    rows = 4 * shard
    patches, width = kv.shape[1:]
    heads = width // HEAD_DIM
    return run(
        functools.partial(text_forward_kernel, n - shard),
        "text_forward",
        cost(
            2 * rows * d * width * 6 + 4 * heads * rows * (rows * 0.6 + patches) * 256,
            2 * rows * d * 3 + 12 * rows * width + 12 * d * width,
            heads * rows * (rows * 0.6 + patches),
        ),
        (tick, info),
        (*pieces, w, wo, kv, *parts, *stacks),
        (
            shape_of((n, d), BF16),
            shape_of((n, d), BF16),
            shape_of((2, n, d), BF16),
            shape_of((4, rows, width), BF16),
            shape_of((2 * width, rows), F32),
            shape_of((2 * heads, 1, rows), F32),
            shape_of((micro + 1, rows, d), BF16),
            shape_of((micro + 1, rows, 2 * width), BF16),
        ),
        [
            pltpu.VMEM((rows, d), BF16),
            pltpu.VMEM(w.shape, BF16),
            pltpu.VMEM(wo.shape, BF16),
            pltpu.VMEM((2, patches, width), BF16),
            pltpu.VMEM((4, rows, width), BF16),
            pltpu.VMEM((2 * width, rows), F32),
            pltpu.VMEM((2 * heads, 1, rows), F32),
            pltpu.VMEM((rows, 2 * width), BF16),
            pltpu.VMEM((rows, d), F32),
            pltpu.VMEM((4, shard, d), BF16),
        ],
        16,
        ((7, 0), (8, 1), (9, 2)) + (((10, 6), (11, 7)) if stacks else ()),
    )


def text_backward_kernel(skip, tick, info, p0, p1, p2, p3, w, wo, kv, qkv, ot, tt, *refs):
    refs = refs[-(6 + 18) :]
    r0, r1, r23, dkv, da, dd = refs[:6]
    (
        da_v, w_v, wo_v, kv_v, qkv_v, ot_v, tt_v, do_v, d_v, dkv_v, part, piece_v,
        dq_tall, k_tall, do_tall, dk_sum, dv_sum, sems,
    ) = refs[6:]
    copies = Copies(sems)
    rows, d = da_v.shape
    shard = rows // 4
    patches, width = kv_v.shape[1:]
    heads = width // HEAD_DIM
    slot = info[AT_STACK + tick[0]]
    last_key = info[AT_LENGTH + tick[0]] - 1
    offs = [pl.multiple_of(info[AT_BLOCK + i] * shard, 8) for i in range(4)]
    loads = [
        copies.start(piece.at[skip:], piece_v.at[i]) for i, piece in enumerate((p0, p1, p2, p3))
    ] + [copies.start(wo, wo_v)]
    more = [copies.start(a, b) for a, b in ((qkv, qkv_v), (tt, tt_v), (ot, ot_v), (kv.at[0:2], kv_v))]
    rest = [copies.start(w, w_v)]
    copies.wait(*loads)
    for i, off in enumerate(offs):
        part[pl.ds(off, shard), :] = piece_v[i].astype(F32)
    da_v[...] = part[...].astype(BF16)
    copies.start(da_v, da.at[slot])
    grads = dot_nt(da_v[...], wo_v[...])
    do_v[...] = grads.astype(BF16)
    do_tall[...] = grads.astype(BF16).astype(F32).T
    copies.wait(*more)
    for kind in range(2):
        span = patches if kind else rows
        whole_keys = kv_v[0] if kind else qkv_v[1]
        k_tall[:, 0:span] = whole_keys.astype(F32).T.astype(BF16)
        dk_sum[...] = jnp.zeros_like(dk_sum)
        dv_sum[...] = jnp.zeros_like(dv_sum)
        for start, size in query_blocks(rows, CROSS_BLOCK if kind else SELF_BLOCK):
            seen = start + size if kind == 0 else patches
            block = slice(start, start + size)
            keys = kv_v[0] if kind else qkv_v[1, 0:seen, :]
            values = kv_v[1] if kind else qkv_v[2, 0:seen, :]
            for head in range(heads):
                at = head * HEAD_DIM
                own = slice(at, at + HEAD_DIM)
                out_own = slice(kind * width + at, kind * width + at + HEAD_DIM)
                query = qkv_v[3 if kind else 0, block, :] * head_mask(head, width, SCALE)
                grad = do_v[block, kind * width : (kind + 1) * width] * head_mask(head, width, 1.0)
                scores = dot_nt(keys, query)
                if kind == 0:
                    scores = causal(scores, start, last_key)
                weights = jnp.exp(scores - tt_v[kind * heads + head, :, block])
                pulled = dot_nt(values, grad)
                delta = jnp.sum(do_tall[out_own, block] * ot_v[out_own, block], axis=0, keepdims=True)
                score_grad = (weights * (pulled - delta)).astype(BF16)
                dv_sum[0:seen, :] += dot(weights.astype(BF16), grad)
                dk_sum[0:seen, :] += dot(score_grad, query)
                dq_tall[own, block] = dot(k_tall[own, 0:seen], score_grad) * SCALE
        if kind == 0:
            d_v[:, 0:width] = dq_tall[...].T.astype(BF16)
            d_v[:, width : 2 * width] = dk_sum[...].astype(BF16)
            d_v[:, 2 * width : 3 * width] = dv_sum[...].astype(BF16)
        else:
            d_v[:, 3 * width :] = dq_tall[...].T.astype(BF16)
            dkv_v[0] = dk_sum[0:patches, :].astype(BF16)
            dkv_v[1] = dv_sum[0:patches, :].astype(BF16)
    copies.start(dkv_v, dkv)
    copies.start(d_v, dd.at[slot])
    copies.wait(*rest)
    part[...] = dot_nt(d_v[...], w_v[...])
    for i, (off, piece) in enumerate(zip(offs, (r0, r1, r23.at[0], r23.at[1]))):
        piece_v[i] = part[pl.ds(off, shard), :].astype(BF16)
        copies.start(piece_v.at[i], piece.at[skip:])
    copies.finish()


def text_backward(tick, info, shard, micro, pieces, w, wo, kv, qkv, ot, tt, stacks):
    n, d = pieces[0].shape
    rows = 4 * shard
    patches, width = kv.shape[1:]
    heads = width // HEAD_DIM
    return run(
        functools.partial(text_backward_kernel, n - shard),
        "text_backward",
        cost(
            2 * rows * d * width * 6 + 10 * heads * rows * (rows * 0.6 + patches) * 256,
            2 * rows * d * 3 + 20 * rows * width + 12 * d * width,
            heads * rows * (rows * 0.6 + patches),
        ),
        (tick, info),
        (*pieces, w, wo, kv, qkv, ot, tt, *stacks),
        (
            shape_of((n, d), BF16),
            shape_of((n, d), BF16),
            shape_of((2, n, d), BF16),
            shape_of((2, patches, width), BF16),
            shape_of((micro + 1, rows, d), BF16),
            shape_of((micro + 1, rows, 4 * width), BF16),
        ),
        [
            pltpu.VMEM((rows, d), BF16),
            pltpu.VMEM(w.shape, BF16),
            pltpu.VMEM(wo.shape, BF16),
            pltpu.VMEM((2, patches, width), BF16),
            pltpu.VMEM((4, rows, width), BF16),
            pltpu.VMEM((2 * width, rows), F32),
            pltpu.VMEM((2 * heads, 1, rows), F32),
            pltpu.VMEM((rows, 2 * width), BF16),
            pltpu.VMEM((rows, 4 * width), BF16),
            pltpu.VMEM((2, patches, width), BF16),
            pltpu.VMEM((rows, d), F32),
            pltpu.VMEM((4, shard, d), BF16),
            pltpu.VMEM((width, rows), F32),
            pltpu.VMEM((width, rows), BF16),
            pltpu.VMEM((2 * width, rows), F32),
            pltpu.VMEM((rows, width), F32),
            pltpu.VMEM((rows, width), F32),
        ],
        18,
        ((10, 4), (11, 5)) if stacks else (),
    )


def attention_weights_kernel(h, dd, o, da, out, w_sum, wo_sum):
    step = pl.program_id(0)
    w_part = dot_tn(h[0], dd[0])
    wo_part = dot_tn(o[0], da[0])

    @pl.when(step == 0)
    def _():
        w_sum[...] = w_part
        wo_sum[...] = wo_part

    @pl.when(step > 0)
    def _():
        w_sum[...] += w_part
        wo_sum[...] += wo_part

    @pl.when(step == pl.num_programs(0) - 1)
    def _():
        chunks = out.shape[0]
        d, columns = w_sum.shape
        rows, wide = d // chunks, wo_sum.shape[1]
        at = rows
        for z in range(chunks):
            out[z, 0:rows, :] = w_sum[z * rows : (z + 1) * rows, :].astype(BF16)
        narrow = d // 4 // chunks
        for part in range(wo_sum.shape[0] // (d // 4)):
            for z in range(chunks):
                top = part * (d // 4) + z * narrow
                out[z, at : at + narrow, 0:wide] = wo_sum[top : top + narrow, :].astype(BF16)
                if columns > wide:
                    out[z, at : at + narrow, wide:] = jnp.zeros((narrow, columns - wide), BF16)
            at += narrow


def attention_weights(h, dd, o, da, chunks, name):
    slots, rows, d = h.shape
    columns, wide = dd.shape[2], o.shape[2]
    out = (chunks, (d + wide) // chunks, columns)
    slot = lambda a: pl.BlockSpec((1, *a.shape[1:]), lambda i: (i, 0, 0))
    return pl.pallas_call(
        attention_weights_kernel,
        grid=(slots - 1,),
        out_shape=shape_of(out, BF16),
        in_specs=[slot(a) for a in (h, dd, o, da)],
        out_specs=whole(*out),
        scratch_shapes=[pltpu.VMEM((d, columns), F32), pltpu.VMEM((wide, d), F32)],
        compiler_params=params(),
        cost_estimate=cost(
            2 * slots * rows * d * (columns + wide), 2 * slots * rows * (2 * d + columns + wide)
        ),
        name=name,
    )(h, dd, o, da)


def ff_forward_kernel(ni, tick, info, x, a, b, c, gain, bias, u0, u1, u2, u3, d0, d1, d2, d3, *refs):
    refs = refs[-(7 + 11) :]
    mid, gp, z, h2, g, image_out, text_out = refs[:7]
    x_v, abc, norm, up, down, mid_v, h2_v, g_v, gp_v, z_v, sems = refs[7:]
    copies = Copies(sems)
    n, d = x_v.shape
    hidden = up.shape[2]
    slot = info[AT_STACK + tick[0]]
    at_row = pl.multiple_of(slot * n, 8)
    loads = [
        copies.start(s, t)
        for s, t in (
            (x, x_v),
            (a, abc.at[0]),
            (b.at[0], abc.at[1]),
            (c, abc.at[2]),
            (gain, norm.at[0]),
            (bias, norm.at[1]),
        )
    ]
    weights = [
        (copies.start(u, up.at[i]), copies.start(w, down.at[i]))
        for i, (u, w) in enumerate(zip((u0, u1, u2, u3), (d0, d1, d2, d3)))
    ]
    copies.wait(*loads)
    values = x_v[...].astype(F32) + (
        abc[0].astype(F32) + abc[1].astype(F32) + abc[2].astype(F32)
    )
    mid_v[...] = values
    unit, _ = normalized(values)
    h2_v[...] = (unit * norm[0, 1:2, :] + norm[1, 1:2, :]).astype(BF16)
    copies.start(mid_v, mid)
    copies.start(h2_v, h2.at[pl.ds(at_row, n)])

    def ascend(i):
        copies.wait(weights[i][0])
        return dot(h2_v[...], up[i])

    def bend(i, u):
        square = u * u
        bent = jnp.tanh(u * (GELU_C + (GELU_C * GELU_A) * square))
        half = 0.5 * (1.0 + bent)
        g_v[i] = (u * half).astype(BF16)
        slope = half + (0.5 * u) * (1.0 - bent * bent) * (GELU_C + (3.0 * GELU_C * GELU_A) * square)
        gp_v[i] = slope.astype(BF16)
        columns = slice(i * hidden, (i + 1) * hidden)
        copies.start(g_v.at[i], g.at[pl.ds(at_row, n), columns])
        copies.start(gp_v.at[i], gp.at[:, columns])

    total = mid_v[...]
    u = ascend(0)
    for i in range(4):
        bend(i, u)
        copies.wait(weights[i][1])
        total = total + dot(g_v[i], down[i])
        u = ascend(i + 1) if i < 3 else None
    z_v[...] = total.astype(BF16)
    copies.start(z_v, z)
    copies.finish()

    @pl.when(info[AT_VALID + tick[0]] > 0)
    def _():
        image_copy = pltpu.make_async_copy(z_v.at[0:ni], image_out.at[slot], sems.at[0])
        text_copy = pltpu.make_async_copy(z_v.at[ni:], text_out.at[slot], sems.at[1])
        image_copy.start()
        text_copy.start()
        image_copy.wait()
        text_copy.wait()


def ff_forward(tick, info, ni, micro, x, parts, gain, bias, up, down, stacks):
    n, d = x.shape
    hidden = up[0].shape[1]
    return run(
        functools.partial(ff_forward_kernel, ni),
        "ff_forward",
        cost(16 * n * d * hidden, 16 * d * hidden + 16 * n * hidden + 16 * n * d, 4 * n * hidden),
        (tick, info),
        (x, *parts, gain, bias, *up, *down, *stacks),
        (
            shape_of((n, d), F32),
            shape_of((n, 4 * hidden), BF16),
            shape_of((n, d), BF16),
            shape_of(((micro + 1) * n, d), BF16),
            shape_of(((micro + 1) * n, 4 * hidden), BF16),
            shape_of((micro, ni, d), BF16),
            shape_of((micro, n - ni, d), BF16),
        ),
        [
            pltpu.VMEM((n, d), BF16),
            pltpu.VMEM((3, n, d), BF16),
            pltpu.VMEM((2, 2, d), F32),
            pltpu.VMEM((4, d, hidden), BF16),
            pltpu.VMEM((4, hidden, d), BF16),
            pltpu.VMEM((n, d), F32),
            pltpu.VMEM((n, d), BF16),
            pltpu.VMEM((4, n, hidden), BF16),
            pltpu.VMEM((4, n, hidden), BF16),
            pltpu.VMEM((n, d), BF16),
        ],
        26,
        ((14, 3), (15, 4), (16, 5), (17, 6)) if stacks else (),
    )


def ff_backward_kernel(
    source, tick, info, coti, cott, back, gp, mid, gain, u0, u1, u2, u3, d0, d1, d2, d3, *refs
):
    refs = refs[-(5 + 13) :]
    dmid, da, sums, dm, du = refs[:5]
    cot_v, back_v, gp_v, mid_v, norm, up, down, rows, dm_v, du_v, da_v, sums_v, sems = refs[5:]
    copies = Copies(sems)
    n, d = mid_v.shape
    ni = coti.shape[1]
    nt = n - ni
    hidden = up.shape[2]
    valid = info[AT_VALID + tick[0]].astype(F32)
    slot = info[AT_STACK + tick[0]]
    at_row = pl.multiple_of(slot * n, 8)
    loads = [
        copies.start(coti.at[source], cot_v.at[0:ni]),
        copies.start(cott.at[source], cot_v.at[ni:]),
        copies.start(back, back_v),
    ]
    weights = []
    for i, (u, w) in enumerate(zip((u0, u1, u2, u3), (d0, d1, d2, d3))):
        columns = slice(i * hidden, (i + 1) * hidden)
        weights.append(
            (
                copies.start(w, down.at[i]),
                copies.start(gp.at[:, columns], gp_v.at[i]),
                copies.start(u, up.at[i]),
            )
        )
    rest = [copies.start(mid, mid_v), copies.start(gain, norm)]
    copies.wait(*loads)
    first = info[AT_SECTION] == 0
    place = lax.broadcasted_iota(jnp.int32, (nt, 1), 0) + info[AT_MP] * nt
    kept = (place < info[AT_LENGTH + tick[0]]).astype(F32)
    rows[0:ni, :] = jnp.where(first, back_v[0:ni, :].astype(F32), cot_v[0:ni, :].astype(F32))
    rows[ni:, :] = jnp.where(first, back_v[ni:, :].astype(F32), cot_v[ni:, :].astype(F32) * kept)
    dm_v[...] = rows[...].astype(BF16)
    copies.start(dm_v, dm.at[pl.ds(at_row, n)])

    def descend(i):
        copies.wait(weights[i][0])
        return dot_nt(dm_v[...], down[i])

    total = None
    act_grad = descend(0)
    for i in range(4):
        later = descend(i + 1) if i < 3 else None
        copies.wait(weights[i][1], weights[i][2])
        du_v[i] = (gp_v[i].astype(F32) * act_grad).astype(BF16)
        copies.start(du_v.at[i], du.at[pl.ds(at_row, n), i * hidden : (i + 1) * hidden])
        part = dot_nt(du_v[i], up[i])
        total = part if total is None else total + part
        act_grad = later
    copies.wait(*rest)
    pulled, gain_sum, bias_sum = norm_pull(total, mid_v[...], norm[1:2, :])
    total = rows[...] + pulled
    rows[...] = total
    da_v[...] = total.astype(BF16)
    sums_v[0:1, :] = gain_sum * valid
    sums_v[1:2, :] = bias_sum * valid
    copies.start(da_v, da)
    copies.start(rows, dmid)
    copies.start(sums_v, sums)
    copies.finish()


def ff_backward(tick, info, source, micro, coti, cott, back, gp, mid, gain, up, down, stacks):
    n, d = mid.shape
    hidden = up[0].shape[1]
    return run(
        functools.partial(ff_backward_kernel, source),
        "ff_backward",
        cost(16 * n * d * hidden, 16 * d * hidden + 16 * n * hidden + 16 * n * d),
        (tick, info),
        (coti, cott, back, gp, mid, gain, *up, *down, *stacks),
        (
            shape_of((n, d), F32),
            shape_of((n, d), BF16),
            shape_of((2, d), F32),
            shape_of(((micro + 1) * n, d), BF16),
            shape_of(((micro + 1) * n, 4 * hidden), BF16),
        ),
        [
            pltpu.VMEM((n, d), BF16),
            pltpu.VMEM((n, d), BF16),
            pltpu.VMEM((4, n, hidden), BF16),
            pltpu.VMEM((n, d), F32),
            pltpu.VMEM((2, d), F32),
            pltpu.VMEM((4, d, hidden), BF16),
            pltpu.VMEM((4, hidden, d), BF16),
            pltpu.VMEM((n, d), F32),
            pltpu.VMEM((n, d), BF16),
            pltpu.VMEM((4, n, hidden), BF16),
            pltpu.VMEM((n, d), BF16),
            pltpu.VMEM((2, d), F32),
        ],
        26,
        ((14, 3), (15, 4)) if stacks else (),
    )


def ff_weights_kernel(h2, dm, du, g, one, two):
    piece = pl.program_id(0)
    up_part = dot_tn(h2[...], du[...]).astype(BF16)
    down_part = dot_tn(g[...], dm[...]).astype(BF16)
    for index, out in enumerate((one, two)):

        @pl.when(piece == index)
        def _():
            chunks, rows = out.shape[0], out.shape[1] // 2
            for z in range(chunks):
                span = slice(z * rows, (z + 1) * rows)
                out[z, 0:rows, :] = up_part[span, :]
                out[z, rows:, :] = down_part[span, :]


def ff_weights(pieces, samples, h2, dm, du, g, chunks):
    d = h2.shape[1]
    hidden = du.shape[1] // 4
    n = h2.shape[0] // (samples + 1) * samples
    one, two = pieces
    part = (chunks, 2 * d // chunks, hidden)
    column = lambda i: one + (two - one) * i
    return pl.pallas_call(
        ff_weights_kernel,
        grid=(2,),
        out_shape=(shape_of(part, BF16),) * 2,
        in_specs=[
            whole(n, d),
            whole(n, d),
            pl.BlockSpec((n, hidden), lambda i: (0, column(i))),
            pl.BlockSpec((n, hidden), lambda i: (0, column(i))),
        ],
        out_specs=(whole(*part), whole(*part)),
        compiler_params=params(),
        cost_estimate=cost(8 * n * d * hidden, 4 * n * d + 8 * n * hidden + 8 * d * hidden),
        name="ff_weights",
    )(h2, dm, du, g)


def close_kernel(ni, tick, info, x, a, b, c, dmid, gain, *refs):
    refs = refs[-(4 + 8) :]
    back, sums, image_grad, text_grad = refs[:4]
    x_v, abc, dmid_v, norm, total_v, back_v, sums_v, sems = refs[4:]
    copies = Copies(sems)
    slot = info[AT_STACK + tick[0]]
    loads = [
        copies.start(s, t)
        for s, t in (
            (a, abc.at[0]),
            (b.at[0], abc.at[1]),
            (c, abc.at[2]),
            (x, x_v),
            (gain, norm),
            (dmid, dmid_v),
        )
    ]
    copies.wait(*loads)
    grad = abc[0].astype(F32) + abc[1].astype(F32) + abc[2].astype(F32)
    pulled, gain_sum, bias_sum = norm_pull(grad, x_v[...].astype(F32), norm[0:1, :])
    total = dmid_v[...] + pulled
    total_v[...] = total
    back_v[...] = total.astype(BF16)
    valid = info[AT_VALID + tick[0]]
    sums_v[0:1, :] = gain_sum * valid.astype(F32)
    sums_v[1:2, :] = bias_sum * valid.astype(F32)
    copies.start(back_v, back)
    copies.start(sums_v, sums)

    @pl.when(valid > 0)
    def _():
        image_copy = pltpu.make_async_copy(total_v.at[0:ni], image_grad.at[slot], sems.at[0])
        text_copy = pltpu.make_async_copy(total_v.at[ni:], text_grad.at[slot], sems.at[1])
        image_copy.start()
        text_copy.start()
        image_copy.wait()
        text_copy.wait()

    copies.finish()


def close(tick, info, ni, micro, x, parts, dmid, gain, stacks):
    n, d = x.shape
    return run(
        functools.partial(close_kernel, ni),
        "input_grad",
        cost(20 * n * d, 18 * n * d),
        (tick, info),
        (x, *parts, dmid, gain, *stacks),
        (
            shape_of((n, d), BF16),
            shape_of((2, d), F32),
            shape_of((micro, ni, d), F32),
            shape_of((micro, n - ni, d), F32),
        ),
        [
            pltpu.VMEM((n, d), BF16),
            pltpu.VMEM((3, n, d), BF16),
            pltpu.VMEM((n, d), F32),
            pltpu.VMEM((2, d), F32),
            pltpu.VMEM((n, d), F32),
            pltpu.VMEM((n, d), BF16),
            pltpu.VMEM((2, d), F32),
        ],
        8,
        ((6, 2), (7, 3)) if stacks else (),
    )


def over_y(array):
    return lax.ppermute(array, "mp", [(m, m ^ 2) for m in range(4)])


def over_core(array):
    return lax.ppermute(array, "mp", [(m, m ^ 1) for m in range(4)])


def gathered(own):
    across = over_y(own)
    return (own, across, over_core(own), over_core(across))


def scattered(r0, r1, r23):
    other = over_core(r23)
    across = (r1.astype(F32) + other[1].astype(F32)).astype(BF16)
    return (r0, other, over_y(across))


def shifted(array, by):
    length = lax.axis_size("section")
    return lax.ppermute(array, "section", [(i, i + by) for i in range(length) if 0 <= i + by < length])


def over_everyone(sums):
    groups = lax.axis_size("dp")
    if groups & (groups - 1):
        return lax.psum_scatter(sums, ("dp", "mp"), scatter_dimension=2, tiled=True)
    for flip in (1, 2):
        sums = sums + lax.ppermute(sums, "mp", [(m, m ^ flip) for m in range(4)])
    flip = 1
    while flip < groups:
        sums = sums + lax.ppermute(sums, "dp", [(z, z ^ flip) for z in range(groups)])
        flip *= 2
    own = sums.shape[2] // (4 * groups)
    mine = lax.axis_index("dp") * 4 + lax.axis_index("mp")
    return lax.dynamic_slice_in_dim(sums, mine * own, own, axis=2)


def after(value, *earlier):
    return lax.optimization_barrier((value, *earlier))[0]


def shards(
    image, text, lengths, image_cot, text_cot, qkv_image, out_image, qkv_text, out_text,
    query_cross, kv_cross, out_cross, up_proj, down_proj, norm_gain, norm_bias,
):
    section = lax.axis_index("section")
    me = lax.axis_index("mp")
    groups = lax.axis_size("dp")
    micro = image.shape[0]
    ticks = micro + SKEW
    ni, d = image.shape[1:]
    nt = text.shape[1]
    gain, bias = norm_gain[0], norm_bias[0]
    width = out_image.shape[1]
    w_image = jnp.concatenate(
        (kv_cross[0].reshape(d, 2 * width), qkv_image[0].reshape(d, 3 * width)), axis=1
    )
    w_text = jnp.concatenate((qkv_text[0].reshape(d, 3 * width), query_cross[0]), axis=1)
    wo_image = out_image[0]
    wo_text = jnp.concatenate((out_text[0], out_cross[0]), axis=0)

    flips = jnp.array(FLIPS, jnp.int32)
    turn = jnp.arange(ticks) - section * SKEW
    valid = (turn >= 0) & (turn < micro)
    gap = jnp.zeros((16 - ticks,), jnp.int32)
    info = jnp.concatenate(
        (
            ((me ^ flips) - section) % 4,
            me ^ flips,
            jnp.stack((section, me)).astype(jnp.int32),
            jnp.zeros((AT_LENGTH - 10,), jnp.int32),
            lengths[jnp.clip(turn, 0, micro - 1)],
            gap,
            valid.astype(jnp.int32),
            gap,
            jnp.where(valid, turn, micro).astype(jnp.int32),
        )
    ).astype(jnp.int32)
    place = jnp.arange(4 * ni)
    turned = (place % PATCH_COLS - section * SHIFT) % PATCH_COLS
    edge = PATCH_ROWS - section * SHIFT
    row_region = (place // PATCH_COLS >= PATCH_ROWS - WIN).astype(jnp.int32) + (
        place // PATCH_COLS >= edge
    ).astype(jnp.int32)
    col_region = (turned >= PATCH_COLS - WIN).astype(jnp.int32) + (turned >= edge).astype(jnp.int32)
    region = row_region * 3 + col_region
    gidc = region[:, None]
    gidr = region[None, :]

    tick_at = [jnp.full((1,), t, jnp.int32) for t in range(ticks)]
    nothing = jnp.zeros((ni + nt, d), BF16)
    up = down = None
    image_stacks = text_stacks = ff_stacks = ()
    state = {}
    relayed = {}

    def attend(t):
        nonlocal image_stacks, text_stacks, up, down
        got = relayed.get(t - SKEW, nothing)
        x, h = entry(tick_at[t], info, min(t, micro - 1), image, text, got, gain, bias)
        pieces = gathered(h)
        if up is None:
            up_own, down_own, _ = lax.optimization_barrier((up_proj[0], down_proj[0], pieces[1]))
            up, down = gathered(up_own), gathered(down_own)
        r0, r1, r23, qkvi, oti, tti, hx, oi = image_forward(
            tick_at[t], info, ni, micro, pieces, w_image, wo_image, gidc, gidr, image_stacks
        )
        image_stacks = (hx, oi)
        r0, r1, r23, qkvt, ott, ttt, hy, o = text_forward(
            tick_at[t], info, nt, micro, pieces, w_text, wo_text, qkvi, (r0, r1, r23), text_stacks
        )
        text_stacks = (hy, o)
        state[t] = [x, qkvi, oti, tti, qkvt, ott, ttt]
        return scattered(r0, r1, r23)

    def feed(t, parts):
        nonlocal ff_stacks
        mid, gp, z, *ff_stacks = ff_forward(
            tick_at[t], info, ni, micro, state[t][0], parts, gain, bias, up, down, ff_stacks
        )
        state[t] += [mid, gp]
        if t + SKEW < ticks:
            relayed[t] = shifted(z, 1)

    for t in range(ticks):
        feed(t, attend(t))
    h2, g, image_result, text_result = ff_stacks

    sums_one = sums_two = jnp.zeros((2, d), F32)
    relayed = {}
    ff_stacks = text_back = image_back = close_stacks = ()
    for k in range(ticks):
        t = ticks - 1 - k
        x, qkvi, oti, tti, qkvt, ott, ttt, mid, gp = state[t]
        back = relayed.get(k - SKEW, nothing)
        dmid, da, sums, *ff_stacks = ff_backward(
            tick_at[t], info, max(t - SKEW, 0), micro, image_cot, text_cot, back, gp, mid, gain,
            up, down, ff_stacks,
        )
        sums_two = sums_two + sums
        pieces = gathered(da)
        if k == ticks - 1:
            dm, du = ff_stacks
            far, y_part = ff_weights((3, 1), micro, h2, dm, du, g, groups)
            near, core_part = ff_weights((0, 2), micro, h2, dm, after(du, far), g, groups)
            across = (y_part.astype(F32) + over_core(far).astype(F32)).astype(BF16)
            near, core_part, across, *pieces = lax.optimization_barrier(
                (near, core_part, across, *pieces)
            )
            a, b, c = near, over_core(core_part), over_y(across)
            ff_sum = (a.astype(F32) + b.astype(F32) + c.astype(F32)).astype(BF16)
        r0, r1, r23, dkv, *text_back = text_backward(
            tick_at[t], info, nt, micro, pieces, w_text, wo_text, qkvi, qkvt, ott, ttt, text_back
        )
        if k == ticks - 1:
            text_w = attention_weights(
                text_stacks[0], text_back[1], text_stacks[1], text_back[0], groups, "text_weights"
            )
            dkv, text_w = lax.optimization_barrier((dkv, text_w))
        r0, r1, r23, *image_back = image_backward(
            tick_at[t], info, ni, micro, pieces, w_image, wo_image, gidc, gidr, qkvi, oti, tti, dkv,
            (r0, r1, r23), image_back,
        )
        parts = scattered(r0, r1, r23)
        if k == ticks - 1:
            image_w = attention_weights(
                image_stacks[0], image_back[1], image_stacks[1], image_back[0], groups, "image_weights"
            )
            dmid = after(dmid, image_w, ff_sum)
        back, sums, *close_stacks = close(
            tick_at[t], info, ni, micro, x, parts, dmid, gain, close_stacks
        )
        sums_one = sums_one + sums
        if k + SKEW < ticks:
            relayed[k] = shifted(back, -1)

    def over_dp(array):
        return lax.psum_scatter(array, "dp", scatter_dimension=0, tiled=True)[0].astype(F32)

    ff_grad = over_dp(ff_sum)
    text_grad = over_dp(text_w)
    image_grad = over_dp(image_w)
    rows, wo_rows = d // groups, width // groups
    gain_grad, bias_grad = over_everyone(jnp.stack((sums_one, sums_two), axis=1))
    return (
        image_result[None],
        text_result[None],
        close_stacks[0][None],
        close_stacks[1][None],
        image_grad[:rows, 2 * width :].reshape(1, rows, 3, width),
        image_grad[rows:, :d][None],
        text_grad[:rows, : 3 * width].reshape(1, rows, 3, width),
        text_grad[rows : rows + wo_rows, :d][None],
        text_grad[:rows, 3 * width :][None],
        image_grad[:rows, : 2 * width].reshape(1, rows, 2, width),
        text_grad[rows + wo_rows :, :d][None],
        ff_grad[:rows][None],
        ff_grad[rows:][None],
        gain_grad[None],
        bias_grad[None],
    )


def solution(mesh):
    return jax.shard_map(
        shards,
        mesh=mesh,
        in_specs=(
            P("dp", "mp", None),
            P("dp", "mp", None),
            P("dp"),
            P("dp", "mp", None),
            P("dp", "mp", None),
            P("section", None, None, "mp"),
            P("section", "mp", None),
            P("section", None, None, "mp"),
            P("section", "mp", None),
            P("section", None, "mp"),
            P("section", None, None, "mp"),
            P("section", "mp", None),
            P("section", None, "mp"),
            P("section", "mp", None),
            P("section", None, None),
            P("section", None, None),
        ),
        out_specs=(
            P("section", "dp", "mp", None),
            P("section", "dp", "mp", None),
            P("section", "dp", "mp", None),
            P("section", "dp", "mp", None),
            P("section", "dp", None, "mp"),
            P("section", ("mp", "dp"), None),
            P("section", "dp", None, "mp"),
            P("section", ("mp", "dp"), None),
            P("section", "dp", "mp"),
            P("section", "dp", None, "mp"),
            P("section", ("mp", "dp"), None),
            P("section", "dp", "mp"),
            P("section", ("mp", "dp"), None),
            P("section", None, ("dp", "mp")),
            P("section", None, ("dp", "mp")),
        ),
        check_vma=False,
    )
```

```python
import functools

import jax
import jax.numpy as jnp
from jax import lax
from jax.experimental import pallas as pl
from jax.experimental.pallas import tpu as pltpu
from jax.sharding import PartitionSpec as P

HEAD_DIM = 64
WIN = 12
PATCH_ROWS = 24
PATCH_COLS = 24
SHIFT = WIN // 2

EPSILON = 1e-05
MASKED_SCORE = -1000000000.0
SCALE = HEAD_DIM**-0.5
GELU_C = 0.7978845608028654
GELU_A = 0.044715

VMEM_MIB = 56
SKEW = 2
SELF_BLOCK = 256
CROSS_BLOCK = 512
CROSS_BACK = 512

F32 = jnp.float32
BF16 = jnp.bfloat16

FLIPS = (0, 2, 1, 3)
AT_SLOT, AT_BLOCK, AT_SECTION, AT_MP, AT_LENGTH, AT_VALID, AT_STACK = 0, 4, 8, 9, 16, 32, 48


def dot(left, right):
    return lax.dot_general(left, right, (((1,), (0,)), ((), ())), preferred_element_type=F32)


def dot_nt(left, right):
    return lax.dot_general(left, right, (((1,), (1,)), ((), ())), preferred_element_type=F32)


def dot_tn(left, right):
    return lax.dot_general(left, right, (((0,), (0,)), ((), ())), preferred_element_type=F32)


def head_mask(head, width, scale):
    lane = lax.broadcasted_iota(jnp.int32, (1, width), 1)
    inside = (lane >= head * HEAD_DIM) & (lane < (head + 1) * HEAD_DIM)
    return jnp.where(inside, F32(scale), F32(0.0)).astype(BF16)


def normalized(values):
    average = jnp.mean(values, axis=-1, keepdims=True)
    centered = values - average
    variance = jnp.mean(centered * centered, axis=-1, keepdims=True)
    inverse = lax.rsqrt(variance + EPSILON)
    return centered * inverse, inverse


def norm_pull(grad, values, gain):
    unit, inverse = normalized(values)
    scaled = grad * gain
    first = jnp.mean(scaled, axis=-1, keepdims=True)
    second = jnp.mean(scaled * unit, axis=-1, keepdims=True)
    pulled = inverse * (scaled - first - unit * second)
    gain_sum = jnp.sum(grad * unit, axis=0, keepdims=True)
    bias_sum = jnp.sum(grad, axis=0, keepdims=True)
    return pulled, gain_sum, bias_sum


SMEM_SPEC = pl.BlockSpec(memory_space=pltpu.SMEM)
ANY_SPEC = pl.BlockSpec(memory_space=pl.ANY)


def whole(*extent):
    zeros = (0,) * len(extent)
    return pl.BlockSpec(extent, lambda *at: zeros, pipeline_mode=pl.Buffered(1))


def params():
    return pltpu.CompilerParams(vmem_limit_bytes=VMEM_MIB << 20)


def cost(flops, moved, exps=0):
    return pl.CostEstimate(flops=int(flops), bytes_accessed=int(moved), transcendentals=int(exps))


def shape_of(extent, dtype):
    return jax.ShapeDtypeStruct(extent, dtype)


class Copies:
    def __init__(self, sems):
        self.sems = sems
        self.used = 0
        self.going = []

    def start(self, source, target):
        copy = pltpu.make_async_copy(source, target, self.sems.at[self.used])
        self.used += 1
        copy.start()
        self.going.append(copy)
        return copy

    def wait(self, *copies):
        for copy in copies:
            copy.wait()
            self.going = [other for other in self.going if other is not copy]

    def finish(self):
        for copy in self.going:
            copy.wait()
        self.going = []


def run(kernel, name, estimate, scalars, arrays, outs, scratch, sems, aliases=()):
    lead = len(scalars)
    return pl.pallas_call(
        kernel,
        out_shape=tuple(outs),
        in_specs=[SMEM_SPEC] * lead + [ANY_SPEC] * len(arrays),
        out_specs=(ANY_SPEC,) * len(outs),
        scratch_shapes=list(scratch) + [pltpu.SemaphoreType.DMA((sems,))],
        input_output_aliases={lead + a: b for a, b in aliases},
        compiler_params=params(),
        cost_estimate=estimate,
        name=name,
    )(*scalars, *arrays)


def entry_kernel(source, tick, info, image, text, got, gain, bias, x, h, own, got_v, norm, xv, hv, sems):
    copies = Copies(sems)
    n, ni = got_v.shape[0], image.shape[1]
    both = [copies.start(gain, norm.at[0]), copies.start(bias, norm.at[1])]
    spans = (slice(0, ni), slice(ni, n))
    loads = [
        (copies.start(rows.at[source], own.at[span]), copies.start(got.at[span], got_v.at[span]))
        for rows, span in zip((image, text), spans)
    ]
    copies.wait(*both)
    first = info[AT_SECTION] == 0
    for span, load in zip(spans, loads):
        copies.wait(*load)
        values = jnp.where(first, own[span, :].astype(F32), got_v[span, :].astype(F32))
        xv[span, :] = values.astype(BF16)
        unit, _ = normalized(values)
        hv[span, :] = (unit * norm[0, 0:1, :] + norm[1, 0:1, :]).astype(BF16)
        copies.start(hv.at[span], h.at[span])
        copies.start(xv.at[span], x.at[span])
    copies.finish()


def entry(tick, info, source, image, text, got, gain, bias):
    n, d = got.shape
    return run(
        functools.partial(entry_kernel, source),
        "entry_norm",
        cost(10 * n * d, 8 * n * d),
        (tick, info),
        (image, text, got, gain, bias),
        (shape_of((n, d), BF16),) * 2,
        [pltpu.VMEM((n, d), BF16), pltpu.VMEM((n, d), BF16), pltpu.VMEM((2, 2, d), F32)]
        + [pltpu.VMEM((n, d), BF16)] * 2,
        10,
    )


def image_forward_kernel(
    tick, info, p0, p1, p2, p3, w, wo, gidc, gidr, *refs
):
    refs = refs[-(8 + 11) :]
    r0, r1, r23, qkv, ot, tt, hx, o = refs[:8]
    hx_v, w_v, wo_v, gidc_v, gidr_v, qkv_v, ot_v, tt_v, o_v, part, sems = refs[8:]
    copies = Copies(sems)
    rows, d = hx_v.shape
    shard = rows // 4
    band = ot_v.shape[2]
    width = wo_v.shape[0]
    heads = width // HEAD_DIM
    slot = info[AT_STACK + tick[0]]
    offs = [pl.multiple_of(info[AT_SLOT + i] * shard, 16) for i in range(4)]
    loads = [
        copies.start(piece.at[0:shard], hx_v.at[pl.ds(off, shard)])
        for off, piece in zip(offs, (p0, p1, p2, p3))
    ] + [copies.start(w, w_v)]
    more = [copies.start(a, b) for a, b in ((gidc, gidc_v), (gidr, gidr_v), (wo, wo_v))]
    copies.wait(*loads)
    projected = dot(hx_v[...], w_v[...])
    for j in range(5):
        qkv_v[j] = projected[:, j * width : (j + 1) * width].astype(BF16)
    copies.start(hx_v, hx.at[slot])
    copies.start(qkv_v, qkv)
    copies.wait(*more)
    spans = [slice(b * band, (b + 1) * band) for b in range(2)]
    allowed = [gidc_v[span, :] == gidr_v[0:1, span] for span in spans]
    bias = [jnp.where(mask, F32(0.0), F32(MASKED_SCORE)) for mask in allowed]
    v_tall = [qkv_v[4, span, :].astype(F32).T.astype(BF16) for span in spans]
    items = [(b, head) for b in range(2) for head in range(heads)]

    def score(b, head):
        query = qkv_v[2, spans[b], :] * head_mask(head, width, SCALE)
        return dot_nt(qkv_v[3, spans[b], :], query) + bias[b]

    scores = score(*items[0])
    for index, (b, head) in enumerate(items):
        later = score(*items[index + 1]) if index + 1 < len(items) else None
        largest = jnp.max(scores, axis=0, keepdims=True)
        weights = jnp.exp(scores - largest)
        total = jnp.sum(weights, axis=0, keepdims=True)
        tt_v[b * heads + head] = largest + jnp.log(total)
        own = slice(head * HEAD_DIM, (head + 1) * HEAD_DIM)
        mixed = dot(v_tall[b][own, :], weights.astype(BF16))
        ot_v[b, own, :] = mixed * (1.0 / total)
        scores = later
    for b, span in enumerate(spans):
        o_v[span, :] = ot_v[b].T.astype(BF16)
    copies.start(ot_v, ot)
    copies.start(tt_v, tt)
    copies.start(o_v, o.at[slot])
    part[...] = dot(o_v[...], wo_v[...]).astype(BF16)
    for off, piece in zip(offs, (r0, r1, r23.at[0], r23.at[1])):
        copies.start(part.at[pl.ds(off, shard)], piece.at[0:shard])
    copies.finish()


def image_forward(tick, info, shard, micro, pieces, w, wo, gidc, gidr, stacks):
    n, d = pieces[0].shape
    rows = 4 * shard
    width = wo.shape[0]
    band = rows // 2
    heads = width // HEAD_DIM
    return run(
        image_forward_kernel,
        "image_forward",
        cost(
            2 * rows * d * width * 6 + 8 * heads * band * band * 256,
            2 * rows * d * 3 + 12 * rows * width + 12 * d * width,
            2 * heads * band * band,
        ),
        (tick, info),
        (*pieces, w, wo, gidc, gidr, *stacks),
        (
            shape_of((n, d), BF16),
            shape_of((n, d), BF16),
            shape_of((2, n, d), BF16),
            shape_of((5, rows, width), BF16),
            shape_of((2, width, band), F32),
            shape_of((2 * heads, 1, band), F32),
            shape_of((micro + 1, rows, d), BF16),
            shape_of((micro + 1, rows, width), BF16),
        ),
        [
            pltpu.VMEM((rows, d), BF16),
            pltpu.VMEM(w.shape, BF16),
            pltpu.VMEM(wo.shape, BF16),
            pltpu.VMEM(gidc.shape, jnp.int32),
            pltpu.VMEM(gidr.shape, jnp.int32),
            pltpu.VMEM((5, rows, width), BF16),
            pltpu.VMEM((2, width, band), F32),
            pltpu.VMEM((2 * heads, 1, band), F32),
            pltpu.VMEM((rows, width), BF16),
            pltpu.VMEM((rows, d), BF16),
        ],
        18,
        ((8, 6), (9, 7)) if stacks else (),
    )


def image_backward_kernel(tick, info, p0, p1, p2, p3, w, wo, gidc, gidr, qkv, ot, tt, dkv, *refs):
    refs = refs[-(5 + 18) :]
    r0, r1, r23, da, dd = refs[:5]
    (
        da_v, w_v, wo_v, gidc_v, gidr_v, qkv_v, ot_v, tt_v, dkv_v, do_v, d_v, part,
        dq_tall, k_tall, do_tall, dk_sum, dv_sum, sems,
    ) = refs[5:]
    copies = Copies(sems)
    rows, d = da_v.shape
    shard = rows // 4
    band = ot_v.shape[2]
    width = wo_v.shape[0]
    heads = width // HEAD_DIM
    slot = info[AT_STACK + tick[0]]
    offs = [pl.multiple_of(info[AT_SLOT + i] * shard, 16) for i in range(4)]
    loads = [
        copies.start(piece.at[0:shard], da_v.at[pl.ds(off, shard)])
        for off, piece in zip(offs, (p0, p1, p2, p3))
    ] + [copies.start(wo, wo_v)]
    more = [
        copies.start(a, b)
        for a, b in ((qkv, qkv_v), (gidc, gidc_v), (gidr, gidr_v), (tt, tt_v), (ot, ot_v))
    ]
    rest = [copies.start(a, b) for a, b in ((dkv, dkv_v), (w, w_v))]
    copies.wait(*loads)
    copies.start(da_v, da.at[slot])
    do_v[...] = dot_nt(da_v[...], wo_v[...]).astype(BF16)
    copies.wait(*more)
    for b in range(2):
        span = slice(b * band, (b + 1) * band)
        bias = jnp.where(gidc_v[span, :] == gidr_v[0:1, span], F32(0.0), F32(MASKED_SCORE))
        k_tall[...] = qkv_v[3, span, :].astype(F32).T.astype(BF16)
        do_tall[...] = do_v[span, :].astype(F32).T
        dk_sum[...] = jnp.zeros_like(dk_sum)
        dv_sum[...] = jnp.zeros_like(dv_sum)
        for head in range(heads):
            at = head * HEAD_DIM
            own = slice(at, at + HEAD_DIM)
            query = qkv_v[2, span, :] * head_mask(head, width, SCALE)
            grad = do_v[span, :] * head_mask(head, width, 1.0)
            scores = dot_nt(qkv_v[3, span, :], query) + bias
            weights = jnp.exp(scores - tt_v[b * heads + head])
            pulled = dot_nt(qkv_v[4, span, :], grad)
            delta = jnp.sum(do_tall[own, :] * ot_v[b, own, :], axis=0, keepdims=True)
            score_grad = (weights * (pulled - delta)).astype(BF16)
            dv_sum[...] += dot(weights.astype(BF16), grad)
            dk_sum[...] += dot(score_grad, query)
            dq_tall[own, :] = dot(k_tall[own, :], score_grad) * SCALE
        d_v[span, 2 * width : 3 * width] = dq_tall[...].T.astype(BF16)
        d_v[span, 3 * width : 4 * width] = dk_sum[...].astype(BF16)
        d_v[span, 4 * width :] = dv_sum[...].astype(BF16)
    copies.wait(*rest)
    d_v[:, 0:width] = dkv_v[0]
    d_v[:, width : 2 * width] = dkv_v[1]
    copies.start(d_v, dd.at[slot])
    part[...] = dot_nt(d_v[...], w_v[...]).astype(BF16)
    for off, piece in zip(offs, (r0, r1, r23.at[0], r23.at[1])):
        copies.start(part.at[pl.ds(off, shard)], piece.at[0:shard])
    copies.finish()


def image_backward(tick, info, shard, micro, pieces, w, wo, gidc, gidr, qkv, ot, tt, dkv, parts, stacks):
    n, d = pieces[0].shape
    rows = 4 * shard
    width = wo.shape[0]
    band = rows // 2
    heads = width // HEAD_DIM
    return run(
        image_backward_kernel,
        "image_backward",
        cost(
            2 * rows * d * width * 6 + 20 * heads * band * band * 256,
            2 * rows * d * 3 + 20 * rows * width + 12 * d * width,
            2 * heads * band * band,
        ),
        (tick, info),
        (*pieces, w, wo, gidc, gidr, qkv, ot, tt, dkv, *parts, *stacks),
        (
            shape_of((n, d), BF16),
            shape_of((n, d), BF16),
            shape_of((2, n, d), BF16),
            shape_of((micro + 1, rows, d), BF16),
            shape_of((micro + 1, rows, 5 * width), BF16),
        ),
        [
            pltpu.VMEM((rows, d), BF16),
            pltpu.VMEM(w.shape, BF16),
            pltpu.VMEM(wo.shape, BF16),
            pltpu.VMEM(gidc.shape, jnp.int32),
            pltpu.VMEM(gidr.shape, jnp.int32),
            pltpu.VMEM((5, rows, width), BF16),
            pltpu.VMEM((2, width, band), F32),
            pltpu.VMEM((2 * heads, 1, band), F32),
            pltpu.VMEM((2, rows, width), BF16),
            pltpu.VMEM((rows, width), BF16),
            pltpu.VMEM((rows, 5 * width), BF16),
            pltpu.VMEM((rows, d), BF16),
            pltpu.VMEM((width, band), F32),
            pltpu.VMEM((width, band), BF16),
            pltpu.VMEM((width, band), F32),
            pltpu.VMEM((band, width), F32),
            pltpu.VMEM((band, width), F32),
        ],
        18,
        ((12, 0), (13, 1), (14, 2)) + (((15, 3), (16, 4)) if stacks else ()),
    )


def query_blocks(rows, size):
    return [(at, min(size, rows - at)) for at in range(0, rows, size)]


def causal(scores, start, last_key):
    key_at = lax.broadcasted_iota(jnp.int32, scores.shape, 0)
    query_at = lax.broadcasted_iota(jnp.int32, (1, scores.shape[1]), 1) + start
    return jnp.where(key_at <= jnp.minimum(query_at, last_key), scores, F32(MASKED_SCORE))


def text_forward_kernel(skip, tick, info, p0, p1, p2, p3, w, wo, kv, *refs):
    refs = refs[-(8 + 11) :]
    r0, r1, r23, qkv, ot, tt, hy, o = refs[:8]
    hy_v, w_v, wo_v, kv_v, qkv_v, ot_v, tt_v, o_v, part, piece_v, sems = refs[8:]
    copies = Copies(sems)
    rows, d = hy_v.shape
    shard = rows // 4
    patches = kv_v.shape[1]
    width = kv_v.shape[2]
    heads = width // HEAD_DIM
    slot = info[AT_STACK + tick[0]]
    last_key = info[AT_LENGTH + tick[0]] - 1
    offs = [pl.multiple_of(info[AT_BLOCK + i] * shard, 8) for i in range(4)]
    loads = [
        copies.start(piece.at[skip:], piece_v.at[i]) for i, piece in enumerate((p0, p1, p2, p3))
    ] + [copies.start(w, w_v)]
    more = [copies.start(kv.at[0:2], kv_v)]
    rest = [copies.start(wo, wo_v)]
    copies.wait(*loads)
    for i, off in enumerate(offs):
        part[pl.ds(off, shard), :] = piece_v[i].astype(F32)
    hy_v[...] = part[...].astype(BF16)
    projected = dot(hy_v[...], w_v[...])
    for j in range(4):
        qkv_v[j] = projected[:, j * width : (j + 1) * width].astype(BF16)
    copies.start(hy_v, hy.at[slot])
    copies.start(qkv_v, qkv)
    copies.wait(*more)
    v_tall = [values.astype(F32).T.astype(BF16) for values in (qkv_v[2], kv_v[1])]
    items = [
        (kind, head, start, size)
        for kind in range(2)
        for start, size in query_blocks(rows, CROSS_BLOCK if kind else SELF_BLOCK)
        for head in range(heads)
    ]

    def score(kind, head, start, size):
        query = qkv_v[3 if kind else 0, start : start + size, :] * head_mask(head, width, SCALE)
        keys = kv_v[0] if kind else qkv_v[1, 0 : start + size, :]
        scores = dot_nt(keys, query)
        return scores if kind else causal(scores, start, last_key)

    scores = score(*items[0])
    for index, (kind, head, start, size) in enumerate(items):
        later = score(*items[index + 1]) if index + 1 < len(items) else None
        at = head * HEAD_DIM
        largest = jnp.max(scores, axis=0, keepdims=True)
        weights = jnp.exp(scores - largest)
        total = jnp.sum(weights, axis=0, keepdims=True)
        tt_v[kind * heads + head, :, start : start + size] = largest + jnp.log(total)
        mixed = dot(v_tall[kind][at : at + HEAD_DIM, 0 : weights.shape[0]], weights.astype(BF16))
        out_at = kind * width + at
        ot_v[out_at : out_at + HEAD_DIM, start : start + size] = mixed * (1.0 / total)
        scores = later
    copies.start(ot_v, ot)
    copies.start(tt_v, tt)
    o_v[...] = ot_v[...].T.astype(BF16)
    copies.start(o_v, o.at[slot])
    copies.wait(*rest)
    part[...] = dot(o_v[...], wo_v[...])
    for i, (off, piece) in enumerate(zip(offs, (r0, r1, r23.at[0], r23.at[1]))):
        piece_v[i] = part[pl.ds(off, shard), :].astype(BF16)
        copies.start(piece_v.at[i], piece.at[skip:])
    copies.finish()


def text_forward(tick, info, shard, micro, pieces, w, wo, kv, parts, stacks):
    n, d = pieces[0].shape
    rows = 4 * shard
    patches, width = kv.shape[1:]
    heads = width // HEAD_DIM
    return run(
        functools.partial(text_forward_kernel, n - shard),
        "text_forward",
        cost(
            2 * rows * d * width * 6 + 4 * heads * rows * (rows * 0.6 + patches) * 256,
            2 * rows * d * 3 + 12 * rows * width + 12 * d * width,
            heads * rows * (rows * 0.6 + patches),
        ),
        (tick, info),
        (*pieces, w, wo, kv, *parts, *stacks),
        (
            shape_of((n, d), BF16),
            shape_of((n, d), BF16),
            shape_of((2, n, d), BF16),
            shape_of((4, rows, width), BF16),
            shape_of((2 * width, rows), F32),
            shape_of((2 * heads, 1, rows), F32),
            shape_of((micro + 1, rows, d), BF16),
            shape_of((micro + 1, rows, 2 * width), BF16),
        ),
        [
            pltpu.VMEM((rows, d), BF16),
            pltpu.VMEM(w.shape, BF16),
            pltpu.VMEM(wo.shape, BF16),
            pltpu.VMEM((2, patches, width), BF16),
            pltpu.VMEM((4, rows, width), BF16),
            pltpu.VMEM((2 * width, rows), F32),
            pltpu.VMEM((2 * heads, 1, rows), F32),
            pltpu.VMEM((rows, 2 * width), BF16),
            pltpu.VMEM((rows, d), F32),
            pltpu.VMEM((4, shard, d), BF16),
        ],
        16,
        ((7, 0), (8, 1), (9, 2)) + (((10, 6), (11, 7)) if stacks else ()),
    )


def text_backward_kernel(skip, tick, info, p0, p1, p2, p3, w, wo, kv, qkv, ot, tt, *refs):
    refs = refs[-(6 + 18) :]
    r0, r1, r23, dkv, da, dd = refs[:6]
    (
        da_v, w_v, wo_v, kv_v, qkv_v, ot_v, tt_v, do_v, d_v, dkv_v, part, piece_v,
        dq_tall, k_tall, do_tall, dk_sum, dv_sum, sems,
    ) = refs[6:]
    copies = Copies(sems)
    rows, d = da_v.shape
    shard = rows // 4
    patches, width = kv_v.shape[1:]
    heads = width // HEAD_DIM
    slot = info[AT_STACK + tick[0]]
    last_key = info[AT_LENGTH + tick[0]] - 1
    offs = [pl.multiple_of(info[AT_BLOCK + i] * shard, 8) for i in range(4)]
    loads = [
        copies.start(piece.at[skip:], piece_v.at[i]) for i, piece in enumerate((p0, p1, p2, p3))
    ] + [copies.start(wo, wo_v)]
    more = [copies.start(a, b) for a, b in ((qkv, qkv_v), (tt, tt_v), (ot, ot_v), (kv.at[0:2], kv_v))]
    rest = [copies.start(w, w_v)]
    copies.wait(*loads)
    for i, off in enumerate(offs):
        part[pl.ds(off, shard), :] = piece_v[i].astype(F32)
    da_v[...] = part[...].astype(BF16)
    copies.start(da_v, da.at[slot])
    grads = dot_nt(da_v[...], wo_v[...])
    do_v[...] = grads.astype(BF16)
    do_tall[...] = grads.astype(BF16).astype(F32).T
    copies.wait(*more)
    for kind in range(2):
        span = patches if kind else rows
        whole_keys = kv_v[0] if kind else qkv_v[1]
        k_tall[:, 0:span] = whole_keys.astype(F32).T.astype(BF16)
        dk_sum[...] = jnp.zeros_like(dk_sum)
        dv_sum[...] = jnp.zeros_like(dv_sum)
        for start, size in query_blocks(rows, CROSS_BACK if kind else SELF_BLOCK):
            seen = start + size if kind == 0 else patches
            block = slice(start, start + size)
            keys = kv_v[0] if kind else qkv_v[1, 0:seen, :]
            values = kv_v[1] if kind else qkv_v[2, 0:seen, :]
            for head in range(heads):
                at = head * HEAD_DIM
                own = slice(at, at + HEAD_DIM)
                out_own = slice(kind * width + at, kind * width + at + HEAD_DIM)
                query = qkv_v[3 if kind else 0, block, :] * head_mask(head, width, SCALE)
                grad = do_v[block, kind * width : (kind + 1) * width] * head_mask(head, width, 1.0)
                scores = dot_nt(keys, query)
                if kind == 0:
                    scores = causal(scores, start, last_key)
                weights = jnp.exp(scores - tt_v[kind * heads + head, :, block])
                pulled = dot_nt(values, grad)
                delta = jnp.sum(do_tall[out_own, block] * ot_v[out_own, block], axis=0, keepdims=True)
                score_grad = (weights * (pulled - delta)).astype(BF16)
                dv_sum[0:seen, :] += dot(weights.astype(BF16), grad)
                dk_sum[0:seen, :] += dot(score_grad, query)
                dq_tall[own, block] = dot(k_tall[own, 0:seen], score_grad) * SCALE
        if kind == 0:
            d_v[:, 0:width] = dq_tall[...].T.astype(BF16)
            d_v[:, width : 2 * width] = dk_sum[...].astype(BF16)
            d_v[:, 2 * width : 3 * width] = dv_sum[...].astype(BF16)
        else:
            d_v[:, 3 * width :] = dq_tall[...].T.astype(BF16)
            dkv_v[0] = dk_sum[0:patches, :].astype(BF16)
            dkv_v[1] = dv_sum[0:patches, :].astype(BF16)
    copies.start(dkv_v, dkv)
    copies.start(d_v, dd.at[slot])
    copies.wait(*rest)
    part[...] = dot_nt(d_v[...], w_v[...])
    for i, (off, piece) in enumerate(zip(offs, (r0, r1, r23.at[0], r23.at[1]))):
        piece_v[i] = part[pl.ds(off, shard), :].astype(BF16)
        copies.start(piece_v.at[i], piece.at[skip:])
    copies.finish()


def text_backward(tick, info, shard, micro, pieces, w, wo, kv, qkv, ot, tt, stacks):
    n, d = pieces[0].shape
    rows = 4 * shard
    patches, width = kv.shape[1:]
    heads = width // HEAD_DIM
    return run(
        functools.partial(text_backward_kernel, n - shard),
        "text_backward",
        cost(
            2 * rows * d * width * 6 + 10 * heads * rows * (rows * 0.6 + patches) * 256,
            2 * rows * d * 3 + 20 * rows * width + 12 * d * width,
            heads * rows * (rows * 0.6 + patches),
        ),
        (tick, info),
        (*pieces, w, wo, kv, qkv, ot, tt, *stacks),
        (
            shape_of((n, d), BF16),
            shape_of((n, d), BF16),
            shape_of((2, n, d), BF16),
            shape_of((2, patches, width), BF16),
            shape_of((micro + 1, rows, d), BF16),
            shape_of((micro + 1, rows, 4 * width), BF16),
        ),
        [
            pltpu.VMEM((rows, d), BF16),
            pltpu.VMEM(w.shape, BF16),
            pltpu.VMEM(wo.shape, BF16),
            pltpu.VMEM((2, patches, width), BF16),
            pltpu.VMEM((4, rows, width), BF16),
            pltpu.VMEM((2 * width, rows), F32),
            pltpu.VMEM((2 * heads, 1, rows), F32),
            pltpu.VMEM((rows, 2 * width), BF16),
            pltpu.VMEM((rows, 4 * width), BF16),
            pltpu.VMEM((2, patches, width), BF16),
            pltpu.VMEM((rows, d), F32),
            pltpu.VMEM((4, shard, d), BF16),
            pltpu.VMEM((width, rows), F32),
            pltpu.VMEM((width, rows), BF16),
            pltpu.VMEM((2 * width, rows), F32),
            pltpu.VMEM((rows, width), F32),
            pltpu.VMEM((rows, width), F32),
        ],
        18,
        ((10, 4), (11, 5)) if stacks else (),
    )


def attention_weights_kernel(h, dd, o, da, out, w_sum, wo_sum):
    step = pl.program_id(0)
    w_part = dot_tn(h[0], dd[0])
    wo_part = dot_tn(o[0], da[0])

    @pl.when(step == 0)
    def _():
        w_sum[...] = w_part
        wo_sum[...] = wo_part

    @pl.when(step > 0)
    def _():
        w_sum[...] += w_part
        wo_sum[...] += wo_part

    @pl.when(step == pl.num_programs(0) - 1)
    def _():
        chunks = out.shape[0]
        d, columns = w_sum.shape
        rows, wide = d // chunks, wo_sum.shape[1]
        at = rows
        for z in range(chunks):
            out[z, 0:rows, :] = w_sum[z * rows : (z + 1) * rows, :].astype(BF16)
        narrow = d // 4 // chunks
        for part in range(wo_sum.shape[0] // (d // 4)):
            for z in range(chunks):
                top = part * (d // 4) + z * narrow
                out[z, at : at + narrow, 0:wide] = wo_sum[top : top + narrow, :].astype(BF16)
                if columns > wide:
                    out[z, at : at + narrow, wide:] = jnp.zeros((narrow, columns - wide), BF16)
            at += narrow


def attention_weights(h, dd, o, da, chunks, name):
    slots, rows, d = h.shape
    columns, wide = dd.shape[2], o.shape[2]
    out = (chunks, (d + wide) // chunks, columns)
    slot = lambda a: pl.BlockSpec((1, *a.shape[1:]), lambda i: (i, 0, 0))
    return pl.pallas_call(
        attention_weights_kernel,
        grid=(slots - 1,),
        out_shape=shape_of(out, BF16),
        in_specs=[slot(a) for a in (h, dd, o, da)],
        out_specs=whole(*out),
        scratch_shapes=[pltpu.VMEM((d, columns), F32), pltpu.VMEM((wide, d), F32)],
        compiler_params=params(),
        cost_estimate=cost(
            2 * slots * rows * d * (columns + wide), 2 * slots * rows * (2 * d + columns + wide)
        ),
        name=name,
    )(h, dd, o, da)


def ff_forward_kernel(ni, tick, info, x, a, b, c, gain, bias, u0, u1, u2, u3, d0, d1, d2, d3, *refs):
    refs = refs[-(7 + 11) :]
    mid, gp, z, h2, g, image_out, text_out = refs[:7]
    x_v, abc, norm, up, down, mid_v, h2_v, g_v, gp_v, z_v, sems = refs[7:]
    copies = Copies(sems)
    n, d = x_v.shape
    hidden = up.shape[2]
    slot = info[AT_STACK + tick[0]]
    at_row = pl.multiple_of(slot * n, 8)
    loads = [
        copies.start(s, t)
        for s, t in (
            (x, x_v),
            (a, abc.at[0]),
            (b.at[0], abc.at[1]),
            (c, abc.at[2]),
            (gain, norm.at[0]),
            (bias, norm.at[1]),
        )
    ]
    weights = [
        (copies.start(u, up.at[i]), copies.start(w, down.at[i]))
        for i, (u, w) in enumerate(zip((u0, u1, u2, u3), (d0, d1, d2, d3)))
    ]
    copies.wait(*loads)
    values = x_v[...].astype(F32) + (
        abc[0].astype(F32) + abc[1].astype(F32) + abc[2].astype(F32)
    )
    mid_v[...] = values
    unit, _ = normalized(values)
    h2_v[...] = (unit * norm[0, 1:2, :] + norm[1, 1:2, :]).astype(BF16)
    copies.start(mid_v, mid)
    copies.start(h2_v, h2.at[pl.ds(at_row, n)])

    def ascend(i):
        copies.wait(weights[i][0])
        return dot(h2_v[...], up[i])

    def bend(i, u):
        square = u * u
        bent = jnp.tanh(u * (GELU_C + (GELU_C * GELU_A) * square))
        half = 0.5 * (1.0 + bent)
        g_v[i] = (u * half).astype(BF16)
        slope = half + (0.5 * u) * (1.0 - bent * bent) * (GELU_C + (3.0 * GELU_C * GELU_A) * square)
        gp_v[i] = slope.astype(BF16)
        columns = slice(i * hidden, (i + 1) * hidden)
        copies.start(g_v.at[i], g.at[pl.ds(at_row, n), columns])
        copies.start(gp_v.at[i], gp.at[:, columns])

    total = mid_v[...]
    u = ascend(0)
    for i in range(4):
        bend(i, u)
        copies.wait(weights[i][1])
        total = total + dot(g_v[i], down[i])
        u = ascend(i + 1) if i < 3 else None
    z_v[...] = total.astype(BF16)
    copies.start(z_v, z)
    copies.finish()

    @pl.when(info[AT_VALID + tick[0]] > 0)
    def _():
        image_copy = pltpu.make_async_copy(z_v.at[0:ni], image_out.at[slot], sems.at[0])
        text_copy = pltpu.make_async_copy(z_v.at[ni:], text_out.at[slot], sems.at[1])
        image_copy.start()
        text_copy.start()
        image_copy.wait()
        text_copy.wait()


def ff_forward(tick, info, ni, micro, x, parts, gain, bias, up, down, stacks):
    n, d = x.shape
    hidden = up[0].shape[1]
    return run(
        functools.partial(ff_forward_kernel, ni),
        "ff_forward",
        cost(16 * n * d * hidden, 16 * d * hidden + 16 * n * hidden + 16 * n * d, 4 * n * hidden),
        (tick, info),
        (x, *parts, gain, bias, *up, *down, *stacks),
        (
            shape_of((n, d), F32),
            shape_of((n, 4 * hidden), BF16),
            shape_of((n, d), BF16),
            shape_of(((micro + 1) * n, d), BF16),
            shape_of(((micro + 1) * n, 4 * hidden), BF16),
            shape_of((micro, ni, d), BF16),
            shape_of((micro, n - ni, d), BF16),
        ),
        [
            pltpu.VMEM((n, d), BF16),
            pltpu.VMEM((3, n, d), BF16),
            pltpu.VMEM((2, 2, d), F32),
            pltpu.VMEM((4, d, hidden), BF16),
            pltpu.VMEM((4, hidden, d), BF16),
            pltpu.VMEM((n, d), F32),
            pltpu.VMEM((n, d), BF16),
            pltpu.VMEM((4, n, hidden), BF16),
            pltpu.VMEM((4, n, hidden), BF16),
            pltpu.VMEM((n, d), BF16),
        ],
        26,
        ((14, 3), (15, 4), (16, 5), (17, 6)) if stacks else (),
    )


def ff_backward_kernel(
    source, tick, info, coti, cott, back, gp, mid, gain, u0, u1, u2, u3, d0, d1, d2, d3, *refs
):
    refs = refs[-(5 + 13) :]
    dmid, da, sums, dm, du = refs[:5]
    cot_v, back_v, gp_v, mid_v, norm, up, down, rows, dm_v, du_v, da_v, sums_v, sems = refs[5:]
    copies = Copies(sems)
    n, d = mid_v.shape
    ni = coti.shape[1]
    nt = n - ni
    hidden = up.shape[2]
    valid = info[AT_VALID + tick[0]].astype(F32)
    slot = info[AT_STACK + tick[0]]
    at_row = pl.multiple_of(slot * n, 8)
    loads = [
        copies.start(coti.at[source], cot_v.at[0:ni]),
        copies.start(cott.at[source], cot_v.at[ni:]),
        copies.start(back, back_v),
    ]
    weights = []
    for i, (u, w) in enumerate(zip((u0, u1, u2, u3), (d0, d1, d2, d3))):
        columns = slice(i * hidden, (i + 1) * hidden)
        weights.append(
            (
                copies.start(w, down.at[i]),
                copies.start(gp.at[:, columns], gp_v.at[i]),
                copies.start(u, up.at[i]),
            )
        )
    rest = [copies.start(mid, mid_v), copies.start(gain, norm)]
    copies.wait(*loads)
    first = info[AT_SECTION] == 0
    place = lax.broadcasted_iota(jnp.int32, (nt, 1), 0) + info[AT_MP] * nt
    kept = (place < info[AT_LENGTH + tick[0]]).astype(F32)
    rows[0:ni, :] = jnp.where(first, back_v[0:ni, :].astype(F32), cot_v[0:ni, :].astype(F32))
    rows[ni:, :] = jnp.where(first, back_v[ni:, :].astype(F32), cot_v[ni:, :].astype(F32) * kept)
    dm_v[...] = rows[...].astype(BF16)
    copies.start(dm_v, dm.at[pl.ds(at_row, n)])

    def descend(i):
        copies.wait(weights[i][0])
        return dot_nt(dm_v[...], down[i])

    total = None
    act_grad = descend(0)
    for i in range(4):
        later = descend(i + 1) if i < 3 else None
        copies.wait(weights[i][1], weights[i][2])
        du_v[i] = (gp_v[i].astype(F32) * act_grad).astype(BF16)
        copies.start(du_v.at[i], du.at[pl.ds(at_row, n), i * hidden : (i + 1) * hidden])
        part = dot_nt(du_v[i], up[i])
        total = part if total is None else total + part
        act_grad = later
    copies.wait(*rest)
    pulled, gain_sum, bias_sum = norm_pull(total, mid_v[...], norm[1:2, :])
    total = rows[...] + pulled
    rows[...] = total
    da_v[...] = total.astype(BF16)
    sums_v[0:1, :] = gain_sum * valid
    sums_v[1:2, :] = bias_sum * valid
    copies.start(da_v, da)
    copies.start(rows, dmid)
    copies.start(sums_v, sums)
    copies.finish()


def ff_backward(tick, info, source, micro, coti, cott, back, gp, mid, gain, up, down, stacks):
    n, d = mid.shape
    hidden = up[0].shape[1]
    return run(
        functools.partial(ff_backward_kernel, source),
        "ff_backward",
        cost(16 * n * d * hidden, 16 * d * hidden + 16 * n * hidden + 16 * n * d),
        (tick, info),
        (coti, cott, back, gp, mid, gain, *up, *down, *stacks),
        (
            shape_of((n, d), F32),
            shape_of((n, d), BF16),
            shape_of((2, d), F32),
            shape_of(((micro + 1) * n, d), BF16),
            shape_of(((micro + 1) * n, 4 * hidden), BF16),
        ),
        [
            pltpu.VMEM((n, d), BF16),
            pltpu.VMEM((n, d), BF16),
            pltpu.VMEM((4, n, hidden), BF16),
            pltpu.VMEM((n, d), F32),
            pltpu.VMEM((2, d), F32),
            pltpu.VMEM((4, d, hidden), BF16),
            pltpu.VMEM((4, hidden, d), BF16),
            pltpu.VMEM((n, d), F32),
            pltpu.VMEM((n, d), BF16),
            pltpu.VMEM((4, n, hidden), BF16),
            pltpu.VMEM((n, d), BF16),
            pltpu.VMEM((2, d), F32),
        ],
        26,
        ((14, 3), (15, 4)) if stacks else (),
    )


def ff_weights_kernel(h2, dm, du, g, one, two):
    piece = pl.program_id(0)
    up_part = dot_tn(h2[...], du[...]).astype(BF16)
    down_part = dot_tn(g[...], dm[...]).astype(BF16)
    for index, out in enumerate((one, two)):

        @pl.when(piece == index)
        def _():
            chunks, rows = out.shape[0], out.shape[1] // 2
            for z in range(chunks):
                span = slice(z * rows, (z + 1) * rows)
                out[z, 0:rows, :] = up_part[span, :]
                out[z, rows:, :] = down_part[span, :]


def ff_weights(pieces, samples, h2, dm, du, g, chunks):
    d = h2.shape[1]
    hidden = du.shape[1] // 4
    n = h2.shape[0] // (samples + 1) * samples
    one, two = pieces
    part = (chunks, 2 * d // chunks, hidden)
    column = lambda i: one + (two - one) * i
    return pl.pallas_call(
        ff_weights_kernel,
        grid=(2,),
        out_shape=(shape_of(part, BF16),) * 2,
        in_specs=[
            whole(n, d),
            whole(n, d),
            pl.BlockSpec((n, hidden), lambda i: (0, column(i))),
            pl.BlockSpec((n, hidden), lambda i: (0, column(i))),
        ],
        out_specs=(whole(*part), whole(*part)),
        compiler_params=params(),
        cost_estimate=cost(8 * n * d * hidden, 4 * n * d + 8 * n * hidden + 8 * d * hidden),
        name="ff_weights",
    )(h2, dm, du, g)


def close_kernel(ni, tick, info, x, a, b, c, dmid, gain, *refs):
    refs = refs[-(4 + 8) :]
    back, sums, image_grad, text_grad = refs[:4]
    x_v, abc, dmid_v, norm, total_v, back_v, sums_v, sems = refs[4:]
    copies = Copies(sems)
    n = x_v.shape[0]
    slot = info[AT_STACK + tick[0]]
    valid = info[AT_VALID + tick[0]]
    ready = copies.start(gain, norm)
    spans = (slice(0, ni), slice(ni, n))
    loads = [
        [
            copies.start(source.at[span], target.at[span])
            for source, target in (
                (a, abc.at[0]),
                (b.at[0], abc.at[1]),
                (c, abc.at[2]),
                (x, x_v),
                (dmid, dmid_v),
            )
        ]
        for span in spans
    ]
    copies.wait(ready)
    gain_total = bias_total = None
    for index, (span, load) in enumerate(zip(spans, loads)):
        copies.wait(*load)
        grad = abc[0, span, :].astype(F32) + abc[1, span, :].astype(F32) + abc[2, span, :].astype(F32)
        pulled, gain_sum, bias_sum = norm_pull(grad, x_v[span, :].astype(F32), norm[0:1, :])
        total = dmid_v[span, :] + pulled
        total_v[span, :] = total
        back_v[span, :] = total.astype(BF16)
        copies.start(back_v.at[span], back.at[span])
        out = (image_grad, text_grad)[index]
        copy = pltpu.make_async_copy(total_v.at[span], out.at[slot], sems.at[16 + index])

        @pl.when(valid > 0)
        def _():
            copy.start()

        gain_total = gain_sum if index == 0 else gain_total + gain_sum
        bias_total = bias_sum if index == 0 else bias_total + bias_sum
    sums_v[0:1, :] = gain_total * valid.astype(F32)
    sums_v[1:2, :] = bias_total * valid.astype(F32)
    copies.start(sums_v, sums)
    copies.finish()
    for index, (span, out) in enumerate(zip(spans, (image_grad, text_grad))):

        @pl.when(valid > 0)
        def _():
            pltpu.make_async_copy(total_v.at[span], out.at[slot], sems.at[16 + index]).wait()


def close(tick, info, ni, micro, x, parts, dmid, gain, stacks):
    n, d = x.shape
    return run(
        functools.partial(close_kernel, ni),
        "input_grad",
        cost(20 * n * d, 18 * n * d),
        (tick, info),
        (x, *parts, dmid, gain, *stacks),
        (
            shape_of((n, d), BF16),
            shape_of((2, d), F32),
            shape_of((micro, ni, d), F32),
            shape_of((micro, n - ni, d), F32),
        ),
        [
            pltpu.VMEM((n, d), BF16),
            pltpu.VMEM((3, n, d), BF16),
            pltpu.VMEM((n, d), F32),
            pltpu.VMEM((2, d), F32),
            pltpu.VMEM((n, d), F32),
            pltpu.VMEM((n, d), BF16),
            pltpu.VMEM((2, d), F32),
        ],
        18,
        ((6, 2), (7, 3)) if stacks else (),
    )


def over_y(array):
    return lax.ppermute(array, "mp", [(m, m ^ 2) for m in range(4)])


def over_core(array):
    return lax.ppermute(array, "mp", [(m, m ^ 1) for m in range(4)])


def gathered(own):
    across = over_y(own)
    return (own, across, over_core(own), over_core(across))


def for_y(r1, r23):
    other = over_core(r23)
    return other, (r1.astype(F32) + other[1].astype(F32)).astype(BF16)


def shifted(array, by):
    length = lax.axis_size("section")
    return lax.ppermute(array, "section", [(i, i + by) for i in range(length) if 0 <= i + by < length])


def over_everyone(sums):
    groups = lax.axis_size("dp")
    if groups & (groups - 1):
        return lax.psum_scatter(sums, ("dp", "mp"), scatter_dimension=2, tiled=True)
    for flip in (1, 2):
        sums = sums + lax.ppermute(sums, "mp", [(m, m ^ flip) for m in range(4)])
    flip = 1
    while flip < groups:
        sums = sums + lax.ppermute(sums, "dp", [(z, z ^ flip) for z in range(groups)])
        flip *= 2
    own = sums.shape[2] // (4 * groups)
    mine = lax.axis_index("dp") * 4 + lax.axis_index("mp")
    return lax.dynamic_slice_in_dim(sums, mine * own, own, axis=2)


def hold(values, *earlier):
    return lax.optimization_barrier((tuple(values), *earlier))[0]


def shards(
    image, text, lengths, image_cot, text_cot, qkv_image, out_image, qkv_text, out_text,
    query_cross, kv_cross, out_cross, up_proj, down_proj, norm_gain, norm_bias,
):
    section = lax.axis_index("section")
    me = lax.axis_index("mp")
    groups = lax.axis_size("dp")
    micro = image.shape[0]
    ticks = micro + SKEW
    ni, d = image.shape[1:]
    nt = text.shape[1]
    gain, bias = norm_gain[0], norm_bias[0]
    width = out_image.shape[1]
    w_image = jnp.concatenate(
        (kv_cross[0].reshape(d, 2 * width), qkv_image[0].reshape(d, 3 * width)), axis=1
    )
    w_text = jnp.concatenate((qkv_text[0].reshape(d, 3 * width), query_cross[0]), axis=1)
    wo_image = out_image[0]
    wo_text = jnp.concatenate((out_text[0], out_cross[0]), axis=0)

    flips = jnp.array(FLIPS, jnp.int32)
    turn = jnp.arange(ticks) - section * SKEW
    valid = (turn >= 0) & (turn < micro)
    gap = jnp.zeros((16 - ticks,), jnp.int32)
    info = jnp.concatenate(
        (
            ((me ^ flips) - section) % 4,
            me ^ flips,
            jnp.stack((section, me)).astype(jnp.int32),
            jnp.zeros((AT_LENGTH - 10,), jnp.int32),
            lengths[jnp.clip(turn, 0, micro - 1)],
            gap,
            valid.astype(jnp.int32),
            gap,
            jnp.where(valid, turn, micro).astype(jnp.int32),
        )
    ).astype(jnp.int32)
    place = jnp.arange(4 * ni)
    turned = (place % PATCH_COLS - section * SHIFT) % PATCH_COLS
    edge = PATCH_ROWS - section * SHIFT
    row_region = (place // PATCH_COLS >= PATCH_ROWS - WIN).astype(jnp.int32) + (
        place // PATCH_COLS >= edge
    ).astype(jnp.int32)
    col_region = (turned >= PATCH_COLS - WIN).astype(jnp.int32) + (turned >= edge).astype(jnp.int32)
    region = row_region * 3 + col_region
    gidc = region[:, None]
    gidr = region[None, :]

    tick_at = [jnp.full((1,), t, jnp.int32) for t in range(ticks)]
    nothing = jnp.zeros((ni + nt, d), BF16)
    up = down = None
    image_stacks = text_stacks = ff_stacks = ()
    state = {}
    relayed = {}
    ahead = {}

    def attend(t):
        nonlocal image_stacks, text_stacks, up, down
        got = relayed.get(t - SKEW, nothing)
        if t >= SKEW and t % SKEW == 0:
            got = hold((got,), ahead["out"])[0]
        x, h = entry(tick_at[t], info, min(t, micro - 1), image, text, got, gain, bias)
        pieces = gathered(h)
        if up is None:
            up_own, down_own, _ = lax.optimization_barrier((up_proj[0], down_proj[0], pieces[1]))
            up, down = gathered(up_own), gathered(down_own)
        second = t % SKEW > 0
        if second:
            pieces = hold(pieces, ahead["own"])
        r0, r1, r23, qkvi, oti, tti, hx, oi = image_forward(
            tick_at[t], info, ni, micro, pieces, w_image, wo_image, gidc, gidr, image_stacks
        )
        image_stacks = (hx, oi)
        if second and t > SKEW:
            r0, r1, r23 = hold((r0, r1, r23), ahead["across"])
        r0, r1, r23, qkvt, ott, ttt, hy, o = text_forward(
            tick_at[t], info, nt, micro, pieces, w_text, wo_text, qkvi, (r0, r1, r23), text_stacks
        )
        text_stacks = (hy, o)
        state[t] = [x, qkvi, oti, tti, qkvt, ott, ttt]
        other, across = for_y(r1, r23)
        ahead.update(own=r0, across=across)
        return (r0, other, over_y(across))

    def feed(t, parts):
        nonlocal ff_stacks
        mid, gp, z, *ff_stacks = ff_forward(
            tick_at[t], info, ni, micro, state[t][0], parts, gain, bias, up, down, ff_stacks
        )
        state[t] += [mid, gp]
        ahead["out"] = z
        if t + SKEW < ticks:
            relayed[t] = shifted(z, 1)

    for t in range(0, ticks, SKEW):
        sums = [attend(t + i) for i in range(SKEW)]
        for i in range(SKEW):
            feed(t + i, sums[i])
    h2, g, image_result, text_result = ff_stacks

    sums_one = sums_two = jnp.zeros((2, d), F32)
    relayed = {}
    ff_stacks = text_back = image_back = close_stacks = ()
    ahead = {}

    def descend(k):
        nonlocal ff_stacks, sums_two
        t = ticks - 1 - k
        mid, gp = state[t][7:9]
        back = relayed.get(k - SKEW, nothing)
        if k >= SKEW and k % SKEW == 0:
            back = hold((back,), ahead["out"])[0]
        dmid, da, sums, *ff_stacks = ff_backward(
            tick_at[t], info, max(t - SKEW, 0), micro, image_cot, text_cot, back, gp, mid, gain,
            up, down, ff_stacks,
        )
        sums_two = sums_two + sums
        return dmid, gathered(da)

    def text_part(k, pieces):
        nonlocal text_back
        t = ticks - 1 - k
        qkvi, _, _, qkvt, ott, ttt = state[t][1:7]
        r0, r1, r23, dkv, *text_back = text_backward(
            tick_at[t], info, nt, micro, pieces, w_text, wo_text, qkvi, qkvt, ott, ttt, text_back
        )
        return (r0, r1, r23), dkv

    def image_part(k, pieces, parts, dkv):
        nonlocal image_back
        t = ticks - 1 - k
        qkvi, oti, tti = state[t][1:4]
        r0, r1, r23, *image_back = image_backward(
            tick_at[t], info, ni, micro, pieces, w_image, wo_image, gidc, gidr, qkvi, oti, tti, dkv,
            parts, image_back,
        )
        other, across = for_y(r1, r23)
        return r0, other, across

    def finish(k, parts, dmid):
        nonlocal close_stacks, sums_one
        t = ticks - 1 - k
        back, sums, *close_stacks = close(
            tick_at[t], info, ni, micro, state[t][0], parts, dmid, gain, close_stacks
        )
        sums_one = sums_one + sums
        ahead["out"] = back
        if k + SKEW < ticks:
            relayed[k] = shifted(back, -1)

    final = ticks - SKEW
    fed = {}
    for k in range(final):
        second = k % SKEW > 0
        if not second:
            fed = {k + i: descend(k + i) for i in range(SKEW)}
        dmid, pieces = fed[k]
        if second:
            pieces = hold(pieces, ahead["own"])
        parts, dkv = text_part(k, pieces)
        if second:
            parts = hold(parts, ahead["across"])
        r0, other, across = image_part(k, pieces, parts, dkv)
        ahead.update(own=r0, across=across)
        fed[k] = (k, (r0, other, over_y(across)), dmid)
        if k % SKEW == SKEW - 1:
            for i in range(k - SKEW + 1, k + 1):
                finish(*fed[i])

    one, two = final, final + 1
    (dmid_one, pieces_one), (dmid_two, pieces_two) = descend(one), descend(two)
    parts_one, dkv_one = text_part(one, pieces_one)
    pieces_two = hold(pieces_two, parts_one[0])
    parts_two, dkv_two = text_part(two, pieces_two)
    text_w = attention_weights(
        text_stacks[0], text_back[1], text_stacks[1], text_back[0], groups, "text_weights"
    )
    dm, du = hold(ff_stacks, text_w)
    far, y_part = ff_weights((3, 1), micro, h2, dm, du, g, groups)
    parts_one = hold(parts_one, far)
    r0_one, other_one, across_one = image_part(one, pieces_one, parts_one, dkv_one)
    ff_across = (y_part.astype(F32) + over_core(far).astype(F32)).astype(BF16)
    parts_two = hold(parts_two, r0_one, ff_across)
    r0_two, other_two, across_two = image_part(two, pieces_two, parts_two, dkv_two)
    quarter = ff_across.shape[1] // 4
    crossed = [over_y(ff_across[:, i * quarter : (i + 1) * quarter]) for i in range(4)]
    image_stacks = hold((*image_stacks, *image_back), crossed[0], across_one)
    image_w = attention_weights(
        image_stacks[0], image_stacks[3], image_stacks[1], image_stacks[2], groups, "image_weights"
    )
    du = hold((du,), image_w, crossed[1], across_two)[0]
    near, core_part = ff_weights((0, 2), micro, h2, dm, du, g, groups)
    core_part = hold((core_part,), crossed[2])[0]
    dmid_one = hold((dmid_one,), near)[0]
    finish(one, (r0_one, other_one, over_y(across_one)), dmid_one)
    dmid_two = hold((dmid_two,), crossed[3])[0]
    finish(two, (r0_two, other_two, over_y(across_two)), dmid_two)
    ff_sum = (
        near.astype(F32) + over_core(core_part).astype(F32) + jnp.concatenate(crossed, axis=1).astype(F32)
    ).astype(BF16)

    def over_dp(array):
        return lax.psum_scatter(array, "dp", scatter_dimension=0, tiled=True)[0].astype(F32)

    ff_grad = over_dp(ff_sum)
    text_grad = over_dp(text_w)
    image_grad = over_dp(image_w)
    rows, wo_rows = d // groups, width // groups
    gain_grad, bias_grad = over_everyone(jnp.stack((sums_one, sums_two), axis=1))
    return (
        image_result[None],
        text_result[None],
        close_stacks[0][None],
        close_stacks[1][None],
        image_grad[:rows, 2 * width :].reshape(1, rows, 3, width),
        image_grad[rows:, :d][None],
        text_grad[:rows, : 3 * width].reshape(1, rows, 3, width),
        text_grad[rows : rows + wo_rows, :d][None],
        text_grad[:rows, 3 * width :][None],
        image_grad[:rows, : 2 * width].reshape(1, rows, 2, width),
        text_grad[rows + wo_rows :, :d][None],
        ff_grad[:rows][None],
        ff_grad[rows:][None],
        gain_grad[None],
        bias_grad[None],
    )


def solution(mesh):
    return jax.shard_map(
        shards,
        mesh=mesh,
        in_specs=(
            P("dp", "mp", None),
            P("dp", "mp", None),
            P("dp"),
            P("dp", "mp", None),
            P("dp", "mp", None),
            P("section", None, None, "mp"),
            P("section", "mp", None),
            P("section", None, None, "mp"),
            P("section", "mp", None),
            P("section", None, "mp"),
            P("section", None, None, "mp"),
            P("section", "mp", None),
            P("section", None, "mp"),
            P("section", "mp", None),
            P("section", None, None),
            P("section", None, None),
        ),
        out_specs=(
            P("section", "dp", "mp", None),
            P("section", "dp", "mp", None),
            P("section", "dp", "mp", None),
            P("section", "dp", "mp", None),
            P("section", "dp", None, "mp"),
            P("section", ("mp", "dp"), None),
            P("section", "dp", None, "mp"),
            P("section", ("mp", "dp"), None),
            P("section", "dp", "mp"),
            P("section", "dp", None, "mp"),
            P("section", ("mp", "dp"), None),
            P("section", "dp", "mp"),
            P("section", ("mp", "dp"), None),
            P("section", None, ("dp", "mp")),
            P("section", None, ("dp", "mp")),
        ),
        check_vma=False,
    )
```

```python
import functools

import jax
import jax.numpy as jnp
from jax import lax
from jax.experimental import pallas as pl
from jax.experimental.pallas import tpu as pltpu
from jax.sharding import PartitionSpec as P

HEAD_DIM = 64
WIN = 12
PATCH_ROWS = 24
PATCH_COLS = 24
SHIFT = WIN // 2

EPSILON = 1e-05
MASKED_SCORE = -1000000000.0
SCALE = HEAD_DIM**-0.5
GELU_C = 0.7978845608028654
GELU_A = 0.044715

VMEM_MIB = 56
SKEW = 2
SELF_BLOCK = 256
CROSS_BLOCK = 512
CROSS_BACK = 512

F32 = jnp.float32
BF16 = jnp.bfloat16

FLIPS = (0, 2, 1, 3)
AT_SLOT, AT_BLOCK, AT_SECTION, AT_MP, AT_LENGTH, AT_VALID, AT_STACK = 0, 4, 8, 9, 16, 32, 48


def dot(left, right):
    return lax.dot_general(left, right, (((1,), (0,)), ((), ())), preferred_element_type=F32)


def dot_nt(left, right):
    return lax.dot_general(left, right, (((1,), (1,)), ((), ())), preferred_element_type=F32)


def dot_tn(left, right):
    return lax.dot_general(left, right, (((0,), (0,)), ((), ())), preferred_element_type=F32)


def head_mask(head, width, scale):
    lane = lax.broadcasted_iota(jnp.int32, (1, width), 1)
    inside = (lane >= head * HEAD_DIM) & (lane < (head + 1) * HEAD_DIM)
    return jnp.where(inside, F32(scale), F32(0.0)).astype(BF16)


def normalized(values):
    average = jnp.mean(values, axis=-1, keepdims=True)
    centered = values - average
    variance = jnp.mean(centered * centered, axis=-1, keepdims=True)
    inverse = lax.rsqrt(variance + EPSILON)
    return centered * inverse, inverse


def norm_pull(grad, values, gain):
    unit, inverse = normalized(values)
    scaled = grad * gain
    first = jnp.mean(scaled, axis=-1, keepdims=True)
    second = jnp.mean(scaled * unit, axis=-1, keepdims=True)
    pulled = inverse * (scaled - first - unit * second)
    gain_sum = jnp.sum(grad * unit, axis=0, keepdims=True)
    bias_sum = jnp.sum(grad, axis=0, keepdims=True)
    return pulled, gain_sum, bias_sum


SMEM_SPEC = pl.BlockSpec(memory_space=pltpu.SMEM)
ANY_SPEC = pl.BlockSpec(memory_space=pl.ANY)


def whole(*extent):
    zeros = (0,) * len(extent)
    return pl.BlockSpec(extent, lambda *at: zeros, pipeline_mode=pl.Buffered(1))


def params():
    return pltpu.CompilerParams(vmem_limit_bytes=VMEM_MIB << 20)


def cost(flops, moved, exps=0):
    return pl.CostEstimate(flops=int(flops), bytes_accessed=int(moved), transcendentals=int(exps))


def shape_of(extent, dtype):
    return jax.ShapeDtypeStruct(extent, dtype)


class Copies:
    def __init__(self, sems):
        self.sems = sems
        self.used = 0
        self.going = []

    def start(self, source, target):
        copy = pltpu.make_async_copy(source, target, self.sems.at[self.used])
        self.used += 1
        copy.start()
        self.going.append(copy)
        return copy

    def wait(self, *copies):
        for copy in copies:
            copy.wait()
            self.going = [other for other in self.going if other is not copy]

    def finish(self):
        for copy in self.going:
            copy.wait()
        self.going = []


def run(kernel, name, estimate, scalars, arrays, outs, scratch, sems, aliases=()):
    lead = len(scalars)
    return pl.pallas_call(
        kernel,
        out_shape=tuple(outs),
        in_specs=[SMEM_SPEC] * lead + [ANY_SPEC] * len(arrays),
        out_specs=(ANY_SPEC,) * len(outs),
        scratch_shapes=list(scratch) + [pltpu.SemaphoreType.DMA((sems,))],
        input_output_aliases={lead + a: b for a, b in aliases},
        compiler_params=params(),
        cost_estimate=estimate,
        name=name,
    )(*scalars, *arrays)


def entry_kernel(source, tick, info, image, text, got, gain, bias, x, h, own, got_v, norm, xv, hv, sems):
    copies = Copies(sems)
    n, ni = got_v.shape[0], image.shape[1]
    both = [copies.start(gain, norm.at[0]), copies.start(bias, norm.at[1])]
    spans = (slice(0, ni), slice(ni, n))
    loads = [
        (copies.start(rows.at[source], own.at[span]), copies.start(got.at[span], got_v.at[span]))
        for rows, span in zip((image, text), spans)
    ]
    copies.wait(*both)
    first = info[AT_SECTION] == 0
    for span, load in zip(spans, loads):
        copies.wait(*load)
        values = jnp.where(first, own[span, :].astype(F32), got_v[span, :].astype(F32))
        xv[span, :] = values.astype(BF16)
        unit, _ = normalized(values)
        hv[span, :] = (unit * norm[0, 0:1, :] + norm[1, 0:1, :]).astype(BF16)
        copies.start(hv.at[span], h.at[span])
        copies.start(xv.at[span], x.at[span])
    copies.finish()


def entry(tick, info, source, image, text, got, gain, bias):
    n, d = got.shape
    return run(
        functools.partial(entry_kernel, source),
        "entry_norm",
        cost(10 * n * d, 8 * n * d),
        (tick, info),
        (image, text, got, gain, bias),
        (shape_of((n, d), BF16),) * 2,
        [pltpu.VMEM((n, d), BF16), pltpu.VMEM((n, d), BF16), pltpu.VMEM((2, 2, d), F32)]
        + [pltpu.VMEM((n, d), BF16)] * 2,
        10,
    )


def image_forward_kernel(
    tick, info, p0, p1, p2, p3, w, wo, gidc, gidr, *refs
):
    refs = refs[-(8 + 11) :]
    r0, r1, r23, qkv, ot, tt, hx, o = refs[:8]
    hx_v, w_v, wo_v, gidc_v, gidr_v, qkv_v, ot_v, tt_v, o_v, part, sems = refs[8:]
    copies = Copies(sems)
    rows, d = hx_v.shape
    shard = rows // 4
    band = ot_v.shape[2]
    width = wo_v.shape[0]
    heads = width // HEAD_DIM
    slot = info[AT_STACK + tick[0]]
    offs = [pl.multiple_of(info[AT_SLOT + i] * shard, 16) for i in range(4)]
    loads = [
        copies.start(piece.at[0:shard], hx_v.at[pl.ds(off, shard)])
        for off, piece in zip(offs, (p0, p1, p2, p3))
    ] + [copies.start(w, w_v)]
    more = [copies.start(a, b) for a, b in ((gidc, gidc_v), (gidr, gidr_v), (wo, wo_v))]
    copies.wait(*loads)
    projected = dot(hx_v[...], w_v[...])
    for j in range(5):
        qkv_v[j] = projected[:, j * width : (j + 1) * width].astype(BF16)
    copies.start(hx_v, hx.at[slot])
    copies.start(qkv_v, qkv)
    copies.wait(*more)
    spans = [slice(b * band, (b + 1) * band) for b in range(2)]
    allowed = [gidc_v[span, :] == gidr_v[0:1, span] for span in spans]
    bias = [jnp.where(mask, F32(0.0), F32(MASKED_SCORE)) for mask in allowed]
    v_tall = [qkv_v[4, span, :].astype(F32).T.astype(BF16) for span in spans]
    items = [(b, head) for b in range(2) for head in range(heads)]

    def score(b, head):
        query = qkv_v[2, spans[b], :] * head_mask(head, width, SCALE)
        return dot_nt(qkv_v[3, spans[b], :], query) + bias[b]

    scores = score(*items[0])
    for index, (b, head) in enumerate(items):
        later = score(*items[index + 1]) if index + 1 < len(items) else None
        largest = jnp.max(scores, axis=0, keepdims=True)
        weights = jnp.exp(scores - largest)
        total = jnp.sum(weights, axis=0, keepdims=True)
        tt_v[b * heads + head] = largest + jnp.log(total)
        own = slice(head * HEAD_DIM, (head + 1) * HEAD_DIM)
        mixed = dot(v_tall[b][own, :], weights.astype(BF16))
        ot_v[b, own, :] = mixed * (1.0 / total)
        scores = later
    for b, span in enumerate(spans):
        o_v[span, :] = ot_v[b].T.astype(BF16)
    copies.start(ot_v, ot)
    copies.start(tt_v, tt)
    copies.start(o_v, o.at[slot])
    part[...] = dot(o_v[...], wo_v[...]).astype(BF16)
    for off, piece in zip(offs, (r0, r1, r23.at[0], r23.at[1])):
        copies.start(part.at[pl.ds(off, shard)], piece.at[0:shard])
    copies.finish()


def image_forward(tick, info, shard, micro, pieces, w, wo, gidc, gidr, stacks):
    n, d = pieces[0].shape
    rows = 4 * shard
    width = wo.shape[0]
    band = rows // 2
    heads = width // HEAD_DIM
    return run(
        image_forward_kernel,
        "image_forward",
        cost(
            2 * rows * d * width * 6 + 8 * heads * band * band * 256,
            2 * rows * d * 3 + 12 * rows * width + 12 * d * width,
            2 * heads * band * band,
        ),
        (tick, info),
        (*pieces, w, wo, gidc, gidr, *stacks),
        (
            shape_of((n, d), BF16),
            shape_of((n, d), BF16),
            shape_of((2, n, d), BF16),
            shape_of((5, rows, width), BF16),
            shape_of((2, width, band), F32),
            shape_of((2 * heads, 1, band), F32),
            shape_of((micro + 1, rows, d), BF16),
            shape_of((micro + 1, rows, width), BF16),
        ),
        [
            pltpu.VMEM((rows, d), BF16),
            pltpu.VMEM(w.shape, BF16),
            pltpu.VMEM(wo.shape, BF16),
            pltpu.VMEM(gidc.shape, jnp.int32),
            pltpu.VMEM(gidr.shape, jnp.int32),
            pltpu.VMEM((5, rows, width), BF16),
            pltpu.VMEM((2, width, band), F32),
            pltpu.VMEM((2 * heads, 1, band), F32),
            pltpu.VMEM((rows, width), BF16),
            pltpu.VMEM((rows, d), BF16),
        ],
        18,
        ((8, 6), (9, 7)) if stacks else (),
    )


def image_backward_kernel(tick, info, p0, p1, p2, p3, w, wo, gidc, gidr, qkv, ot, tt, dkv, *refs):
    refs = refs[-(5 + 18) :]
    r0, r1, r23, da, dd = refs[:5]
    (
        da_v, w_v, wo_v, gidc_v, gidr_v, qkv_v, ot_v, tt_v, dkv_v, do_v, d_v, part,
        dq_tall, k_tall, do_tall, dk_sum, dv_sum, sems,
    ) = refs[5:]
    copies = Copies(sems)
    rows, d = da_v.shape
    shard = rows // 4
    band = ot_v.shape[2]
    width = wo_v.shape[0]
    heads = width // HEAD_DIM
    slot = info[AT_STACK + tick[0]]
    offs = [pl.multiple_of(info[AT_SLOT + i] * shard, 16) for i in range(4)]
    loads = [
        copies.start(piece.at[0:shard], da_v.at[pl.ds(off, shard)])
        for off, piece in zip(offs, (p0, p1, p2, p3))
    ] + [copies.start(wo, wo_v)]
    more = [
        copies.start(a, b)
        for a, b in ((qkv, qkv_v), (gidc, gidc_v), (gidr, gidr_v), (tt, tt_v), (ot, ot_v))
    ]
    rest = [copies.start(a, b) for a, b in ((dkv, dkv_v), (w, w_v))]
    copies.wait(*loads)
    copies.start(da_v, da.at[slot])
    do_v[...] = dot_nt(da_v[...], wo_v[...]).astype(BF16)
    copies.wait(*more)
    for b in range(2):
        span = slice(b * band, (b + 1) * band)
        bias = jnp.where(gidc_v[span, :] == gidr_v[0:1, span], F32(0.0), F32(MASKED_SCORE))
        k_tall[...] = qkv_v[3, span, :].astype(F32).T.astype(BF16)
        do_tall[...] = do_v[span, :].astype(F32).T
        dk_sum[...] = jnp.zeros_like(dk_sum)
        dv_sum[...] = jnp.zeros_like(dv_sum)
        for head in range(heads):
            at = head * HEAD_DIM
            own = slice(at, at + HEAD_DIM)
            query = qkv_v[2, span, :] * head_mask(head, width, SCALE)
            grad = do_v[span, :] * head_mask(head, width, 1.0)
            scores = dot_nt(qkv_v[3, span, :], query) + bias
            weights = jnp.exp(scores - tt_v[b * heads + head])
            pulled = dot_nt(qkv_v[4, span, :], grad)
            delta = jnp.sum(do_tall[own, :] * ot_v[b, own, :], axis=0, keepdims=True)
            score_grad = (weights * (pulled - delta)).astype(BF16)
            dv_sum[...] += dot(weights.astype(BF16), grad)
            dk_sum[...] += dot(score_grad, query)
            dq_tall[own, :] = dot(k_tall[own, :], score_grad) * SCALE
        d_v[span, 2 * width : 3 * width] = dq_tall[...].T.astype(BF16)
        d_v[span, 3 * width : 4 * width] = dk_sum[...].astype(BF16)
        d_v[span, 4 * width :] = dv_sum[...].astype(BF16)
    copies.wait(*rest)
    d_v[:, 0:width] = dkv_v[0]
    d_v[:, width : 2 * width] = dkv_v[1]
    copies.start(d_v, dd.at[slot])
    part[...] = dot_nt(d_v[...], w_v[...]).astype(BF16)
    for off, piece in zip(offs, (r0, r1, r23.at[0], r23.at[1])):
        copies.start(part.at[pl.ds(off, shard)], piece.at[0:shard])
    copies.finish()


def image_backward(tick, info, shard, micro, pieces, w, wo, gidc, gidr, qkv, ot, tt, dkv, parts, stacks):
    n, d = pieces[0].shape
    rows = 4 * shard
    width = wo.shape[0]
    band = rows // 2
    heads = width // HEAD_DIM
    return run(
        image_backward_kernel,
        "image_backward",
        cost(
            2 * rows * d * width * 6 + 20 * heads * band * band * 256,
            2 * rows * d * 3 + 20 * rows * width + 12 * d * width,
            2 * heads * band * band,
        ),
        (tick, info),
        (*pieces, w, wo, gidc, gidr, qkv, ot, tt, dkv, *parts, *stacks),
        (
            shape_of((n, d), BF16),
            shape_of((n, d), BF16),
            shape_of((2, n, d), BF16),
            shape_of((micro + 1, rows, d), BF16),
            shape_of((micro + 1, rows, 5 * width), BF16),
        ),
        [
            pltpu.VMEM((rows, d), BF16),
            pltpu.VMEM(w.shape, BF16),
            pltpu.VMEM(wo.shape, BF16),
            pltpu.VMEM(gidc.shape, jnp.int32),
            pltpu.VMEM(gidr.shape, jnp.int32),
            pltpu.VMEM((5, rows, width), BF16),
            pltpu.VMEM((2, width, band), F32),
            pltpu.VMEM((2 * heads, 1, band), F32),
            pltpu.VMEM((2, rows, width), BF16),
            pltpu.VMEM((rows, width), BF16),
            pltpu.VMEM((rows, 5 * width), BF16),
            pltpu.VMEM((rows, d), BF16),
            pltpu.VMEM((width, band), F32),
            pltpu.VMEM((width, band), BF16),
            pltpu.VMEM((width, band), F32),
            pltpu.VMEM((band, width), F32),
            pltpu.VMEM((band, width), F32),
        ],
        18,
        ((12, 0), (13, 1), (14, 2)) + (((15, 3), (16, 4)) if stacks else ()),
    )


def query_blocks(rows, size):
    return [(at, min(size, rows - at)) for at in range(0, rows, size)]


def causal(scores, start, last_key):
    key_at = lax.broadcasted_iota(jnp.int32, scores.shape, 0)
    query_at = lax.broadcasted_iota(jnp.int32, (1, scores.shape[1]), 1) + start
    return jnp.where(key_at <= jnp.minimum(query_at, last_key), scores, F32(MASKED_SCORE))


def text_forward_kernel(skip, tick, info, p0, p1, p2, p3, w, wo, kv, *refs):
    refs = refs[-(8 + 11) :]
    r0, r1, r23, qkv, ot, tt, hy, o = refs[:8]
    hy_v, w_v, wo_v, kv_v, qkv_v, ot_v, tt_v, o_v, part, piece_v, sems = refs[8:]
    copies = Copies(sems)
    rows, d = hy_v.shape
    shard = rows // 4
    patches = kv_v.shape[1]
    width = kv_v.shape[2]
    heads = width // HEAD_DIM
    slot = info[AT_STACK + tick[0]]
    last_key = info[AT_LENGTH + tick[0]] - 1
    offs = [pl.multiple_of(info[AT_BLOCK + i] * shard, 8) for i in range(4)]
    loads = [
        copies.start(piece.at[skip:], piece_v.at[i]) for i, piece in enumerate((p0, p1, p2, p3))
    ] + [copies.start(w, w_v)]
    more = [copies.start(kv.at[0:2], kv_v)]
    rest = [copies.start(wo, wo_v)]
    copies.wait(*loads)
    for i, off in enumerate(offs):
        part[pl.ds(off, shard), :] = piece_v[i].astype(F32)
    hy_v[...] = part[...].astype(BF16)
    projected = dot(hy_v[...], w_v[...])
    for j in range(4):
        qkv_v[j] = projected[:, j * width : (j + 1) * width].astype(BF16)
    copies.start(hy_v, hy.at[slot])
    copies.start(qkv_v, qkv)
    copies.wait(*more)
    v_tall = [values.astype(F32).T.astype(BF16) for values in (qkv_v[2], kv_v[1])]
    items = [
        (kind, head, start, size)
        for kind in range(2)
        for start, size in query_blocks(rows, CROSS_BLOCK if kind else SELF_BLOCK)
        for head in range(heads)
    ]

    def score(kind, head, start, size):
        query = qkv_v[3 if kind else 0, start : start + size, :] * head_mask(head, width, SCALE)
        keys = kv_v[0] if kind else qkv_v[1, 0 : start + size, :]
        scores = dot_nt(keys, query)
        return scores if kind else causal(scores, start, last_key)

    scores = score(*items[0])
    for index, (kind, head, start, size) in enumerate(items):
        later = score(*items[index + 1]) if index + 1 < len(items) else None
        at = head * HEAD_DIM
        largest = jnp.max(scores, axis=0, keepdims=True)
        weights = jnp.exp(scores - largest)
        total = jnp.sum(weights, axis=0, keepdims=True)
        tt_v[kind * heads + head, :, start : start + size] = largest + jnp.log(total)
        mixed = dot(v_tall[kind][at : at + HEAD_DIM, 0 : weights.shape[0]], weights.astype(BF16))
        out_at = kind * width + at
        ot_v[out_at : out_at + HEAD_DIM, start : start + size] = mixed * (1.0 / total)
        scores = later
    copies.start(ot_v, ot)
    copies.start(tt_v, tt)
    o_v[...] = ot_v[...].T.astype(BF16)
    copies.start(o_v, o.at[slot])
    copies.wait(*rest)
    part[...] = dot(o_v[...], wo_v[...])
    for i, (off, piece) in enumerate(zip(offs, (r0, r1, r23.at[0], r23.at[1]))):
        piece_v[i] = part[pl.ds(off, shard), :].astype(BF16)
        copies.start(piece_v.at[i], piece.at[skip:])
    copies.finish()


def text_forward(tick, info, shard, micro, pieces, w, wo, kv, parts, stacks):
    n, d = pieces[0].shape
    rows = 4 * shard
    patches, width = kv.shape[1:]
    heads = width // HEAD_DIM
    return run(
        functools.partial(text_forward_kernel, n - shard),
        "text_forward",
        cost(
            2 * rows * d * width * 6 + 4 * heads * rows * (rows * 0.6 + patches) * 256,
            2 * rows * d * 3 + 12 * rows * width + 12 * d * width,
            heads * rows * (rows * 0.6 + patches),
        ),
        (tick, info),
        (*pieces, w, wo, kv, *parts, *stacks),
        (
            shape_of((n, d), BF16),
            shape_of((n, d), BF16),
            shape_of((2, n, d), BF16),
            shape_of((4, rows, width), BF16),
            shape_of((2 * width, rows), F32),
            shape_of((2 * heads, 1, rows), F32),
            shape_of((micro + 1, rows, d), BF16),
            shape_of((micro + 1, rows, 2 * width), BF16),
        ),
        [
            pltpu.VMEM((rows, d), BF16),
            pltpu.VMEM(w.shape, BF16),
            pltpu.VMEM(wo.shape, BF16),
            pltpu.VMEM((2, patches, width), BF16),
            pltpu.VMEM((4, rows, width), BF16),
            pltpu.VMEM((2 * width, rows), F32),
            pltpu.VMEM((2 * heads, 1, rows), F32),
            pltpu.VMEM((rows, 2 * width), BF16),
            pltpu.VMEM((rows, d), F32),
            pltpu.VMEM((4, shard, d), BF16),
        ],
        16,
        ((7, 0), (8, 1), (9, 2)) + (((10, 6), (11, 7)) if stacks else ()),
    )


def text_backward_kernel(skip, tick, info, p0, p1, p2, p3, w, wo, kv, qkv, ot, tt, *refs):
    refs = refs[-(6 + 18) :]
    r0, r1, r23, dkv, da, dd = refs[:6]
    (
        da_v, w_v, wo_v, kv_v, qkv_v, ot_v, tt_v, do_v, d_v, dkv_v, part, piece_v,
        dq_tall, k_tall, do_tall, dk_sum, dv_sum, sems,
    ) = refs[6:]
    copies = Copies(sems)
    rows, d = da_v.shape
    shard = rows // 4
    patches, width = kv_v.shape[1:]
    heads = width // HEAD_DIM
    slot = info[AT_STACK + tick[0]]
    last_key = info[AT_LENGTH + tick[0]] - 1
    offs = [pl.multiple_of(info[AT_BLOCK + i] * shard, 8) for i in range(4)]
    loads = [
        copies.start(piece.at[skip:], piece_v.at[i]) for i, piece in enumerate((p0, p1, p2, p3))
    ] + [copies.start(wo, wo_v)]
    more = [copies.start(a, b) for a, b in ((qkv, qkv_v), (tt, tt_v), (ot, ot_v), (kv.at[0:2], kv_v))]
    rest = [copies.start(w, w_v)]
    copies.wait(*loads)
    for i, off in enumerate(offs):
        part[pl.ds(off, shard), :] = piece_v[i].astype(F32)
    da_v[...] = part[...].astype(BF16)
    copies.start(da_v, da.at[slot])
    grads = dot_nt(da_v[...], wo_v[...])
    do_v[...] = grads.astype(BF16)
    do_tall[...] = grads.astype(BF16).astype(F32).T
    copies.wait(*more)
    for kind in range(2):
        span = patches if kind else rows
        whole_keys = kv_v[0] if kind else qkv_v[1]
        k_tall[:, 0:span] = whole_keys.astype(F32).T.astype(BF16)
        dk_sum[...] = jnp.zeros_like(dk_sum)
        dv_sum[...] = jnp.zeros_like(dv_sum)
        for start, size in query_blocks(rows, CROSS_BACK if kind else SELF_BLOCK):
            seen = start + size if kind == 0 else patches
            block = slice(start, start + size)
            keys = kv_v[0] if kind else qkv_v[1, 0:seen, :]
            values = kv_v[1] if kind else qkv_v[2, 0:seen, :]
            for head in range(heads):
                at = head * HEAD_DIM
                own = slice(at, at + HEAD_DIM)
                out_own = slice(kind * width + at, kind * width + at + HEAD_DIM)
                query = qkv_v[3 if kind else 0, block, :] * head_mask(head, width, SCALE)
                grad = do_v[block, kind * width : (kind + 1) * width] * head_mask(head, width, 1.0)
                scores = dot_nt(keys, query)
                if kind == 0:
                    scores = causal(scores, start, last_key)
                weights = jnp.exp(scores - tt_v[kind * heads + head, :, block])
                pulled = dot_nt(values, grad)
                delta = jnp.sum(do_tall[out_own, block] * ot_v[out_own, block], axis=0, keepdims=True)
                score_grad = (weights * (pulled - delta)).astype(BF16)
                dv_sum[0:seen, :] += dot(weights.astype(BF16), grad)
                dk_sum[0:seen, :] += dot(score_grad, query)
                dq_tall[own, block] = dot(k_tall[own, 0:seen], score_grad) * SCALE
        if kind == 0:
            d_v[:, 0:width] = dq_tall[...].T.astype(BF16)
            d_v[:, width : 2 * width] = dk_sum[...].astype(BF16)
            d_v[:, 2 * width : 3 * width] = dv_sum[...].astype(BF16)
        else:
            d_v[:, 3 * width :] = dq_tall[...].T.astype(BF16)
            dkv_v[0] = dk_sum[0:patches, :].astype(BF16)
            dkv_v[1] = dv_sum[0:patches, :].astype(BF16)
    copies.start(dkv_v, dkv)
    copies.start(d_v, dd.at[slot])
    copies.wait(*rest)
    part[...] = dot_nt(d_v[...], w_v[...])
    for i, (off, piece) in enumerate(zip(offs, (r0, r1, r23.at[0], r23.at[1]))):
        piece_v[i] = part[pl.ds(off, shard), :].astype(BF16)
        copies.start(piece_v.at[i], piece.at[skip:])
    copies.finish()


def text_backward(tick, info, shard, micro, pieces, w, wo, kv, qkv, ot, tt, stacks):
    n, d = pieces[0].shape
    rows = 4 * shard
    patches, width = kv.shape[1:]
    heads = width // HEAD_DIM
    return run(
        functools.partial(text_backward_kernel, n - shard),
        "text_backward",
        cost(
            2 * rows * d * width * 6 + 10 * heads * rows * (rows * 0.6 + patches) * 256,
            2 * rows * d * 3 + 20 * rows * width + 12 * d * width,
            heads * rows * (rows * 0.6 + patches),
        ),
        (tick, info),
        (*pieces, w, wo, kv, qkv, ot, tt, *stacks),
        (
            shape_of((n, d), BF16),
            shape_of((n, d), BF16),
            shape_of((2, n, d), BF16),
            shape_of((2, patches, width), BF16),
            shape_of((micro + 1, rows, d), BF16),
            shape_of((micro + 1, rows, 4 * width), BF16),
        ),
        [
            pltpu.VMEM((rows, d), BF16),
            pltpu.VMEM(w.shape, BF16),
            pltpu.VMEM(wo.shape, BF16),
            pltpu.VMEM((2, patches, width), BF16),
            pltpu.VMEM((4, rows, width), BF16),
            pltpu.VMEM((2 * width, rows), F32),
            pltpu.VMEM((2 * heads, 1, rows), F32),
            pltpu.VMEM((rows, 2 * width), BF16),
            pltpu.VMEM((rows, 4 * width), BF16),
            pltpu.VMEM((2, patches, width), BF16),
            pltpu.VMEM((rows, d), F32),
            pltpu.VMEM((4, shard, d), BF16),
            pltpu.VMEM((width, rows), F32),
            pltpu.VMEM((width, rows), BF16),
            pltpu.VMEM((2 * width, rows), F32),
            pltpu.VMEM((rows, width), F32),
            pltpu.VMEM((rows, width), F32),
        ],
        18,
        ((10, 4), (11, 5)) if stacks else (),
    )


def attention_weights_kernel(h, dd, o, da, out, w_sum, wo_sum):
    step = pl.program_id(0)
    w_part = dot_tn(h[0], dd[0])
    wo_part = dot_tn(o[0], da[0])

    @pl.when(step == 0)
    def _():
        w_sum[...] = w_part
        wo_sum[...] = wo_part

    @pl.when(step > 0)
    def _():
        w_sum[...] += w_part
        wo_sum[...] += wo_part

    @pl.when(step == pl.num_programs(0) - 1)
    def _():
        chunks = out.shape[0]
        d, columns = w_sum.shape
        rows, wide = d // chunks, wo_sum.shape[1]
        at = rows
        for z in range(chunks):
            out[z, 0:rows, :] = w_sum[z * rows : (z + 1) * rows, :].astype(BF16)
        narrow = d // 4 // chunks
        for part in range(wo_sum.shape[0] // (d // 4)):
            for z in range(chunks):
                top = part * (d // 4) + z * narrow
                out[z, at : at + narrow, 0:wide] = wo_sum[top : top + narrow, :].astype(BF16)
                if columns > wide:
                    out[z, at : at + narrow, wide:] = jnp.zeros((narrow, columns - wide), BF16)
            at += narrow


def attention_weights(h, dd, o, da, chunks, name):
    slots, rows, d = h.shape
    columns, wide = dd.shape[2], o.shape[2]
    out = (chunks, (d + wide) // chunks, columns)
    slot = lambda a: pl.BlockSpec((1, *a.shape[1:]), lambda i: (i, 0, 0))
    return pl.pallas_call(
        attention_weights_kernel,
        grid=(slots - 1,),
        out_shape=shape_of(out, BF16),
        in_specs=[slot(a) for a in (h, dd, o, da)],
        out_specs=whole(*out),
        scratch_shapes=[pltpu.VMEM((d, columns), F32), pltpu.VMEM((wide, d), F32)],
        compiler_params=params(),
        cost_estimate=cost(
            2 * slots * rows * d * (columns + wide), 2 * slots * rows * (2 * d + columns + wide)
        ),
        name=name,
    )(h, dd, o, da)


def ff_forward_kernel(ni, tick, info, x, a, b, c, gain, bias, u0, u1, u2, u3, d0, d1, d2, d3, *refs):
    refs = refs[-(7 + 11) :]
    mid, gp, z, h2, g, image_out, text_out = refs[:7]
    x_v, abc, norm, up, down, mid_v, h2_v, g_v, gp_v, z_v, sems = refs[7:]
    copies = Copies(sems)
    n, d = x_v.shape
    hidden = up.shape[2]
    slot = info[AT_STACK + tick[0]]
    at_row = pl.multiple_of(slot * n, 8)
    loads = [
        copies.start(s, t)
        for s, t in (
            (x, x_v),
            (a, abc.at[0]),
            (b.at[0], abc.at[1]),
            (c, abc.at[2]),
            (gain, norm.at[0]),
            (bias, norm.at[1]),
        )
    ]
    weights = [
        (copies.start(u, up.at[i]), copies.start(w, down.at[i]))
        for i, (u, w) in enumerate(zip((u0, u1, u2, u3), (d0, d1, d2, d3)))
    ]
    copies.wait(*loads)
    values = x_v[...].astype(F32) + (
        abc[0].astype(F32) + abc[1].astype(F32) + abc[2].astype(F32)
    )
    mid_v[...] = values
    unit, _ = normalized(values)
    h2_v[...] = (unit * norm[0, 1:2, :] + norm[1, 1:2, :]).astype(BF16)
    copies.start(mid_v, mid)
    copies.start(h2_v, h2.at[pl.ds(at_row, n)])

    def ascend(i):
        copies.wait(weights[i][0])
        return dot(h2_v[...], up[i])

    def bend(i, u):
        square = u * u
        bent = jnp.tanh(u * (GELU_C + (GELU_C * GELU_A) * square))
        half = 0.5 * (1.0 + bent)
        g_v[i] = (u * half).astype(BF16)
        slope = half + (0.5 * u) * (1.0 - bent * bent) * (GELU_C + (3.0 * GELU_C * GELU_A) * square)
        gp_v[i] = slope.astype(BF16)
        columns = slice(i * hidden, (i + 1) * hidden)
        copies.start(g_v.at[i], g.at[pl.ds(at_row, n), columns])
        copies.start(gp_v.at[i], gp.at[:, columns])

    total = mid_v[...]
    u = ascend(0)
    for i in range(4):
        bend(i, u)
        copies.wait(weights[i][1])
        total = total + dot(g_v[i], down[i])
        u = ascend(i + 1) if i < 3 else None
    z_v[...] = total.astype(BF16)
    copies.start(z_v, z)
    copies.finish()

    @pl.when(info[AT_VALID + tick[0]] > 0)
    def _():
        image_copy = pltpu.make_async_copy(z_v.at[0:ni], image_out.at[slot], sems.at[0])
        text_copy = pltpu.make_async_copy(z_v.at[ni:], text_out.at[slot], sems.at[1])
        image_copy.start()
        text_copy.start()
        image_copy.wait()
        text_copy.wait()


def ff_forward(tick, info, ni, micro, x, parts, gain, bias, up, down, stacks):
    n, d = x.shape
    hidden = up[0].shape[1]
    return run(
        functools.partial(ff_forward_kernel, ni),
        "ff_forward",
        cost(16 * n * d * hidden, 16 * d * hidden + 16 * n * hidden + 16 * n * d, 4 * n * hidden),
        (tick, info),
        (x, *parts, gain, bias, *up, *down, *stacks),
        (
            shape_of((n, d), F32),
            shape_of((n, 4 * hidden), BF16),
            shape_of((n, d), BF16),
            shape_of(((micro + 1) * n, d), BF16),
            shape_of(((micro + 1) * n, 4 * hidden), BF16),
            shape_of((micro, ni, d), BF16),
            shape_of((micro, n - ni, d), BF16),
        ),
        [
            pltpu.VMEM((n, d), BF16),
            pltpu.VMEM((3, n, d), BF16),
            pltpu.VMEM((2, 2, d), F32),
            pltpu.VMEM((4, d, hidden), BF16),
            pltpu.VMEM((4, hidden, d), BF16),
            pltpu.VMEM((n, d), F32),
            pltpu.VMEM((n, d), BF16),
            pltpu.VMEM((4, n, hidden), BF16),
            pltpu.VMEM((4, n, hidden), BF16),
            pltpu.VMEM((n, d), BF16),
        ],
        26,
        ((14, 3), (15, 4), (16, 5), (17, 6)) if stacks else (),
    )


def ff_backward_kernel(
    source, tick, info, coti, cott, back, gp, mid, gain, u0, u1, u2, u3, d0, d1, d2, d3, *refs
):
    refs = refs[-(5 + 13) :]
    dmid, da, sums, dm, du = refs[:5]
    cot_v, back_v, gp_v, mid_v, norm, up, down, rows, dm_v, du_v, da_v, sums_v, sems = refs[5:]
    copies = Copies(sems)
    n, d = mid_v.shape
    ni = coti.shape[1]
    nt = n - ni
    hidden = up.shape[2]
    valid = info[AT_VALID + tick[0]].astype(F32)
    slot = info[AT_STACK + tick[0]]
    at_row = pl.multiple_of(slot * n, 8)
    loads = [
        copies.start(coti.at[source], cot_v.at[0:ni]),
        copies.start(cott.at[source], cot_v.at[ni:]),
        copies.start(back, back_v),
    ]
    weights = []
    for i, (u, w) in enumerate(zip((u0, u1, u2, u3), (d0, d1, d2, d3))):
        columns = slice(i * hidden, (i + 1) * hidden)
        weights.append(
            (
                copies.start(w, down.at[i]),
                copies.start(gp.at[:, columns], gp_v.at[i]),
                copies.start(u, up.at[i]),
            )
        )
    rest = [copies.start(mid, mid_v), copies.start(gain, norm)]
    copies.wait(*loads)
    first = info[AT_SECTION] == 0
    place = lax.broadcasted_iota(jnp.int32, (nt, 1), 0) + info[AT_MP] * nt
    kept = (place < info[AT_LENGTH + tick[0]]).astype(F32)
    rows[0:ni, :] = jnp.where(first, back_v[0:ni, :].astype(F32), cot_v[0:ni, :].astype(F32))
    rows[ni:, :] = jnp.where(first, back_v[ni:, :].astype(F32), cot_v[ni:, :].astype(F32) * kept)
    dm_v[...] = rows[...].astype(BF16)
    copies.start(dm_v, dm.at[pl.ds(at_row, n)])

    def descend(i):
        copies.wait(weights[i][0])
        return dot_nt(dm_v[...], down[i])

    total = None
    act_grad = descend(0)
    for i in range(4):
        later = descend(i + 1) if i < 3 else None
        copies.wait(weights[i][1], weights[i][2])
        du_v[i] = (gp_v[i].astype(F32) * act_grad).astype(BF16)
        copies.start(du_v.at[i], du.at[pl.ds(at_row, n), i * hidden : (i + 1) * hidden])
        part = dot_nt(du_v[i], up[i])
        total = part if total is None else total + part
        act_grad = later
    copies.wait(*rest)
    pulled, gain_sum, bias_sum = norm_pull(total, mid_v[...], norm[1:2, :])
    total = rows[...] + pulled
    rows[...] = total
    da_v[...] = total.astype(BF16)
    sums_v[0:1, :] = gain_sum * valid
    sums_v[1:2, :] = bias_sum * valid
    copies.start(da_v, da)
    copies.start(rows, dmid)
    copies.start(sums_v, sums)
    copies.finish()


def ff_backward(tick, info, source, micro, coti, cott, back, gp, mid, gain, up, down, stacks):
    n, d = mid.shape
    hidden = up[0].shape[1]
    return run(
        functools.partial(ff_backward_kernel, source),
        "ff_backward",
        cost(16 * n * d * hidden, 16 * d * hidden + 16 * n * hidden + 16 * n * d),
        (tick, info),
        (coti, cott, back, gp, mid, gain, *up, *down, *stacks),
        (
            shape_of((n, d), F32),
            shape_of((n, d), BF16),
            shape_of((2, d), F32),
            shape_of(((micro + 1) * n, d), BF16),
            shape_of(((micro + 1) * n, 4 * hidden), BF16),
        ),
        [
            pltpu.VMEM((n, d), BF16),
            pltpu.VMEM((n, d), BF16),
            pltpu.VMEM((4, n, hidden), BF16),
            pltpu.VMEM((n, d), F32),
            pltpu.VMEM((2, d), F32),
            pltpu.VMEM((4, d, hidden), BF16),
            pltpu.VMEM((4, hidden, d), BF16),
            pltpu.VMEM((n, d), F32),
            pltpu.VMEM((n, d), BF16),
            pltpu.VMEM((4, n, hidden), BF16),
            pltpu.VMEM((n, d), BF16),
            pltpu.VMEM((2, d), F32),
        ],
        26,
        ((14, 3), (15, 4)) if stacks else (),
    )


def ff_weights_kernel(h2, dm, du, g, one, two):
    piece = pl.program_id(0)
    up_part = dot_tn(h2[...], du[...]).astype(BF16)
    down_part = dot_tn(g[...], dm[...]).astype(BF16)
    for index, out in enumerate((one, two)):

        @pl.when(piece == index)
        def _():
            chunks, rows = out.shape[0], out.shape[1] // 2
            for z in range(chunks):
                span = slice(z * rows, (z + 1) * rows)
                out[z, 0:rows, :] = up_part[span, :]
                out[z, rows:, :] = down_part[span, :]


def ff_weights(pieces, samples, h2, dm, du, g, chunks):
    d = h2.shape[1]
    hidden = du.shape[1] // 4
    n = h2.shape[0] // (samples + 1) * samples
    one, two = pieces
    part = (chunks, 2 * d // chunks, hidden)
    column = lambda i: one + (two - one) * i
    return pl.pallas_call(
        ff_weights_kernel,
        grid=(2,),
        out_shape=(shape_of(part, BF16),) * 2,
        in_specs=[
            whole(n, d),
            whole(n, d),
            pl.BlockSpec((n, hidden), lambda i: (0, column(i))),
            pl.BlockSpec((n, hidden), lambda i: (0, column(i))),
        ],
        out_specs=(whole(*part), whole(*part)),
        compiler_params=params(),
        cost_estimate=cost(8 * n * d * hidden, 4 * n * d + 8 * n * hidden + 8 * d * hidden),
        name="ff_weights",
    )(h2, dm, du, g)


def close_kernel(ni, tick, info, x, a, b, c, dmid, gain, *refs):
    refs = refs[-(4 + 8) :]
    back, sums, image_grad, text_grad = refs[:4]
    x_v, abc, dmid_v, norm, total_v, back_v, sums_v, sems = refs[4:]
    copies = Copies(sems)
    n = x_v.shape[0]
    slot = info[AT_STACK + tick[0]]
    valid = info[AT_VALID + tick[0]]
    ready = copies.start(gain, norm)
    spans = (slice(0, ni), slice(ni, n))
    loads = [
        [
            copies.start(source.at[span], target.at[span])
            for source, target in (
                (a, abc.at[0]),
                (b.at[0], abc.at[1]),
                (c, abc.at[2]),
                (x, x_v),
                (dmid, dmid_v),
            )
        ]
        for span in spans
    ]
    copies.wait(ready)
    gain_total = bias_total = None
    for index, (span, load) in enumerate(zip(spans, loads)):
        copies.wait(*load)
        grad = abc[0, span, :].astype(F32) + abc[1, span, :].astype(F32) + abc[2, span, :].astype(F32)
        pulled, gain_sum, bias_sum = norm_pull(grad, x_v[span, :].astype(F32), norm[0:1, :])
        total = dmid_v[span, :] + pulled
        total_v[span, :] = total
        back_v[span, :] = total.astype(BF16)
        copies.start(back_v.at[span], back.at[span])
        out = (image_grad, text_grad)[index]
        copy = pltpu.make_async_copy(total_v.at[span], out.at[slot], sems.at[16 + index])

        @pl.when(valid > 0)
        def _():
            copy.start()

        gain_total = gain_sum if index == 0 else gain_total + gain_sum
        bias_total = bias_sum if index == 0 else bias_total + bias_sum
    sums_v[0:1, :] = gain_total * valid.astype(F32)
    sums_v[1:2, :] = bias_total * valid.astype(F32)
    copies.start(sums_v, sums)
    copies.finish()
    for index, (span, out) in enumerate(zip(spans, (image_grad, text_grad))):

        @pl.when(valid > 0)
        def _():
            pltpu.make_async_copy(total_v.at[span], out.at[slot], sems.at[16 + index]).wait()


def close(tick, info, ni, micro, x, parts, dmid, gain, stacks):
    n, d = x.shape
    return run(
        functools.partial(close_kernel, ni),
        "input_grad",
        cost(20 * n * d, 18 * n * d),
        (tick, info),
        (x, *parts, dmid, gain, *stacks),
        (
            shape_of((n, d), BF16),
            shape_of((2, d), F32),
            shape_of((micro, ni, d), F32),
            shape_of((micro, n - ni, d), F32),
        ),
        [
            pltpu.VMEM((n, d), BF16),
            pltpu.VMEM((3, n, d), BF16),
            pltpu.VMEM((n, d), F32),
            pltpu.VMEM((2, d), F32),
            pltpu.VMEM((n, d), F32),
            pltpu.VMEM((n, d), BF16),
            pltpu.VMEM((2, d), F32),
        ],
        18,
        ((6, 2), (7, 3)) if stacks else (),
    )


def over_y(array):
    return lax.ppermute(array, "mp", [(m, m ^ 2) for m in range(4)])


def over_core(array):
    return lax.ppermute(array, "mp", [(m, m ^ 1) for m in range(4)])


def gathered(own, across=None):
    across = over_y(own) if across is None else across
    return (own, across, over_core(own), over_core(across))


def for_y(r1, r23):
    other = over_core(r23)
    return other, (r1.astype(F32) + other[1].astype(F32)).astype(BF16)


def shifted(array, by):
    length = lax.axis_size("section")
    return lax.ppermute(array, "section", [(i, i + by) for i in range(length) if 0 <= i + by < length])


def over_everyone(sums):
    groups = lax.axis_size("dp")
    if groups & (groups - 1):
        return lax.psum_scatter(sums, ("dp", "mp"), scatter_dimension=2, tiled=True)
    for flip in (1, 2):
        sums = sums + lax.ppermute(sums, "mp", [(m, m ^ flip) for m in range(4)])
    flip = 1
    while flip < groups:
        sums = sums + lax.ppermute(sums, "dp", [(z, z ^ flip) for z in range(groups)])
        flip *= 2
    own = sums.shape[2] // (4 * groups)
    mine = lax.axis_index("dp") * 4 + lax.axis_index("mp")
    return lax.dynamic_slice_in_dim(sums, mine * own, own, axis=2)


def hold(values, *earlier):
    return lax.optimization_barrier((tuple(values), *earlier))[0]


def shards(
    image, text, lengths, image_cot, text_cot, qkv_image, out_image, qkv_text, out_text,
    query_cross, kv_cross, out_cross, up_proj, down_proj, norm_gain, norm_bias,
):
    section = lax.axis_index("section")
    me = lax.axis_index("mp")
    groups = lax.axis_size("dp")
    micro = image.shape[0]
    ticks = micro + SKEW
    ni, d = image.shape[1:]
    nt = text.shape[1]
    gain, bias = norm_gain[0], norm_bias[0]
    width = out_image.shape[1]
    w_image = jnp.concatenate(
        (kv_cross[0].reshape(d, 2 * width), qkv_image[0].reshape(d, 3 * width)), axis=1
    )
    w_text = jnp.concatenate((qkv_text[0].reshape(d, 3 * width), query_cross[0]), axis=1)
    wo_image = out_image[0]
    wo_text = jnp.concatenate((out_text[0], out_cross[0]), axis=0)

    flips = jnp.array(FLIPS, jnp.int32)
    turn = jnp.arange(ticks) - section * SKEW
    valid = (turn >= 0) & (turn < micro)
    gap = jnp.zeros((16 - ticks,), jnp.int32)
    info = jnp.concatenate(
        (
            ((me ^ flips) - section) % 4,
            me ^ flips,
            jnp.stack((section, me)).astype(jnp.int32),
            jnp.zeros((AT_LENGTH - 10,), jnp.int32),
            lengths[jnp.clip(turn, 0, micro - 1)],
            gap,
            valid.astype(jnp.int32),
            gap,
            jnp.where(valid, turn, micro).astype(jnp.int32),
        )
    ).astype(jnp.int32)
    place = jnp.arange(4 * ni)
    turned = (place % PATCH_COLS - section * SHIFT) % PATCH_COLS
    edge = PATCH_ROWS - section * SHIFT
    row_region = (place // PATCH_COLS >= PATCH_ROWS - WIN).astype(jnp.int32) + (
        place // PATCH_COLS >= edge
    ).astype(jnp.int32)
    col_region = (turned >= PATCH_COLS - WIN).astype(jnp.int32) + (turned >= edge).astype(jnp.int32)
    region = row_region * 3 + col_region
    gidc = region[:, None]
    gidr = region[None, :]

    tick_at = [jnp.full((1,), t, jnp.int32) for t in range(ticks)]
    nothing = jnp.zeros((ni + nt, d), BF16)
    up = down = None
    image_stacks = text_stacks = ff_stacks = ()
    state = {}
    relayed = {}
    ahead = {}

    def attend(t):
        nonlocal image_stacks, text_stacks, up, down
        got = relayed.get(t - SKEW, nothing)
        if t >= SKEW and t % SKEW == 0:
            got = hold((got,), ahead["out"])[0]
        elif t % SKEW > 0:
            got = hold((got,), ahead["h"])[0]
        x, h = entry(tick_at[t], info, min(t, micro - 1), image, text, got, gain, bias)
        ahead["h"] = h
        pieces = gathered(h)
        if up is None:
            up_own, down_own, _ = lax.optimization_barrier((up_proj[0], down_proj[0], pieces[1]))
            up, down = gathered(up_own), gathered(down_own)
        second = t % SKEW > 0
        if second:
            pieces = hold(pieces, ahead["own"])
        r0, r1, r23, qkvi, oti, tti, hx, oi = image_forward(
            tick_at[t], info, ni, micro, pieces, w_image, wo_image, gidc, gidr, image_stacks
        )
        image_stacks = (hx, oi)
        if second and t > SKEW:
            r0, r1, r23 = hold((r0, r1, r23), ahead["across"])
        r0, r1, r23, qkvt, ott, ttt, hy, o = text_forward(
            tick_at[t], info, nt, micro, pieces, w_text, wo_text, qkvi, (r0, r1, r23), text_stacks
        )
        text_stacks = (hy, o)
        state[t] = [x, qkvi, oti, tti, qkvt, ott, ttt]
        other, across = for_y(r1, r23)
        ahead.update(own=r0, across=across)
        return (r0, other, over_y(across))

    def feed(t, parts):
        nonlocal ff_stacks
        x = hold((state[t][0],), ahead["out"])[0] if t % SKEW > 0 else state[t][0]
        mid, gp, z, *ff_stacks = ff_forward(
            tick_at[t], info, ni, micro, x, parts, gain, bias, up, down, ff_stacks
        )
        state[t] += [mid, gp]
        ahead["out"] = z
        if t + SKEW < ticks:
            relayed[t] = shifted(z, 1)

    for t in range(0, ticks, SKEW):
        sums = [attend(t + i) for i in range(SKEW)]
        for i in range(SKEW):
            feed(t + i, sums[i])
    h2, g, image_result, text_result = ff_stacks

    sums_one = sums_two = jnp.zeros((2, d), F32)
    relayed = {}
    ff_stacks = text_back = image_back = close_stacks = ()
    ahead = {}

    def descend(k):
        nonlocal ff_stacks, sums_two
        t = ticks - 1 - k
        mid, gp = state[t][7:9]
        back = relayed.get(k - SKEW, nothing)
        if k >= SKEW and k % SKEW == 0:
            back = hold((back,), ahead["out"])[0]
        elif k % SKEW > 0:
            back = hold((back,), ahead["da"])[0]
        dmid, da, sums, *ff_stacks = ff_backward(
            tick_at[t], info, max(t - SKEW, 0), micro, image_cot, text_cot, back, gp, mid, gain,
            up, down, ff_stacks,
        )
        sums_two = sums_two + sums
        ahead["da"] = da
        return dmid, da, over_y(da)

    def text_part(k, pieces):
        nonlocal text_back
        t = ticks - 1 - k
        qkvi, _, _, qkvt, ott, ttt = state[t][1:7]
        r0, r1, r23, dkv, *text_back = text_backward(
            tick_at[t], info, nt, micro, pieces, w_text, wo_text, qkvi, qkvt, ott, ttt, text_back
        )
        return (r0, r1, r23), dkv

    def image_part(k, pieces, parts, dkv):
        nonlocal image_back
        t = ticks - 1 - k
        qkvi, oti, tti = state[t][1:4]
        r0, r1, r23, *image_back = image_backward(
            tick_at[t], info, ni, micro, pieces, w_image, wo_image, gidc, gidr, qkvi, oti, tti, dkv,
            parts, image_back,
        )
        other, across = for_y(r1, r23)
        return r0, other, across

    def finish(k, parts, dmid):
        nonlocal close_stacks, sums_one
        t = ticks - 1 - k
        if k % SKEW > 0:
            dmid = hold((dmid,), ahead["out"])[0]
        back, sums, *close_stacks = close(
            tick_at[t], info, ni, micro, state[t][0], parts, dmid, gain, close_stacks
        )
        sums_one = sums_one + sums
        ahead["out"] = back
        if k + SKEW < ticks:
            relayed[k] = shifted(back, -1)

    final = ticks - SKEW
    fed = {}
    for k in range(final):
        second = k % SKEW > 0
        if not second:
            fed = {k + i: descend(k + i) for i in range(SKEW)}
        dmid, da, across = fed[k]
        across = hold((across,), ahead["text"] if second else ahead["da"])[0]
        pieces = gathered(da, across)
        if second:
            pieces = hold(pieces, ahead["own"])
        parts, dkv = text_part(k, pieces)
        ahead["text"] = parts[0]
        if second:
            parts = hold(parts, ahead["crossed"])
        r0, other, across = image_part(k, pieces, parts, dkv)
        crossed = over_y(across)
        ahead.update(own=r0, crossed=crossed)
        fed[k] = (k, (r0, other, crossed), dmid)
        if k % SKEW == SKEW - 1:
            for i in range(k - SKEW + 1, k + 1):
                finish(*fed[i])

    one, two = final, final + 1
    (dmid_one, da_one, a_one), (dmid_two, da_two, a_two) = descend(one), descend(two)
    pieces_one = gathered(da_one, *hold((a_one,), da_two))
    parts_one, dkv_one = text_part(one, pieces_one)
    pieces_two = hold(gathered(da_two, *hold((a_two,), parts_one[0])), parts_one[0])
    parts_two, dkv_two = text_part(two, pieces_two)
    dm, du = hold(ff_stacks, parts_two[0])
    far, y_part = ff_weights((3, 1), micro, h2, dm, du, g, groups)
    text_all = hold((*text_stacks, *text_back), far)
    text_w = attention_weights(
        text_all[0], text_all[3], text_all[1], text_all[2], groups, "text_weights"
    )
    parts_one = hold(parts_one, text_w)
    r0_one, other_one, across_one = image_part(one, pieces_one, parts_one, dkv_one)
    ff_across = (y_part.astype(F32) + over_core(far).astype(F32)).astype(BF16)
    parts_two = hold(parts_two, r0_one, ff_across)
    r0_two, other_two, across_two = image_part(two, pieces_two, parts_two, dkv_two)
    quarter = ff_across.shape[1] // 4
    crossed = [over_y(ff_across[:, i * quarter : (i + 1) * quarter]) for i in range(4)]
    image_stacks = hold((*image_stacks, *image_back), crossed[0], across_one)
    image_w = attention_weights(
        image_stacks[0], image_stacks[3], image_stacks[1], image_stacks[2], groups, "image_weights"
    )
    du = hold((du,), image_w, crossed[1], across_two)[0]
    near, core_part = ff_weights((0, 2), micro, h2, dm, du, g, groups)
    core_part = hold((core_part,), crossed[2])[0]
    dmid_one = hold((dmid_one,), near)[0]
    dmid_two = hold((dmid_two,), crossed[3])[0]
    finish(one, (r0_one, other_one, over_y(across_one)), dmid_one)
    finish(two, (r0_two, other_two, over_y(across_two)), dmid_two)
    ff_sum = (
        near.astype(F32) + over_core(core_part).astype(F32) + jnp.concatenate(crossed, axis=1).astype(F32)
    ).astype(BF16)

    def over_dp(array):
        return lax.psum_scatter(array, "dp", scatter_dimension=0, tiled=True)[0].astype(F32)

    ff_grad = over_dp(ff_sum)
    text_grad = over_dp(text_w)
    image_grad = over_dp(image_w)
    rows, wo_rows = d // groups, width // groups
    gain_grad, bias_grad = over_everyone(jnp.stack((sums_one, sums_two), axis=1))
    return (
        image_result[None],
        text_result[None],
        close_stacks[0][None],
        close_stacks[1][None],
        image_grad[:rows, 2 * width :].reshape(1, rows, 3, width),
        image_grad[rows:, :d][None],
        text_grad[:rows, : 3 * width].reshape(1, rows, 3, width),
        text_grad[rows : rows + wo_rows, :d][None],
        text_grad[:rows, 3 * width :][None],
        image_grad[:rows, : 2 * width].reshape(1, rows, 2, width),
        text_grad[rows + wo_rows :, :d][None],
        ff_grad[:rows][None],
        ff_grad[rows:][None],
        gain_grad[None],
        bias_grad[None],
    )


def solution(mesh):
    return jax.shard_map(
        shards,
        mesh=mesh,
        in_specs=(
            P("dp", "mp", None),
            P("dp", "mp", None),
            P("dp"),
            P("dp", "mp", None),
            P("dp", "mp", None),
            P("section", None, None, "mp"),
            P("section", "mp", None),
            P("section", None, None, "mp"),
            P("section", "mp", None),
            P("section", None, "mp"),
            P("section", None, None, "mp"),
            P("section", "mp", None),
            P("section", None, "mp"),
            P("section", "mp", None),
            P("section", None, None),
            P("section", None, None),
        ),
        out_specs=(
            P("section", "dp", "mp", None),
            P("section", "dp", "mp", None),
            P("section", "dp", "mp", None),
            P("section", "dp", "mp", None),
            P("section", "dp", None, "mp"),
            P("section", ("mp", "dp"), None),
            P("section", "dp", None, "mp"),
            P("section", ("mp", "dp"), None),
            P("section", "dp", "mp"),
            P("section", "dp", None, "mp"),
            P("section", ("mp", "dp"), None),
            P("section", "dp", "mp"),
            P("section", ("mp", "dp"), None),
            P("section", None, ("dp", "mp")),
            P("section", None, ("dp", "mp")),
        ),
        check_vma=False,
    )
```

```python
import functools

import jax
import jax.numpy as jnp
from jax import lax
from jax.experimental import pallas as pl
from jax.experimental.pallas import tpu as pltpu
from jax.sharding import PartitionSpec as P

HEAD_DIM = 64
WIN = 12
PATCH_ROWS = 24
PATCH_COLS = 24
SHIFT = WIN // 2

EPSILON = 1e-05
MASKED_SCORE = -1000000000.0
SCALE = HEAD_DIM**-0.5
GELU_C = 0.7978845608028654
GELU_A = 0.044715

VMEM_MIB = 56
SKEW = 2
SELF_BLOCK = 256
CROSS_BLOCK = 512
CROSS_BACK = 512

F32 = jnp.float32
BF16 = jnp.bfloat16

FLIPS = (0, 2, 1, 3)
AT_SLOT, AT_BLOCK, AT_SECTION, AT_MP, AT_LENGTH, AT_VALID, AT_STACK = 0, 4, 8, 9, 16, 32, 48


def dot(left, right):
    return lax.dot_general(left, right, (((1,), (0,)), ((), ())), preferred_element_type=F32)


def dot_nt(left, right):
    return lax.dot_general(left, right, (((1,), (1,)), ((), ())), preferred_element_type=F32)


def dot_tn(left, right):
    return lax.dot_general(left, right, (((0,), (0,)), ((), ())), preferred_element_type=F32)


def head_mask(head, width, scale):
    lane = lax.broadcasted_iota(jnp.int32, (1, width), 1)
    inside = (lane >= head * HEAD_DIM) & (lane < (head + 1) * HEAD_DIM)
    return jnp.where(inside, F32(scale), F32(0.0)).astype(BF16)


def normalized(values):
    average = jnp.mean(values, axis=-1, keepdims=True)
    centered = values - average
    variance = jnp.mean(centered * centered, axis=-1, keepdims=True)
    inverse = lax.rsqrt(variance + EPSILON)
    return centered * inverse, inverse


def norm_pull(grad, values, gain):
    unit, inverse = normalized(values)
    scaled = grad * gain
    first = jnp.mean(scaled, axis=-1, keepdims=True)
    second = jnp.mean(scaled * unit, axis=-1, keepdims=True)
    pulled = inverse * (scaled - first - unit * second)
    gain_sum = jnp.sum(grad * unit, axis=0, keepdims=True)
    bias_sum = jnp.sum(grad, axis=0, keepdims=True)
    return pulled, gain_sum, bias_sum


SMEM_SPEC = pl.BlockSpec(memory_space=pltpu.SMEM)
ANY_SPEC = pl.BlockSpec(memory_space=pl.ANY)


def whole(*extent):
    zeros = (0,) * len(extent)
    return pl.BlockSpec(extent, lambda *at: zeros, pipeline_mode=pl.Buffered(1))


def params():
    return pltpu.CompilerParams(vmem_limit_bytes=VMEM_MIB << 20)


def cost(flops, moved, exps=0):
    return pl.CostEstimate(flops=int(flops), bytes_accessed=int(moved), transcendentals=int(exps))


def shape_of(extent, dtype):
    return jax.ShapeDtypeStruct(extent, dtype)


class Copies:
    def __init__(self, sems):
        self.sems = sems
        self.used = 0
        self.going = []

    def start(self, source, target):
        copy = pltpu.make_async_copy(source, target, self.sems.at[self.used])
        self.used += 1
        copy.start()
        self.going.append(copy)
        return copy

    def wait(self, *copies):
        for copy in copies:
            copy.wait()
            self.going = [other for other in self.going if other is not copy]

    def finish(self):
        for copy in self.going:
            copy.wait()
        self.going = []


def run(kernel, name, estimate, scalars, arrays, outs, scratch, sems, aliases=()):
    lead = len(scalars)
    return pl.pallas_call(
        kernel,
        out_shape=tuple(outs),
        in_specs=[SMEM_SPEC] * lead + [ANY_SPEC] * len(arrays),
        out_specs=(ANY_SPEC,) * len(outs),
        scratch_shapes=list(scratch) + [pltpu.SemaphoreType.DMA((sems,))],
        input_output_aliases={lead + a: b for a, b in aliases},
        compiler_params=params(),
        cost_estimate=estimate,
        name=name,
    )(*scalars, *arrays)


def entry_kernel(source, tick, info, image, text, got, gain, bias, x, h, own, got_v, norm, xv, hv, sems):
    copies = Copies(sems)
    n, ni = got_v.shape[0], image.shape[1]
    both = [copies.start(gain, norm.at[0]), copies.start(bias, norm.at[1])]
    spans = (slice(0, ni), slice(ni, n))
    loads = [
        (copies.start(rows.at[source], own.at[span]), copies.start(got.at[span], got_v.at[span]))
        for rows, span in zip((image, text), spans)
    ]
    copies.wait(*both)
    first = info[AT_SECTION] == 0
    for span, load in zip(spans, loads):
        copies.wait(*load)
        values = jnp.where(first, own[span, :].astype(F32), got_v[span, :].astype(F32))
        xv[span, :] = values.astype(BF16)
        unit, _ = normalized(values)
        hv[span, :] = (unit * norm[0, 0:1, :] + norm[1, 0:1, :]).astype(BF16)
        copies.start(hv.at[span], h.at[span])
        copies.start(xv.at[span], x.at[span])
    copies.finish()


def entry(tick, info, source, image, text, got, gain, bias):
    n, d = got.shape
    return run(
        functools.partial(entry_kernel, source),
        "entry_norm",
        cost(10 * n * d, 8 * n * d),
        (tick, info),
        (image, text, got, gain, bias),
        (shape_of((n, d), BF16),) * 2,
        [pltpu.VMEM((n, d), BF16), pltpu.VMEM((n, d), BF16), pltpu.VMEM((2, 2, d), F32)]
        + [pltpu.VMEM((n, d), BF16)] * 2,
        10,
    )


def image_forward_kernel(
    tick, info, p0, p1, p2, p3, w, wo, gidc, gidr, *refs
):
    refs = refs[-(8 + 11) :]
    r0, r1, r23, qkv, ot, tt, hx, o = refs[:8]
    hx_v, w_v, wo_v, gidc_v, gidr_v, qkv_v, ot_v, tt_v, o_v, part, sems = refs[8:]
    copies = Copies(sems)
    rows, d = hx_v.shape
    shard = rows // 4
    band = ot_v.shape[2]
    width = wo_v.shape[0]
    heads = width // HEAD_DIM
    slot = info[AT_STACK + tick[0]]
    offs = [pl.multiple_of(info[AT_SLOT + i] * shard, 16) for i in range(4)]
    loads = [
        copies.start(piece.at[0:shard], hx_v.at[pl.ds(off, shard)])
        for off, piece in zip(offs, (p0, p1, p2, p3))
    ] + [copies.start(w, w_v)]
    more = [copies.start(a, b) for a, b in ((gidc, gidc_v), (gidr, gidr_v), (wo, wo_v))]
    copies.wait(*loads)
    projected = dot(hx_v[...], w_v[...])
    for j in range(5):
        qkv_v[j] = projected[:, j * width : (j + 1) * width].astype(BF16)
    copies.start(hx_v, hx.at[slot])
    copies.start(qkv_v, qkv)
    copies.wait(*more)
    spans = [slice(b * band, (b + 1) * band) for b in range(2)]
    allowed = [gidc_v[span, :] == gidr_v[0:1, span] for span in spans]
    bias = [jnp.where(mask, F32(0.0), F32(MASKED_SCORE)) for mask in allowed]
    v_tall = [qkv_v[4, span, :].astype(F32).T.astype(BF16) for span in spans]
    items = [(b, head) for b in range(2) for head in range(heads)]

    def score(b, head):
        query = qkv_v[2, spans[b], :] * head_mask(head, width, SCALE)
        return dot_nt(qkv_v[3, spans[b], :], query) + bias[b]

    scores = score(*items[0])
    for index, (b, head) in enumerate(items):
        later = score(*items[index + 1]) if index + 1 < len(items) else None
        largest = jnp.max(scores, axis=0, keepdims=True)
        weights = jnp.exp(scores - largest)
        total = jnp.sum(weights, axis=0, keepdims=True)
        tt_v[b * heads + head] = largest + jnp.log(total)
        own = slice(head * HEAD_DIM, (head + 1) * HEAD_DIM)
        mixed = dot(v_tall[b][own, :], weights.astype(BF16))
        ot_v[b, own, :] = mixed * (1.0 / total)
        scores = later
    for b, span in enumerate(spans):
        o_v[span, :] = ot_v[b].T.astype(BF16)
    copies.start(ot_v, ot)
    copies.start(tt_v, tt)
    copies.start(o_v, o.at[slot])
    part[...] = dot(o_v[...], wo_v[...]).astype(BF16)
    for off, piece in zip(offs, (r0, r1, r23.at[0], r23.at[1])):
        copies.start(part.at[pl.ds(off, shard)], piece.at[0:shard])
    copies.finish()


def image_forward(tick, info, shard, micro, pieces, w, wo, gidc, gidr, stacks):
    n, d = pieces[0].shape
    rows = 4 * shard
    width = wo.shape[0]
    band = rows // 2
    heads = width // HEAD_DIM
    return run(
        image_forward_kernel,
        "image_forward",
        cost(
            2 * rows * d * width * 6 + 8 * heads * band * band * 256,
            2 * rows * d * 3 + 12 * rows * width + 12 * d * width,
            2 * heads * band * band,
        ),
        (tick, info),
        (*pieces, w, wo, gidc, gidr, *stacks),
        (
            shape_of((n, d), BF16),
            shape_of((n, d), BF16),
            shape_of((2, n, d), BF16),
            shape_of((5, rows, width), BF16),
            shape_of((2, width, band), F32),
            shape_of((2 * heads, 1, band), F32),
            shape_of((micro + 1, rows, d), BF16),
            shape_of((micro + 1, rows, width), BF16),
        ),
        [
            pltpu.VMEM((rows, d), BF16),
            pltpu.VMEM(w.shape, BF16),
            pltpu.VMEM(wo.shape, BF16),
            pltpu.VMEM(gidc.shape, jnp.int32),
            pltpu.VMEM(gidr.shape, jnp.int32),
            pltpu.VMEM((5, rows, width), BF16),
            pltpu.VMEM((2, width, band), F32),
            pltpu.VMEM((2 * heads, 1, band), F32),
            pltpu.VMEM((rows, width), BF16),
            pltpu.VMEM((rows, d), BF16),
        ],
        18,
        ((8, 6), (9, 7)) if stacks else (),
    )


def image_backward_kernel(tick, info, p0, p1, p2, p3, w, wo, gidc, gidr, qkv, ot, tt, dkv, *refs):
    refs = refs[-(5 + 18) :]
    r0, r1, r23, da, dd = refs[:5]
    (
        da_v, w_v, wo_v, gidc_v, gidr_v, qkv_v, ot_v, tt_v, dkv_v, do_v, d_v, part,
        dq_tall, k_tall, do_tall, dk_sum, dv_sum, sems,
    ) = refs[5:]
    copies = Copies(sems)
    rows, d = da_v.shape
    shard = rows // 4
    band = ot_v.shape[2]
    width = wo_v.shape[0]
    heads = width // HEAD_DIM
    slot = info[AT_STACK + tick[0]]
    offs = [pl.multiple_of(info[AT_SLOT + i] * shard, 16) for i in range(4)]
    loads = [
        copies.start(piece.at[0:shard], da_v.at[pl.ds(off, shard)])
        for off, piece in zip(offs, (p0, p1, p2, p3))
    ] + [copies.start(wo, wo_v)]
    more = [
        copies.start(a, b)
        for a, b in ((qkv, qkv_v), (gidc, gidc_v), (gidr, gidr_v), (tt, tt_v), (ot, ot_v))
    ]
    rest = [copies.start(a, b) for a, b in ((dkv, dkv_v), (w, w_v))]
    copies.wait(*loads)
    copies.start(da_v, da.at[slot])
    do_v[...] = dot_nt(da_v[...], wo_v[...]).astype(BF16)
    copies.wait(*more)
    for b in range(2):
        span = slice(b * band, (b + 1) * band)
        bias = jnp.where(gidc_v[span, :] == gidr_v[0:1, span], F32(0.0), F32(MASKED_SCORE))
        k_tall[...] = qkv_v[3, span, :].astype(F32).T.astype(BF16)
        do_tall[...] = do_v[span, :].astype(F32).T
        dk_sum[...] = jnp.zeros_like(dk_sum)
        dv_sum[...] = jnp.zeros_like(dv_sum)
        for head in range(heads):
            at = head * HEAD_DIM
            own = slice(at, at + HEAD_DIM)
            query = qkv_v[2, span, :] * head_mask(head, width, SCALE)
            grad = do_v[span, :] * head_mask(head, width, 1.0)
            scores = dot_nt(qkv_v[3, span, :], query) + bias
            weights = jnp.exp(scores - tt_v[b * heads + head])
            pulled = dot_nt(qkv_v[4, span, :], grad)
            delta = jnp.sum(do_tall[own, :] * ot_v[b, own, :], axis=0, keepdims=True)
            score_grad = (weights * (pulled - delta)).astype(BF16)
            dv_sum[...] += dot(weights.astype(BF16), grad)
            dk_sum[...] += dot(score_grad, query)
            dq_tall[own, :] = dot(k_tall[own, :], score_grad) * SCALE
        d_v[span, 2 * width : 3 * width] = dq_tall[...].T.astype(BF16)
        d_v[span, 3 * width : 4 * width] = dk_sum[...].astype(BF16)
        d_v[span, 4 * width :] = dv_sum[...].astype(BF16)
    copies.wait(*rest)
    d_v[:, 0:width] = dkv_v[0]
    d_v[:, width : 2 * width] = dkv_v[1]
    copies.start(d_v, dd.at[slot])
    part[...] = dot_nt(d_v[...], w_v[...]).astype(BF16)
    for off, piece in zip(offs, (r0, r1, r23.at[0], r23.at[1])):
        copies.start(part.at[pl.ds(off, shard)], piece.at[0:shard])
    copies.finish()


def image_backward(tick, info, shard, micro, pieces, w, wo, gidc, gidr, qkv, ot, tt, dkv, parts, stacks):
    n, d = pieces[0].shape
    rows = 4 * shard
    width = wo.shape[0]
    band = rows // 2
    heads = width // HEAD_DIM
    return run(
        image_backward_kernel,
        "image_backward",
        cost(
            2 * rows * d * width * 6 + 20 * heads * band * band * 256,
            2 * rows * d * 3 + 20 * rows * width + 12 * d * width,
            2 * heads * band * band,
        ),
        (tick, info),
        (*pieces, w, wo, gidc, gidr, qkv, ot, tt, dkv, *parts, *stacks),
        (
            shape_of((n, d), BF16),
            shape_of((n, d), BF16),
            shape_of((2, n, d), BF16),
            shape_of((micro + 1, rows, d), BF16),
            shape_of((micro + 1, rows, 5 * width), BF16),
        ),
        [
            pltpu.VMEM((rows, d), BF16),
            pltpu.VMEM(w.shape, BF16),
            pltpu.VMEM(wo.shape, BF16),
            pltpu.VMEM(gidc.shape, jnp.int32),
            pltpu.VMEM(gidr.shape, jnp.int32),
            pltpu.VMEM((5, rows, width), BF16),
            pltpu.VMEM((2, width, band), F32),
            pltpu.VMEM((2 * heads, 1, band), F32),
            pltpu.VMEM((2, rows, width), BF16),
            pltpu.VMEM((rows, width), BF16),
            pltpu.VMEM((rows, 5 * width), BF16),
            pltpu.VMEM((rows, d), BF16),
            pltpu.VMEM((width, band), F32),
            pltpu.VMEM((width, band), BF16),
            pltpu.VMEM((width, band), F32),
            pltpu.VMEM((band, width), F32),
            pltpu.VMEM((band, width), F32),
        ],
        18,
        ((12, 0), (13, 1), (14, 2)) + (((15, 3), (16, 4)) if stacks else ()),
    )


def query_blocks(rows, size):
    return [(at, min(size, rows - at)) for at in range(0, rows, size)]


def causal(scores, start, last_key):
    key_at = lax.broadcasted_iota(jnp.int32, scores.shape, 0)
    query_at = lax.broadcasted_iota(jnp.int32, (1, scores.shape[1]), 1) + start
    return jnp.where(key_at <= jnp.minimum(query_at, last_key), scores, F32(MASKED_SCORE))


def text_forward_kernel(skip, tick, info, p0, p1, p2, p3, w, wo, kv, *refs):
    refs = refs[-(8 + 11) :]
    r0, r1, r23, qkv, ot, tt, hy, o = refs[:8]
    hy_v, w_v, wo_v, kv_v, qkv_v, ot_v, tt_v, o_v, part, piece_v, sems = refs[8:]
    copies = Copies(sems)
    rows, d = hy_v.shape
    shard = rows // 4
    patches = kv_v.shape[1]
    width = kv_v.shape[2]
    heads = width // HEAD_DIM
    slot = info[AT_STACK + tick[0]]
    last_key = info[AT_LENGTH + tick[0]] - 1
    offs = [pl.multiple_of(info[AT_BLOCK + i] * shard, 8) for i in range(4)]
    loads = [
        copies.start(piece.at[skip:], piece_v.at[i]) for i, piece in enumerate((p0, p1, p2, p3))
    ] + [copies.start(w, w_v)]
    more = [copies.start(kv.at[0:2], kv_v)]
    rest = [copies.start(wo, wo_v)]
    copies.wait(*loads)
    for i, off in enumerate(offs):
        part[pl.ds(off, shard), :] = piece_v[i].astype(F32)
    hy_v[...] = part[...].astype(BF16)
    projected = dot(hy_v[...], w_v[...])
    for j in range(4):
        qkv_v[j] = projected[:, j * width : (j + 1) * width].astype(BF16)
    copies.start(hy_v, hy.at[slot])
    copies.start(qkv_v, qkv)
    copies.wait(*more)
    v_tall = [values.astype(F32).T.astype(BF16) for values in (qkv_v[2], kv_v[1])]
    items = [
        (kind, head, start, size)
        for kind in range(2)
        for start, size in query_blocks(rows, CROSS_BLOCK if kind else SELF_BLOCK)
        for head in range(heads)
    ]

    def score(kind, head, start, size):
        query = qkv_v[3 if kind else 0, start : start + size, :] * head_mask(head, width, SCALE)
        keys = kv_v[0] if kind else qkv_v[1, 0 : start + size, :]
        scores = dot_nt(keys, query)
        return scores if kind else causal(scores, start, last_key)

    scores = score(*items[0])
    for index, (kind, head, start, size) in enumerate(items):
        later = score(*items[index + 1]) if index + 1 < len(items) else None
        at = head * HEAD_DIM
        largest = jnp.max(scores, axis=0, keepdims=True)
        weights = jnp.exp(scores - largest)
        total = jnp.sum(weights, axis=0, keepdims=True)
        tt_v[kind * heads + head, :, start : start + size] = largest + jnp.log(total)
        mixed = dot(v_tall[kind][at : at + HEAD_DIM, 0 : weights.shape[0]], weights.astype(BF16))
        out_at = kind * width + at
        ot_v[out_at : out_at + HEAD_DIM, start : start + size] = mixed * (1.0 / total)
        scores = later
    copies.start(ot_v, ot)
    copies.start(tt_v, tt)
    o_v[...] = ot_v[...].T.astype(BF16)
    copies.start(o_v, o.at[slot])
    copies.wait(*rest)
    part[...] = dot(o_v[...], wo_v[...])
    for i, (off, piece) in enumerate(zip(offs, (r0, r1, r23.at[0], r23.at[1]))):
        piece_v[i] = part[pl.ds(off, shard), :].astype(BF16)
        copies.start(piece_v.at[i], piece.at[skip:])
    copies.finish()


def text_forward(tick, info, shard, micro, pieces, w, wo, kv, parts, stacks):
    n, d = pieces[0].shape
    rows = 4 * shard
    patches, width = kv.shape[1:]
    heads = width // HEAD_DIM
    return run(
        functools.partial(text_forward_kernel, n - shard),
        "text_forward",
        cost(
            2 * rows * d * width * 6 + 4 * heads * rows * (rows * 0.6 + patches) * 256,
            2 * rows * d * 3 + 12 * rows * width + 12 * d * width,
            heads * rows * (rows * 0.6 + patches),
        ),
        (tick, info),
        (*pieces, w, wo, kv, *parts, *stacks),
        (
            shape_of((n, d), BF16),
            shape_of((n, d), BF16),
            shape_of((2, n, d), BF16),
            shape_of((4, rows, width), BF16),
            shape_of((2 * width, rows), F32),
            shape_of((2 * heads, 1, rows), F32),
            shape_of((micro + 1, rows, d), BF16),
            shape_of((micro + 1, rows, 2 * width), BF16),
        ),
        [
            pltpu.VMEM((rows, d), BF16),
            pltpu.VMEM(w.shape, BF16),
            pltpu.VMEM(wo.shape, BF16),
            pltpu.VMEM((2, patches, width), BF16),
            pltpu.VMEM((4, rows, width), BF16),
            pltpu.VMEM((2 * width, rows), F32),
            pltpu.VMEM((2 * heads, 1, rows), F32),
            pltpu.VMEM((rows, 2 * width), BF16),
            pltpu.VMEM((rows, d), F32),
            pltpu.VMEM((4, shard, d), BF16),
        ],
        16,
        ((7, 0), (8, 1), (9, 2)) + (((10, 6), (11, 7)) if stacks else ()),
    )


def text_backward_kernel(skip, tick, info, p0, p1, p2, p3, w, wo, kv, qkv, ot, tt, *refs):
    refs = refs[-(6 + 18) :]
    r0, r1, r23, dkv, da, dd = refs[:6]
    (
        da_v, w_v, wo_v, kv_v, qkv_v, ot_v, tt_v, do_v, d_v, dkv_v, part, piece_v,
        dq_tall, k_tall, do_tall, dk_sum, dv_sum, sems,
    ) = refs[6:]
    copies = Copies(sems)
    rows, d = da_v.shape
    shard = rows // 4
    patches, width = kv_v.shape[1:]
    heads = width // HEAD_DIM
    slot = info[AT_STACK + tick[0]]
    last_key = info[AT_LENGTH + tick[0]] - 1
    offs = [pl.multiple_of(info[AT_BLOCK + i] * shard, 8) for i in range(4)]
    loads = [
        copies.start(piece.at[skip:], piece_v.at[i]) for i, piece in enumerate((p0, p1, p2, p3))
    ] + [copies.start(wo, wo_v)]
    more = [copies.start(a, b) for a, b in ((qkv, qkv_v), (tt, tt_v), (ot, ot_v), (kv.at[0:2], kv_v))]
    rest = [copies.start(w, w_v)]
    copies.wait(*loads)
    for i, off in enumerate(offs):
        part[pl.ds(off, shard), :] = piece_v[i].astype(F32)
    da_v[...] = part[...].astype(BF16)
    copies.start(da_v, da.at[slot])
    grads = dot_nt(da_v[...], wo_v[...])
    do_v[...] = grads.astype(BF16)
    do_tall[...] = grads.astype(BF16).astype(F32).T
    copies.wait(*more)
    for kind in range(2):
        span = patches if kind else rows
        whole_keys = kv_v[0] if kind else qkv_v[1]
        k_tall[:, 0:span] = whole_keys.astype(F32).T.astype(BF16)
        dk_sum[...] = jnp.zeros_like(dk_sum)
        dv_sum[...] = jnp.zeros_like(dv_sum)
        for start, size in query_blocks(rows, CROSS_BACK if kind else SELF_BLOCK):
            seen = start + size if kind == 0 else patches
            block = slice(start, start + size)
            keys = kv_v[0] if kind else qkv_v[1, 0:seen, :]
            values = kv_v[1] if kind else qkv_v[2, 0:seen, :]
            for head in range(heads):
                at = head * HEAD_DIM
                own = slice(at, at + HEAD_DIM)
                out_own = slice(kind * width + at, kind * width + at + HEAD_DIM)
                query = qkv_v[3 if kind else 0, block, :] * head_mask(head, width, SCALE)
                grad = do_v[block, kind * width : (kind + 1) * width] * head_mask(head, width, 1.0)
                scores = dot_nt(keys, query)
                if kind == 0:
                    scores = causal(scores, start, last_key)
                weights = jnp.exp(scores - tt_v[kind * heads + head, :, block])
                pulled = dot_nt(values, grad)
                delta = jnp.sum(do_tall[out_own, block] * ot_v[out_own, block], axis=0, keepdims=True)
                score_grad = (weights * (pulled - delta)).astype(BF16)
                dv_sum[0:seen, :] += dot(weights.astype(BF16), grad)
                dk_sum[0:seen, :] += dot(score_grad, query)
                dq_tall[own, block] = dot(k_tall[own, 0:seen], score_grad) * SCALE
        if kind == 0:
            d_v[:, 0:width] = dq_tall[...].T.astype(BF16)
            d_v[:, width : 2 * width] = dk_sum[...].astype(BF16)
            d_v[:, 2 * width : 3 * width] = dv_sum[...].astype(BF16)
        else:
            d_v[:, 3 * width :] = dq_tall[...].T.astype(BF16)
            dkv_v[0] = dk_sum[0:patches, :].astype(BF16)
            dkv_v[1] = dv_sum[0:patches, :].astype(BF16)
    copies.start(dkv_v, dkv)
    copies.start(d_v, dd.at[slot])
    copies.wait(*rest)
    part[...] = dot_nt(d_v[...], w_v[...])
    for i, (off, piece) in enumerate(zip(offs, (r0, r1, r23.at[0], r23.at[1]))):
        piece_v[i] = part[pl.ds(off, shard), :].astype(BF16)
        copies.start(piece_v.at[i], piece.at[skip:])
    copies.finish()


def text_backward(tick, info, shard, micro, pieces, w, wo, kv, qkv, ot, tt, stacks):
    n, d = pieces[0].shape
    rows = 4 * shard
    patches, width = kv.shape[1:]
    heads = width // HEAD_DIM
    return run(
        functools.partial(text_backward_kernel, n - shard),
        "text_backward",
        cost(
            2 * rows * d * width * 6 + 10 * heads * rows * (rows * 0.6 + patches) * 256,
            2 * rows * d * 3 + 20 * rows * width + 12 * d * width,
            heads * rows * (rows * 0.6 + patches),
        ),
        (tick, info),
        (*pieces, w, wo, kv, qkv, ot, tt, *stacks),
        (
            shape_of((n, d), BF16),
            shape_of((n, d), BF16),
            shape_of((2, n, d), BF16),
            shape_of((2, patches, width), BF16),
            shape_of((micro + 1, rows, d), BF16),
            shape_of((micro + 1, rows, 4 * width), BF16),
        ),
        [
            pltpu.VMEM((rows, d), BF16),
            pltpu.VMEM(w.shape, BF16),
            pltpu.VMEM(wo.shape, BF16),
            pltpu.VMEM((2, patches, width), BF16),
            pltpu.VMEM((4, rows, width), BF16),
            pltpu.VMEM((2 * width, rows), F32),
            pltpu.VMEM((2 * heads, 1, rows), F32),
            pltpu.VMEM((rows, 2 * width), BF16),
            pltpu.VMEM((rows, 4 * width), BF16),
            pltpu.VMEM((2, patches, width), BF16),
            pltpu.VMEM((rows, d), F32),
            pltpu.VMEM((4, shard, d), BF16),
            pltpu.VMEM((width, rows), F32),
            pltpu.VMEM((width, rows), BF16),
            pltpu.VMEM((2 * width, rows), F32),
            pltpu.VMEM((rows, width), F32),
            pltpu.VMEM((rows, width), F32),
        ],
        18,
        ((10, 4), (11, 5)) if stacks else (),
    )


def attention_weights_kernel(h, dd, o, da, out, w_sum, wo_sum):
    step = pl.program_id(0)
    w_part = dot_tn(h[0], dd[0])
    wo_part = dot_tn(o[0], da[0])

    @pl.when(step == 0)
    def _():
        w_sum[...] = w_part
        wo_sum[...] = wo_part

    @pl.when(step > 0)
    def _():
        w_sum[...] += w_part
        wo_sum[...] += wo_part

    @pl.when(step == pl.num_programs(0) - 1)
    def _():
        chunks = out.shape[0]
        d, columns = w_sum.shape
        rows, wide = d // chunks, wo_sum.shape[1]
        at = rows
        for z in range(chunks):
            out[z, 0:rows, :] = w_sum[z * rows : (z + 1) * rows, :].astype(BF16)
        narrow = d // 4 // chunks
        for part in range(wo_sum.shape[0] // (d // 4)):
            for z in range(chunks):
                top = part * (d // 4) + z * narrow
                out[z, at : at + narrow, 0:wide] = wo_sum[top : top + narrow, :].astype(BF16)
                if columns > wide:
                    out[z, at : at + narrow, wide:] = jnp.zeros((narrow, columns - wide), BF16)
            at += narrow


def attention_weights(h, dd, o, da, chunks, name):
    slots, rows, d = h.shape
    columns, wide = dd.shape[2], o.shape[2]
    out = (chunks, (d + wide) // chunks, columns)
    slot = lambda a: pl.BlockSpec((1, *a.shape[1:]), lambda i: (i, 0, 0))
    return pl.pallas_call(
        attention_weights_kernel,
        grid=(slots - 1,),
        out_shape=shape_of(out, BF16),
        in_specs=[slot(a) for a in (h, dd, o, da)],
        out_specs=whole(*out),
        scratch_shapes=[pltpu.VMEM((d, columns), F32), pltpu.VMEM((wide, d), F32)],
        compiler_params=params(),
        cost_estimate=cost(
            2 * slots * rows * d * (columns + wide), 2 * slots * rows * (2 * d + columns + wide)
        ),
        name=name,
    )(h, dd, o, da)


def ff_forward_kernel(ni, tick, info, x, a, b, c, gain, bias, u0, u1, u2, u3, d0, d1, d2, d3, *refs):
    refs = refs[-(7 + 11) :]
    mid, gp, z, h2, g, image_out, text_out = refs[:7]
    x_v, abc, norm, up, down, mid_v, h2_v, g_v, gp_v, z_v, sems = refs[7:]
    copies = Copies(sems)
    n, d = x_v.shape
    hidden = up.shape[2]
    slot = info[AT_STACK + tick[0]]
    at_row = pl.multiple_of(slot * n, 8)
    loads = [
        copies.start(s, t)
        for s, t in (
            (x, x_v),
            (a, abc.at[0]),
            (b.at[0], abc.at[1]),
            (c, abc.at[2]),
            (gain, norm.at[0]),
            (bias, norm.at[1]),
        )
    ]
    weights = [
        (copies.start(u, up.at[i]), copies.start(w, down.at[i]))
        for i, (u, w) in enumerate(zip((u0, u1, u2, u3), (d0, d1, d2, d3)))
    ]
    copies.wait(*loads)
    values = x_v[...].astype(F32) + (
        abc[0].astype(F32) + abc[1].astype(F32) + abc[2].astype(F32)
    )
    mid_v[...] = values
    unit, _ = normalized(values)
    h2_v[...] = (unit * norm[0, 1:2, :] + norm[1, 1:2, :]).astype(BF16)
    copies.start(mid_v, mid)
    copies.start(h2_v, h2.at[pl.ds(at_row, n)])

    def ascend(i):
        copies.wait(weights[i][0])
        return dot(h2_v[...], up[i])

    def bend(i, u):
        square = u * u
        bent = jnp.tanh(u * (GELU_C + (GELU_C * GELU_A) * square))
        half = 0.5 * (1.0 + bent)
        g_v[i] = (u * half).astype(BF16)
        slope = half + (0.5 * u) * (1.0 - bent * bent) * (GELU_C + (3.0 * GELU_C * GELU_A) * square)
        gp_v[i] = slope.astype(BF16)
        columns = slice(i * hidden, (i + 1) * hidden)
        copies.start(g_v.at[i], g.at[pl.ds(at_row, n), columns])
        copies.start(gp_v.at[i], gp.at[:, columns])

    total = mid_v[...]
    u = ascend(0)
    for i in range(4):
        bend(i, u)
        copies.wait(weights[i][1])
        total = total + dot(g_v[i], down[i])
        u = ascend(i + 1) if i < 3 else None
    z_v[...] = total.astype(BF16)
    copies.start(z_v, z)
    copies.finish()

    @pl.when(info[AT_VALID + tick[0]] > 0)
    def _():
        image_copy = pltpu.make_async_copy(z_v.at[0:ni], image_out.at[slot], sems.at[0])
        text_copy = pltpu.make_async_copy(z_v.at[ni:], text_out.at[slot], sems.at[1])
        image_copy.start()
        text_copy.start()
        image_copy.wait()
        text_copy.wait()


def ff_forward(tick, info, ni, micro, x, parts, gain, bias, up, down, stacks):
    n, d = x.shape
    hidden = up[0].shape[1]
    return run(
        functools.partial(ff_forward_kernel, ni),
        "ff_forward",
        cost(16 * n * d * hidden, 16 * d * hidden + 16 * n * hidden + 16 * n * d, 4 * n * hidden),
        (tick, info),
        (x, *parts, gain, bias, *up, *down, *stacks),
        (
            shape_of((n, d), F32),
            shape_of((n, 4 * hidden), BF16),
            shape_of((n, d), BF16),
            shape_of(((micro + 1) * n, d), BF16),
            shape_of(((micro + 1) * n, 4 * hidden), BF16),
            shape_of((micro, ni, d), BF16),
            shape_of((micro, n - ni, d), BF16),
        ),
        [
            pltpu.VMEM((n, d), BF16),
            pltpu.VMEM((3, n, d), BF16),
            pltpu.VMEM((2, 2, d), F32),
            pltpu.VMEM((4, d, hidden), BF16),
            pltpu.VMEM((4, hidden, d), BF16),
            pltpu.VMEM((n, d), F32),
            pltpu.VMEM((n, d), BF16),
            pltpu.VMEM((4, n, hidden), BF16),
            pltpu.VMEM((4, n, hidden), BF16),
            pltpu.VMEM((n, d), BF16),
        ],
        26,
        ((14, 3), (15, 4), (16, 5), (17, 6)) if stacks else (),
    )


def ff_backward_kernel(
    source, tick, info, coti, cott, back, gp, mid, gain, u0, u1, u2, u3, d0, d1, d2, d3, *refs
):
    refs = refs[-(5 + 13) :]
    dmid, da, sums, dm, du = refs[:5]
    cot_v, back_v, gp_v, mid_v, norm, up, down, rows, dm_v, du_v, da_v, sums_v, sems = refs[5:]
    copies = Copies(sems)
    n, d = mid_v.shape
    ni = coti.shape[1]
    nt = n - ni
    hidden = up.shape[2]
    valid = info[AT_VALID + tick[0]].astype(F32)
    slot = info[AT_STACK + tick[0]]
    at_row = pl.multiple_of(slot * n, 8)
    loads = [
        copies.start(coti.at[source], cot_v.at[0:ni]),
        copies.start(cott.at[source], cot_v.at[ni:]),
        copies.start(back, back_v),
    ]
    weights = []
    for i, (u, w) in enumerate(zip((u0, u1, u2, u3), (d0, d1, d2, d3))):
        columns = slice(i * hidden, (i + 1) * hidden)
        weights.append(
            (
                copies.start(w, down.at[i]),
                copies.start(gp.at[:, columns], gp_v.at[i]),
                copies.start(u, up.at[i]),
            )
        )
    rest = [copies.start(mid, mid_v), copies.start(gain, norm)]
    copies.wait(*loads)
    first = info[AT_SECTION] == 0
    place = lax.broadcasted_iota(jnp.int32, (nt, 1), 0) + info[AT_MP] * nt
    kept = (place < info[AT_LENGTH + tick[0]]).astype(F32)
    rows[0:ni, :] = jnp.where(first, back_v[0:ni, :].astype(F32), cot_v[0:ni, :].astype(F32))
    rows[ni:, :] = jnp.where(first, back_v[ni:, :].astype(F32), cot_v[ni:, :].astype(F32) * kept)
    dm_v[...] = rows[...].astype(BF16)
    copies.start(dm_v, dm.at[pl.ds(at_row, n)])

    def descend(i):
        copies.wait(weights[i][0])
        return dot_nt(dm_v[...], down[i])

    total = None
    act_grad = descend(0)
    for i in range(4):
        later = descend(i + 1) if i < 3 else None
        copies.wait(weights[i][1], weights[i][2])
        du_v[i] = (gp_v[i].astype(F32) * act_grad).astype(BF16)
        copies.start(du_v.at[i], du.at[pl.ds(at_row, n), i * hidden : (i + 1) * hidden])
        part = dot_nt(du_v[i], up[i])
        total = part if total is None else total + part
        act_grad = later
    copies.wait(*rest)
    pulled, gain_sum, bias_sum = norm_pull(total, mid_v[...], norm[1:2, :])
    total = rows[...] + pulled
    rows[...] = total
    da_v[...] = total.astype(BF16)
    sums_v[0:1, :] = gain_sum * valid
    sums_v[1:2, :] = bias_sum * valid
    copies.start(da_v, da)
    copies.start(rows, dmid)
    copies.start(sums_v, sums)
    copies.finish()


def ff_backward(tick, info, source, micro, coti, cott, back, gp, mid, gain, up, down, stacks):
    n, d = mid.shape
    hidden = up[0].shape[1]
    return run(
        functools.partial(ff_backward_kernel, source),
        "ff_backward",
        cost(16 * n * d * hidden, 16 * d * hidden + 16 * n * hidden + 16 * n * d),
        (tick, info),
        (coti, cott, back, gp, mid, gain, *up, *down, *stacks),
        (
            shape_of((n, d), F32),
            shape_of((n, d), BF16),
            shape_of((2, d), F32),
            shape_of(((micro + 1) * n, d), BF16),
            shape_of(((micro + 1) * n, 4 * hidden), BF16),
        ),
        [
            pltpu.VMEM((n, d), BF16),
            pltpu.VMEM((n, d), BF16),
            pltpu.VMEM((4, n, hidden), BF16),
            pltpu.VMEM((n, d), F32),
            pltpu.VMEM((2, d), F32),
            pltpu.VMEM((4, d, hidden), BF16),
            pltpu.VMEM((4, hidden, d), BF16),
            pltpu.VMEM((n, d), F32),
            pltpu.VMEM((n, d), BF16),
            pltpu.VMEM((4, n, hidden), BF16),
            pltpu.VMEM((n, d), BF16),
            pltpu.VMEM((2, d), F32),
        ],
        26,
        ((14, 3), (15, 4)) if stacks else (),
    )


def ff_weights_kernel(h2, dm, du, g, one, two):
    piece = pl.program_id(0)
    up_part = dot_tn(h2[...], du[...]).astype(BF16)
    down_part = dot_tn(g[...], dm[...]).astype(BF16)
    for index, out in enumerate((one, two)):

        @pl.when(piece == index)
        def _():
            chunks, rows = out.shape[0], out.shape[1] // 2
            for z in range(chunks):
                span = slice(z * rows, (z + 1) * rows)
                out[z, 0:rows, :] = up_part[span, :]
                out[z, rows:, :] = down_part[span, :]


def ff_weights(pieces, samples, h2, dm, du, g, chunks):
    d = h2.shape[1]
    hidden = du.shape[1] // 4
    n = h2.shape[0] // (samples + 1) * samples
    one, two = pieces
    part = (chunks, 2 * d // chunks, hidden)
    column = lambda i: one + (two - one) * i
    return pl.pallas_call(
        ff_weights_kernel,
        grid=(2,),
        out_shape=(shape_of(part, BF16),) * 2,
        in_specs=[
            whole(n, d),
            whole(n, d),
            pl.BlockSpec((n, hidden), lambda i: (0, column(i))),
            pl.BlockSpec((n, hidden), lambda i: (0, column(i))),
        ],
        out_specs=(whole(*part), whole(*part)),
        compiler_params=params(),
        cost_estimate=cost(8 * n * d * hidden, 4 * n * d + 8 * n * hidden + 8 * d * hidden),
        name="ff_weights",
    )(h2, dm, du, g)


def close_kernel(ni, tick, info, x, a, b, c, dmid, gain, *refs):
    refs = refs[-(4 + 8) :]
    back, sums, image_grad, text_grad = refs[:4]
    x_v, abc, dmid_v, norm, total_v, back_v, sums_v, sems = refs[4:]
    copies = Copies(sems)
    n = x_v.shape[0]
    slot = info[AT_STACK + tick[0]]
    valid = info[AT_VALID + tick[0]]
    ready = copies.start(gain, norm)
    spans = (slice(0, ni), slice(ni, n))
    loads = [
        [
            copies.start(source.at[span], target.at[span])
            for source, target in (
                (a, abc.at[0]),
                (b.at[0], abc.at[1]),
                (c, abc.at[2]),
                (x, x_v),
                (dmid, dmid_v),
            )
        ]
        for span in spans
    ]
    copies.wait(ready)
    gain_total = bias_total = None
    for index, (span, load) in enumerate(zip(spans, loads)):
        copies.wait(*load)
        grad = abc[0, span, :].astype(F32) + abc[1, span, :].astype(F32) + abc[2, span, :].astype(F32)
        pulled, gain_sum, bias_sum = norm_pull(grad, x_v[span, :].astype(F32), norm[0:1, :])
        total = dmid_v[span, :] + pulled
        total_v[span, :] = total
        back_v[span, :] = total.astype(BF16)
        copies.start(back_v.at[span], back.at[span])
        out = (image_grad, text_grad)[index]
        copy = pltpu.make_async_copy(total_v.at[span], out.at[slot], sems.at[16 + index])

        @pl.when(valid > 0)
        def _():
            copy.start()

        gain_total = gain_sum if index == 0 else gain_total + gain_sum
        bias_total = bias_sum if index == 0 else bias_total + bias_sum
    sums_v[0:1, :] = gain_total * valid.astype(F32)
    sums_v[1:2, :] = bias_total * valid.astype(F32)
    copies.start(sums_v, sums)
    copies.finish()
    for index, (span, out) in enumerate(zip(spans, (image_grad, text_grad))):

        @pl.when(valid > 0)
        def _():
            pltpu.make_async_copy(total_v.at[span], out.at[slot], sems.at[16 + index]).wait()


def close(tick, info, ni, micro, x, parts, dmid, gain, stacks):
    n, d = x.shape
    return run(
        functools.partial(close_kernel, ni),
        "input_grad",
        cost(20 * n * d, 18 * n * d),
        (tick, info),
        (x, *parts, dmid, gain, *stacks),
        (
            shape_of((n, d), BF16),
            shape_of((2, d), F32),
            shape_of((micro, ni, d), F32),
            shape_of((micro, n - ni, d), F32),
        ),
        [
            pltpu.VMEM((n, d), BF16),
            pltpu.VMEM((3, n, d), BF16),
            pltpu.VMEM((n, d), F32),
            pltpu.VMEM((2, d), F32),
            pltpu.VMEM((n, d), F32),
            pltpu.VMEM((n, d), BF16),
            pltpu.VMEM((2, d), F32),
        ],
        18,
        ((6, 2), (7, 3)) if stacks else (),
    )


def over_y(array):
    return lax.ppermute(array, "mp", [(m, m ^ 2) for m in range(4)])


def over_core(array):
    return lax.ppermute(array, "mp", [(m, m ^ 1) for m in range(4)])


def gathered(own, across=None):
    across = over_y(own) if across is None else across
    return (own, across, over_core(own), over_core(across))


def for_y(r1, r23):
    other = over_core(r23)
    return other, (r1.astype(F32) + other[1].astype(F32)).astype(BF16)


def shifted(array, by):
    length = lax.axis_size("section")
    return lax.ppermute(array, "section", [(i, i + by) for i in range(length) if 0 <= i + by < length])


def over_everyone(sums):
    groups = lax.axis_size("dp")
    if groups & (groups - 1):
        return lax.psum_scatter(sums, ("dp", "mp"), scatter_dimension=2, tiled=True)
    for flip in (1, 2):
        sums = sums + lax.ppermute(sums, "mp", [(m, m ^ flip) for m in range(4)])
    flip = 1
    while flip < groups:
        sums = sums + lax.ppermute(sums, "dp", [(z, z ^ flip) for z in range(groups)])
        flip *= 2
    own = sums.shape[2] // (4 * groups)
    mine = lax.axis_index("dp") * 4 + lax.axis_index("mp")
    return lax.dynamic_slice_in_dim(sums, mine * own, own, axis=2)


def hold(values, *earlier):
    return lax.optimization_barrier((tuple(values), *earlier))[0]


def shards(
    image, text, lengths, image_cot, text_cot, qkv_image, out_image, qkv_text, out_text,
    query_cross, kv_cross, out_cross, up_proj, down_proj, norm_gain, norm_bias,
):
    section = lax.axis_index("section")
    me = lax.axis_index("mp")
    groups = lax.axis_size("dp")
    micro = image.shape[0]
    ticks = micro + SKEW
    ni, d = image.shape[1:]
    nt = text.shape[1]
    gain, bias = norm_gain[0], norm_bias[0]
    width = out_image.shape[1]
    w_image = jnp.concatenate(
        (kv_cross[0].reshape(d, 2 * width), qkv_image[0].reshape(d, 3 * width)), axis=1
    )
    w_text = jnp.concatenate((qkv_text[0].reshape(d, 3 * width), query_cross[0]), axis=1)
    wo_image = out_image[0]
    wo_text = jnp.concatenate((out_text[0], out_cross[0]), axis=0)

    flips = jnp.array(FLIPS, jnp.int32)
    turn = jnp.arange(ticks) - section * SKEW
    valid = (turn >= 0) & (turn < micro)
    gap = jnp.zeros((16 - ticks,), jnp.int32)
    info = jnp.concatenate(
        (
            ((me ^ flips) - section) % 4,
            me ^ flips,
            jnp.stack((section, me)).astype(jnp.int32),
            jnp.zeros((AT_LENGTH - 10,), jnp.int32),
            lengths[jnp.clip(turn, 0, micro - 1)],
            gap,
            valid.astype(jnp.int32),
            gap,
            jnp.where(valid, turn, micro).astype(jnp.int32),
        )
    ).astype(jnp.int32)
    place = jnp.arange(4 * ni)
    turned = (place % PATCH_COLS - section * SHIFT) % PATCH_COLS
    edge = PATCH_ROWS - section * SHIFT
    row_region = (place // PATCH_COLS >= PATCH_ROWS - WIN).astype(jnp.int32) + (
        place // PATCH_COLS >= edge
    ).astype(jnp.int32)
    col_region = (turned >= PATCH_COLS - WIN).astype(jnp.int32) + (turned >= edge).astype(jnp.int32)
    region = row_region * 3 + col_region
    gidc = region[:, None]
    gidr = region[None, :]

    tick_at = [jnp.full((1,), t, jnp.int32) for t in range(ticks)]
    nothing = jnp.zeros((ni + nt, d), BF16)
    up = down = None
    image_stacks = text_stacks = ff_stacks = ()
    state = {}
    relayed = {}
    ahead = {}

    def attend(t):
        nonlocal image_stacks, text_stacks, up, down
        got = relayed.get(t - SKEW, nothing)
        if t >= SKEW and t % SKEW == 0:
            got = hold((got,), ahead["out"])[0]
        elif t % SKEW > 0:
            got = hold((got,), ahead["h"])[0]
        x, h = entry(tick_at[t], info, min(t, micro - 1), image, text, got, gain, bias)
        ahead["h"] = h
        pieces = gathered(h)
        if up is None:
            up_own, down_own, _ = lax.optimization_barrier((up_proj[0], down_proj[0], pieces[1]))
            up = gathered(up_own)
            part = down_own.shape[0] // groups
            own_part = lax.dynamic_slice_in_dim(down_own, lax.axis_index("dp") * part, part, axis=0)
            part = over_y(own_part)
        second = t % SKEW > 0
        if second:
            pieces = hold(pieces, ahead["own"])
        r0, r1, r23, qkvi, oti, tti, hx, oi = image_forward(
            tick_at[t], info, ni, micro, pieces, w_image, wo_image, gidc, gidr, image_stacks
        )
        image_stacks = (hx, oi)
        if second and t > SKEW:
            r0, r1, r23 = hold((r0, r1, r23), ahead["across"])
        r0, r1, r23, qkvt, ott, ttt, hy, o = text_forward(
            tick_at[t], info, nt, micro, pieces, w_text, wo_text, qkvi, (r0, r1, r23), text_stacks
        )
        text_stacks = (hy, o)
        state[t] = [x, qkvi, oti, tti, qkvt, ott, ttt]
        other, across = for_y(r1, r23)
        ahead.update(own=r0, across=across)
        if down is None:
            part = lax.all_gather(hold((part,), r0)[0], "dp", axis=0, tiled=True)
            down = gathered(down_own, part)
        return (r0, other, over_y(across))

    def feed(t, parts):
        nonlocal ff_stacks
        x = hold((state[t][0],), ahead["out"])[0] if t % SKEW > 0 else state[t][0]
        mid, gp, z, *ff_stacks = ff_forward(
            tick_at[t], info, ni, micro, x, parts, gain, bias, up, down, ff_stacks
        )
        state[t] += [mid, gp]
        ahead["out"] = z
        if t + SKEW < ticks:
            relayed[t] = shifted(z, 1)

    for t in range(0, ticks, SKEW):
        sums = [attend(t + i) for i in range(SKEW)]
        for i in range(SKEW):
            feed(t + i, sums[i])
    h2, g, image_result, text_result = ff_stacks

    sums_one = sums_two = jnp.zeros((2, d), F32)
    relayed = {}
    ff_stacks = text_back = image_back = close_stacks = ()
    ahead = {}

    def descend(k):
        nonlocal ff_stacks, sums_two
        t = ticks - 1 - k
        mid, gp = state[t][7:9]
        back = relayed.get(k - SKEW, nothing)
        if k >= SKEW and k % SKEW == 0:
            back = hold((back,), ahead["out"])[0]
        elif k % SKEW > 0:
            back = hold((back,), ahead["da"])[0]
        dmid, da, sums, *ff_stacks = ff_backward(
            tick_at[t], info, max(t - SKEW, 0), micro, image_cot, text_cot, back, gp, mid, gain,
            up, down, ff_stacks,
        )
        sums_two = sums_two + sums
        ahead["da"] = da
        return dmid, da, over_y(da)

    def text_part(k, pieces):
        nonlocal text_back
        t = ticks - 1 - k
        qkvi, _, _, qkvt, ott, ttt = state[t][1:7]
        r0, r1, r23, dkv, *text_back = text_backward(
            tick_at[t], info, nt, micro, pieces, w_text, wo_text, qkvi, qkvt, ott, ttt, text_back
        )
        return (r0, r1, r23), dkv

    def image_part(k, pieces, parts, dkv):
        nonlocal image_back
        t = ticks - 1 - k
        qkvi, oti, tti = state[t][1:4]
        r0, r1, r23, *image_back = image_backward(
            tick_at[t], info, ni, micro, pieces, w_image, wo_image, gidc, gidr, qkvi, oti, tti, dkv,
            parts, image_back,
        )
        other, across = for_y(r1, r23)
        return r0, other, across

    def finish(k, parts, dmid):
        nonlocal close_stacks, sums_one
        t = ticks - 1 - k
        if k % SKEW > 0:
            dmid = hold((dmid,), ahead["out"])[0]
        back, sums, *close_stacks = close(
            tick_at[t], info, ni, micro, state[t][0], parts, dmid, gain, close_stacks
        )
        sums_one = sums_one + sums
        ahead["out"] = back
        if k + SKEW < ticks:
            relayed[k] = shifted(back, -1)

    final = ticks - SKEW
    fed = {}
    for k in range(final):
        second = k % SKEW > 0
        if not second:
            fed = {k + i: descend(k + i) for i in range(SKEW)}
        dmid, da, across = fed[k]
        across = hold((across,), ahead["text"] if second else ahead["da"])[0]
        pieces = gathered(da, across)
        if second:
            pieces = hold(pieces, ahead["own"])
        parts, dkv = text_part(k, pieces)
        ahead["text"] = parts[0]
        if second:
            parts = hold(parts, ahead["crossed"])
        r0, other, across = image_part(k, pieces, parts, dkv)
        crossed = over_y(across)
        ahead.update(own=r0, crossed=crossed)
        fed[k] = (k, (r0, other, crossed), dmid)
        if k % SKEW == SKEW - 1:
            for i in range(k - SKEW + 1, k + 1):
                finish(*fed[i])

    one, two = final, final + 1
    (dmid_one, da_one, a_one), (dmid_two, da_two, a_two) = descend(one), descend(two)
    pieces_one = gathered(da_one, *hold((a_one,), da_two))
    parts_one, dkv_one = text_part(one, pieces_one)
    pieces_two = hold(gathered(da_two, *hold((a_two,), parts_one[0])), parts_one[0])
    parts_two, dkv_two = text_part(two, pieces_two)
    dm, du = hold(ff_stacks, parts_two[0])
    far, y_part = ff_weights((3, 1), micro, h2, dm, du, g, groups)
    text_all = hold((*text_stacks, *text_back), far)
    text_w = attention_weights(
        text_all[0], text_all[3], text_all[1], text_all[2], groups, "text_weights"
    )
    parts_one = hold(parts_one, text_w)
    r0_one, other_one, across_one = image_part(one, pieces_one, parts_one, dkv_one)
    ff_across = (y_part.astype(F32) + over_core(far).astype(F32)).astype(BF16)
    parts_two = hold(parts_two, r0_one, ff_across)
    r0_two, other_two, across_two = image_part(two, pieces_two, parts_two, dkv_two)
    quarter = ff_across.shape[1] // 4
    crossed = [over_y(ff_across[:, i * quarter : (i + 1) * quarter]) for i in range(4)]
    image_stacks = hold((*image_stacks, *image_back), crossed[0], across_one)
    image_w = attention_weights(
        image_stacks[0], image_stacks[3], image_stacks[1], image_stacks[2], groups, "image_weights"
    )
    du = hold((du,), image_w, crossed[1], across_two)[0]
    near, core_part = ff_weights((0, 2), micro, h2, dm, du, g, groups)
    core_part = hold((core_part,), crossed[2])[0]
    dmid_one = hold((dmid_one,), near)[0]
    dmid_two = hold((dmid_two,), crossed[3])[0]
    finish(one, (r0_one, other_one, over_y(across_one)), dmid_one)
    finish(two, (r0_two, other_two, over_y(across_two)), dmid_two)
    ff_sum = (
        near.astype(F32) + over_core(core_part).astype(F32) + jnp.concatenate(crossed, axis=1).astype(F32)
    ).astype(BF16)

    def over_dp(array):
        return lax.psum_scatter(array, "dp", scatter_dimension=0, tiled=True)[0].astype(F32)

    ff_grad = over_dp(ff_sum)
    text_grad = over_dp(text_w)
    image_grad = over_dp(image_w)
    rows, wo_rows = d // groups, width // groups
    gain_grad, bias_grad = over_everyone(jnp.stack((sums_one, sums_two), axis=1))
    return (
        image_result[None],
        text_result[None],
        close_stacks[0][None],
        close_stacks[1][None],
        image_grad[:rows, 2 * width :].reshape(1, rows, 3, width),
        image_grad[rows:, :d][None],
        text_grad[:rows, : 3 * width].reshape(1, rows, 3, width),
        text_grad[rows : rows + wo_rows, :d][None],
        text_grad[:rows, 3 * width :][None],
        image_grad[:rows, : 2 * width].reshape(1, rows, 2, width),
        text_grad[rows + wo_rows :, :d][None],
        ff_grad[:rows][None],
        ff_grad[rows:][None],
        gain_grad[None],
        bias_grad[None],
    )


def solution(mesh):
    return jax.shard_map(
        shards,
        mesh=mesh,
        in_specs=(
            P("dp", "mp", None),
            P("dp", "mp", None),
            P("dp"),
            P("dp", "mp", None),
            P("dp", "mp", None),
            P("section", None, None, "mp"),
            P("section", "mp", None),
            P("section", None, None, "mp"),
            P("section", "mp", None),
            P("section", None, "mp"),
            P("section", None, None, "mp"),
            P("section", "mp", None),
            P("section", None, "mp"),
            P("section", "mp", None),
            P("section", None, None),
            P("section", None, None),
        ),
        out_specs=(
            P("section", "dp", "mp", None),
            P("section", "dp", "mp", None),
            P("section", "dp", "mp", None),
            P("section", "dp", "mp", None),
            P("section", "dp", None, "mp"),
            P("section", ("mp", "dp"), None),
            P("section", "dp", None, "mp"),
            P("section", ("mp", "dp"), None),
            P("section", "dp", "mp"),
            P("section", "dp", None, "mp"),
            P("section", ("mp", "dp"), None),
            P("section", "dp", "mp"),
            P("section", ("mp", "dp"), None),
            P("section", None, ("dp", "mp")),
            P("section", None, ("dp", "mp")),
        ),
        check_vma=False,
    )
```

```python
import functools

import jax
import jax.numpy as jnp
from jax import lax
from jax.experimental import pallas as pl
from jax.experimental.pallas import tpu as pltpu
from jax.sharding import PartitionSpec as P

HEAD_DIM = 64
WIN = 12
PATCH_ROWS = 24
PATCH_COLS = 24
SHIFT = WIN // 2

EPSILON = 1e-05
MASKED_SCORE = -1000000000.0
SCALE = HEAD_DIM**-0.5
GELU_C = 0.7978845608028654
GELU_A = 0.044715

VMEM_MIB = 56
SKEW = 2
SELF_BLOCK = 256
SELF_AHEAD = 512
CROSS_BLOCK = 512
CROSS_BACK = 512

F32 = jnp.float32
BF16 = jnp.bfloat16

FLIPS = (0, 2, 1, 3)
AT_SLOT, AT_BLOCK, AT_SECTION, AT_MP, AT_LENGTH, AT_VALID, AT_STACK = 0, 4, 8, 9, 16, 32, 48


def dot(left, right):
    return lax.dot_general(left, right, (((1,), (0,)), ((), ())), preferred_element_type=F32)


def dot_nt(left, right):
    return lax.dot_general(left, right, (((1,), (1,)), ((), ())), preferred_element_type=F32)


def dot_tn(left, right):
    return lax.dot_general(left, right, (((0,), (0,)), ((), ())), preferred_element_type=F32)


def head_mask(head, width, scale):
    lane = lax.broadcasted_iota(jnp.int32, (1, width), 1)
    inside = (lane >= head * HEAD_DIM) & (lane < (head + 1) * HEAD_DIM)
    return jnp.where(inside, F32(scale), F32(0.0)).astype(BF16)


def normalized(values):
    average = jnp.mean(values, axis=-1, keepdims=True)
    centered = values - average
    variance = jnp.mean(centered * centered, axis=-1, keepdims=True)
    inverse = lax.rsqrt(variance + EPSILON)
    return centered * inverse, inverse


def norm_pull(grad, values, gain):
    unit, inverse = normalized(values)
    scaled = grad * gain
    first = jnp.mean(scaled, axis=-1, keepdims=True)
    second = jnp.mean(scaled * unit, axis=-1, keepdims=True)
    pulled = inverse * (scaled - first - unit * second)
    gain_sum = jnp.sum(grad * unit, axis=0, keepdims=True)
    bias_sum = jnp.sum(grad, axis=0, keepdims=True)
    return pulled, gain_sum, bias_sum


SMEM_SPEC = pl.BlockSpec(memory_space=pltpu.SMEM)
ANY_SPEC = pl.BlockSpec(memory_space=pl.ANY)


def whole(*extent):
    zeros = (0,) * len(extent)
    return pl.BlockSpec(extent, lambda *at: zeros, pipeline_mode=pl.Buffered(1))


def params():
    return pltpu.CompilerParams(vmem_limit_bytes=VMEM_MIB << 20)


def cost(flops, moved, exps=0):
    return pl.CostEstimate(flops=int(flops), bytes_accessed=int(moved), transcendentals=int(exps))


def shape_of(extent, dtype):
    return jax.ShapeDtypeStruct(extent, dtype)


class Copies:
    def __init__(self, sems):
        self.sems = sems
        self.used = 0
        self.going = []

    def start(self, source, target):
        copy = pltpu.make_async_copy(source, target, self.sems.at[self.used])
        self.used += 1
        copy.start()
        self.going.append(copy)
        return copy

    def wait(self, *copies):
        for copy in copies:
            copy.wait()
            self.going = [other for other in self.going if other is not copy]

    def finish(self):
        for copy in self.going:
            copy.wait()
        self.going = []


def run(kernel, name, estimate, scalars, arrays, outs, scratch, sems, aliases=()):
    lead = len(scalars)
    return pl.pallas_call(
        kernel,
        out_shape=tuple(outs),
        in_specs=[SMEM_SPEC] * lead + [ANY_SPEC] * len(arrays),
        out_specs=(ANY_SPEC,) * len(outs),
        scratch_shapes=list(scratch) + [pltpu.SemaphoreType.DMA((sems,))],
        input_output_aliases={lead + a: b for a, b in aliases},
        compiler_params=params(),
        cost_estimate=estimate,
        name=name,
    )(*scalars, *arrays)


def entry_kernel(source, tick, info, image, text, got, gain, bias, x, h, own, got_v, norm, xv, hv, sems):
    copies = Copies(sems)
    n, ni = got_v.shape[0], image.shape[1]
    both = [copies.start(gain, norm.at[0]), copies.start(bias, norm.at[1])]
    spans = (slice(0, ni), slice(ni, n))
    loads = [
        (copies.start(rows.at[source], own.at[span]), copies.start(got.at[span], got_v.at[span]))
        for rows, span in zip((image, text), spans)
    ]
    copies.wait(*both)
    first = info[AT_SECTION] == 0
    for span, load in zip(spans, loads):
        copies.wait(*load)
        values = jnp.where(first, own[span, :].astype(F32), got_v[span, :].astype(F32))
        xv[span, :] = values.astype(BF16)
        unit, _ = normalized(values)
        hv[span, :] = (unit * norm[0, 0:1, :] + norm[1, 0:1, :]).astype(BF16)
        copies.start(hv.at[span], h.at[span])
        copies.start(xv.at[span], x.at[span])
    copies.finish()


def entry(tick, info, source, image, text, got, gain, bias):
    n, d = got.shape
    return run(
        functools.partial(entry_kernel, source),
        "entry_norm",
        cost(10 * n * d, 8 * n * d),
        (tick, info),
        (image, text, got, gain, bias),
        (shape_of((n, d), BF16),) * 2,
        [pltpu.VMEM((n, d), BF16), pltpu.VMEM((n, d), BF16), pltpu.VMEM((2, 2, d), F32)]
        + [pltpu.VMEM((n, d), BF16)] * 2,
        10,
    )


def image_forward_kernel(
    tick, info, p0, p1, p2, p3, w, wo, gidc, gidr, *refs
):
    refs = refs[-(8 + 11) :]
    r0, r1, r23, qkv, ot, tt, hx, o = refs[:8]
    hx_v, w_v, wo_v, gidc_v, gidr_v, qkv_v, ot_v, tt_v, o_v, part, sems = refs[8:]
    copies = Copies(sems)
    rows, d = hx_v.shape
    shard = rows // 4
    band = ot_v.shape[2]
    width = wo_v.shape[0]
    heads = width // HEAD_DIM
    slot = info[AT_STACK + tick[0]]
    offs = [pl.multiple_of(info[AT_SLOT + i] * shard, 16) for i in range(4)]
    loads = [
        copies.start(piece.at[0:shard], hx_v.at[pl.ds(off, shard)])
        for off, piece in zip(offs, (p0, p1, p2, p3))
    ] + [copies.start(w, w_v)]
    more = [copies.start(a, b) for a, b in ((gidc, gidc_v), (gidr, gidr_v), (wo, wo_v))]
    copies.wait(*loads)
    projected = dot(hx_v[...], w_v[...])
    for j in range(5):
        qkv_v[j] = projected[:, j * width : (j + 1) * width].astype(BF16)
    copies.start(hx_v, hx.at[slot])
    copies.start(qkv_v, qkv)
    copies.wait(*more)
    spans = [slice(b * band, (b + 1) * band) for b in range(2)]
    allowed = [gidc_v[span, :] == gidr_v[0:1, span] for span in spans]
    bias = [jnp.where(mask, F32(0.0), F32(MASKED_SCORE)) for mask in allowed]
    v_tall = [qkv_v[4, span, :].astype(F32).T.astype(BF16) for span in spans]
    items = [(b, head) for b in range(2) for head in range(heads)]

    def score(b, head):
        query = qkv_v[2, spans[b], :] * head_mask(head, width, SCALE)
        return dot_nt(qkv_v[3, spans[b], :], query) + bias[b]

    scores = score(*items[0])
    for index, (b, head) in enumerate(items):
        later = score(*items[index + 1]) if index + 1 < len(items) else None
        largest = jnp.max(scores, axis=0, keepdims=True)
        weights = jnp.exp(scores - largest)
        total = jnp.sum(weights, axis=0, keepdims=True)
        tt_v[b * heads + head] = largest + jnp.log(total)
        own = slice(head * HEAD_DIM, (head + 1) * HEAD_DIM)
        mixed = dot(v_tall[b][own, :], weights.astype(BF16))
        ot_v[b, own, :] = mixed * (1.0 / total)
        scores = later
    for b, span in enumerate(spans):
        o_v[span, :] = ot_v[b].T.astype(BF16)
    copies.start(ot_v, ot)
    copies.start(tt_v, tt)
    copies.start(o_v, o.at[slot])
    part[...] = dot(o_v[...], wo_v[...]).astype(BF16)
    for off, piece in zip(offs, (r0, r1, r23.at[0], r23.at[1])):
        copies.start(part.at[pl.ds(off, shard)], piece.at[0:shard])
    copies.finish()


def image_forward(tick, info, shard, micro, pieces, w, wo, gidc, gidr, stacks):
    n, d = pieces[0].shape
    rows = 4 * shard
    width = wo.shape[0]
    band = rows // 2
    heads = width // HEAD_DIM
    return run(
        image_forward_kernel,
        "image_forward",
        cost(
            2 * rows * d * width * 6 + 8 * heads * band * band * 256,
            2 * rows * d * 3 + 12 * rows * width + 12 * d * width,
            2 * heads * band * band,
        ),
        (tick, info),
        (*pieces, w, wo, gidc, gidr, *stacks),
        (
            shape_of((n, d), BF16),
            shape_of((n, d), BF16),
            shape_of((2, n, d), BF16),
            shape_of((5, rows, width), BF16),
            shape_of((2, width, band), F32),
            shape_of((2 * heads, 1, band), F32),
            shape_of((micro + 1, rows, d), BF16),
            shape_of((micro + 1, rows, width), BF16),
        ),
        [
            pltpu.VMEM((rows, d), BF16),
            pltpu.VMEM(w.shape, BF16),
            pltpu.VMEM(wo.shape, BF16),
            pltpu.VMEM(gidc.shape, jnp.int32),
            pltpu.VMEM(gidr.shape, jnp.int32),
            pltpu.VMEM((5, rows, width), BF16),
            pltpu.VMEM((2, width, band), F32),
            pltpu.VMEM((2 * heads, 1, band), F32),
            pltpu.VMEM((rows, width), BF16),
            pltpu.VMEM((rows, d), BF16),
        ],
        18,
        ((8, 6), (9, 7)) if stacks else (),
    )


def image_backward_kernel(tick, info, p0, p1, p2, p3, w, wo, gidc, gidr, qkv, ot, tt, dkv, *refs):
    refs = refs[-(5 + 18) :]
    r0, r1, r23, da, dd = refs[:5]
    (
        da_v, w_v, wo_v, gidc_v, gidr_v, qkv_v, ot_v, tt_v, dkv_v, do_v, d_v, part,
        dq_tall, k_tall, do_tall, dk_sum, dv_sum, sems,
    ) = refs[5:]
    copies = Copies(sems)
    rows, d = da_v.shape
    shard = rows // 4
    band = ot_v.shape[2]
    width = wo_v.shape[0]
    heads = width // HEAD_DIM
    slot = info[AT_STACK + tick[0]]
    offs = [pl.multiple_of(info[AT_SLOT + i] * shard, 16) for i in range(4)]
    loads = [
        copies.start(piece.at[0:shard], da_v.at[pl.ds(off, shard)])
        for off, piece in zip(offs, (p0, p1, p2, p3))
    ] + [copies.start(wo, wo_v)]
    more = [
        copies.start(a, b)
        for a, b in ((qkv, qkv_v), (gidc, gidc_v), (gidr, gidr_v), (tt, tt_v), (ot, ot_v))
    ]
    rest = [copies.start(a, b) for a, b in ((dkv, dkv_v), (w, w_v))]
    copies.wait(*loads)
    copies.start(da_v, da.at[slot])
    do_v[...] = dot_nt(da_v[...], wo_v[...]).astype(BF16)
    copies.wait(*more)
    for b in range(2):
        span = slice(b * band, (b + 1) * band)
        bias = jnp.where(gidc_v[span, :] == gidr_v[0:1, span], F32(0.0), F32(MASKED_SCORE))
        k_tall[...] = qkv_v[3, span, :].astype(F32).T.astype(BF16)
        do_tall[...] = do_v[span, :].astype(F32).T
        dk_sum[...] = jnp.zeros_like(dk_sum)
        dv_sum[...] = jnp.zeros_like(dv_sum)
        for head in range(heads):
            at = head * HEAD_DIM
            own = slice(at, at + HEAD_DIM)
            query = qkv_v[2, span, :] * head_mask(head, width, SCALE)
            grad = do_v[span, :] * head_mask(head, width, 1.0)
            scores = dot_nt(qkv_v[3, span, :], query) + bias
            weights = jnp.exp(scores - tt_v[b * heads + head])
            pulled = dot_nt(qkv_v[4, span, :], grad)
            delta = jnp.sum(do_tall[own, :] * ot_v[b, own, :], axis=0, keepdims=True)
            score_grad = (weights * (pulled - delta)).astype(BF16)
            dv_sum[...] += dot(weights.astype(BF16), grad)
            dk_sum[...] += dot(score_grad, query)
            dq_tall[own, :] = dot(k_tall[own, :], score_grad) * SCALE
        d_v[span, 2 * width : 3 * width] = dq_tall[...].T.astype(BF16)
        d_v[span, 3 * width : 4 * width] = dk_sum[...].astype(BF16)
        d_v[span, 4 * width :] = dv_sum[...].astype(BF16)
    copies.wait(*rest)
    d_v[:, 0:width] = dkv_v[0]
    d_v[:, width : 2 * width] = dkv_v[1]
    copies.start(d_v, dd.at[slot])
    part[...] = dot_nt(d_v[...], w_v[...]).astype(BF16)
    for off, piece in zip(offs, (r0, r1, r23.at[0], r23.at[1])):
        copies.start(part.at[pl.ds(off, shard)], piece.at[0:shard])
    copies.finish()


def image_backward(tick, info, shard, micro, pieces, w, wo, gidc, gidr, qkv, ot, tt, dkv, parts, stacks):
    n, d = pieces[0].shape
    rows = 4 * shard
    width = wo.shape[0]
    band = rows // 2
    heads = width // HEAD_DIM
    return run(
        image_backward_kernel,
        "image_backward",
        cost(
            2 * rows * d * width * 6 + 20 * heads * band * band * 256,
            2 * rows * d * 3 + 20 * rows * width + 12 * d * width,
            2 * heads * band * band,
        ),
        (tick, info),
        (*pieces, w, wo, gidc, gidr, qkv, ot, tt, dkv, *parts, *stacks),
        (
            shape_of((n, d), BF16),
            shape_of((n, d), BF16),
            shape_of((2, n, d), BF16),
            shape_of((micro + 1, rows, d), BF16),
            shape_of((micro + 1, rows, 5 * width), BF16),
        ),
        [
            pltpu.VMEM((rows, d), BF16),
            pltpu.VMEM(w.shape, BF16),
            pltpu.VMEM(wo.shape, BF16),
            pltpu.VMEM(gidc.shape, jnp.int32),
            pltpu.VMEM(gidr.shape, jnp.int32),
            pltpu.VMEM((5, rows, width), BF16),
            pltpu.VMEM((2, width, band), F32),
            pltpu.VMEM((2 * heads, 1, band), F32),
            pltpu.VMEM((2, rows, width), BF16),
            pltpu.VMEM((rows, width), BF16),
            pltpu.VMEM((rows, 5 * width), BF16),
            pltpu.VMEM((rows, d), BF16),
            pltpu.VMEM((width, band), F32),
            pltpu.VMEM((width, band), BF16),
            pltpu.VMEM((width, band), F32),
            pltpu.VMEM((band, width), F32),
            pltpu.VMEM((band, width), F32),
        ],
        18,
        ((12, 0), (13, 1), (14, 2)) + (((15, 3), (16, 4)) if stacks else ()),
    )


def query_blocks(rows, size):
    return [(at, min(size, rows - at)) for at in range(0, rows, size)]


def causal(scores, start, last_key):
    key_at = lax.broadcasted_iota(jnp.int32, scores.shape, 0)
    query_at = lax.broadcasted_iota(jnp.int32, (1, scores.shape[1]), 1) + start
    return jnp.where(key_at <= jnp.minimum(query_at, last_key), scores, F32(MASKED_SCORE))


def text_forward_kernel(skip, tick, info, p0, p1, p2, p3, w, wo, kv, *refs):
    refs = refs[-(8 + 11) :]
    r0, r1, r23, qkv, ot, tt, hy, o = refs[:8]
    hy_v, w_v, wo_v, kv_v, qkv_v, ot_v, tt_v, o_v, part, piece_v, sems = refs[8:]
    copies = Copies(sems)
    rows, d = hy_v.shape
    shard = rows // 4
    patches = kv_v.shape[1]
    width = kv_v.shape[2]
    heads = width // HEAD_DIM
    slot = info[AT_STACK + tick[0]]
    last_key = info[AT_LENGTH + tick[0]] - 1
    offs = [pl.multiple_of(info[AT_BLOCK + i] * shard, 8) for i in range(4)]
    loads = [
        copies.start(piece.at[skip:], piece_v.at[i]) for i, piece in enumerate((p0, p1, p2, p3))
    ] + [copies.start(w, w_v)]
    more = [copies.start(kv.at[0:2], kv_v)]
    rest = [copies.start(wo, wo_v)]
    copies.wait(*loads)
    for i, off in enumerate(offs):
        part[pl.ds(off, shard), :] = piece_v[i].astype(F32)
    hy_v[...] = part[...].astype(BF16)
    projected = dot(hy_v[...], w_v[...])
    for j in range(4):
        qkv_v[j] = projected[:, j * width : (j + 1) * width].astype(BF16)
    copies.start(hy_v, hy.at[slot])
    copies.start(qkv_v, qkv)
    copies.wait(*more)
    v_tall = [values.astype(F32).T.astype(BF16) for values in (qkv_v[2], kv_v[1])]
    items = [
        (kind, head, start, size)
        for kind in range(2)
        for start, size in query_blocks(rows, CROSS_BLOCK if kind else SELF_AHEAD)
        for head in range(heads)
    ]

    def score(kind, head, start, size):
        query = qkv_v[3 if kind else 0, start : start + size, :] * head_mask(head, width, SCALE)
        keys = kv_v[0] if kind else qkv_v[1, 0 : start + size, :]
        scores = dot_nt(keys, query)
        return scores if kind else causal(scores, start, last_key)

    scores = score(*items[0])
    for index, (kind, head, start, size) in enumerate(items):
        later = score(*items[index + 1]) if index + 1 < len(items) else None
        at = head * HEAD_DIM
        largest = jnp.max(scores, axis=0, keepdims=True)
        weights = jnp.exp(scores - largest)
        total = jnp.sum(weights, axis=0, keepdims=True)
        tt_v[kind * heads + head, :, start : start + size] = largest + jnp.log(total)
        mixed = dot(v_tall[kind][at : at + HEAD_DIM, 0 : weights.shape[0]], weights.astype(BF16))
        out_at = kind * width + at
        ot_v[out_at : out_at + HEAD_DIM, start : start + size] = mixed * (1.0 / total)
        scores = later
    copies.start(ot_v, ot)
    copies.start(tt_v, tt)
    o_v[...] = ot_v[...].T.astype(BF16)
    copies.start(o_v, o.at[slot])
    copies.wait(*rest)
    part[...] = dot(o_v[...], wo_v[...])
    for i, (off, piece) in enumerate(zip(offs, (r0, r1, r23.at[0], r23.at[1]))):
        piece_v[i] = part[pl.ds(off, shard), :].astype(BF16)
        copies.start(piece_v.at[i], piece.at[skip:])
    copies.finish()


def text_forward(tick, info, shard, micro, pieces, w, wo, kv, parts, stacks):
    n, d = pieces[0].shape
    rows = 4 * shard
    patches, width = kv.shape[1:]
    heads = width // HEAD_DIM
    return run(
        functools.partial(text_forward_kernel, n - shard),
        "text_forward",
        cost(
            2 * rows * d * width * 6 + 4 * heads * rows * (rows * 0.6 + patches) * 256,
            2 * rows * d * 3 + 12 * rows * width + 12 * d * width,
            heads * rows * (rows * 0.6 + patches),
        ),
        (tick, info),
        (*pieces, w, wo, kv, *parts, *stacks),
        (
            shape_of((n, d), BF16),
            shape_of((n, d), BF16),
            shape_of((2, n, d), BF16),
            shape_of((4, rows, width), BF16),
            shape_of((2 * width, rows), F32),
            shape_of((2 * heads, 1, rows), F32),
            shape_of((micro + 1, rows, d), BF16),
            shape_of((micro + 1, rows, 2 * width), BF16),
        ),
        [
            pltpu.VMEM((rows, d), BF16),
            pltpu.VMEM(w.shape, BF16),
            pltpu.VMEM(wo.shape, BF16),
            pltpu.VMEM((2, patches, width), BF16),
            pltpu.VMEM((4, rows, width), BF16),
            pltpu.VMEM((2 * width, rows), F32),
            pltpu.VMEM((2 * heads, 1, rows), F32),
            pltpu.VMEM((rows, 2 * width), BF16),
            pltpu.VMEM((rows, d), F32),
            pltpu.VMEM((4, shard, d), BF16),
        ],
        16,
        ((7, 0), (8, 1), (9, 2)) + (((10, 6), (11, 7)) if stacks else ()),
    )


def text_backward_kernel(skip, tick, info, p0, p1, p2, p3, w, wo, kv, qkv, ot, tt, *refs):
    refs = refs[-(6 + 18) :]
    r0, r1, r23, dkv, da, dd = refs[:6]
    (
        da_v, w_v, wo_v, kv_v, qkv_v, ot_v, tt_v, do_v, d_v, dkv_v, part, piece_v,
        dq_tall, k_tall, do_tall, dk_sum, dv_sum, sems,
    ) = refs[6:]
    copies = Copies(sems)
    rows, d = da_v.shape
    shard = rows // 4
    patches, width = kv_v.shape[1:]
    heads = width // HEAD_DIM
    slot = info[AT_STACK + tick[0]]
    last_key = info[AT_LENGTH + tick[0]] - 1
    offs = [pl.multiple_of(info[AT_BLOCK + i] * shard, 8) for i in range(4)]
    loads = [
        copies.start(piece.at[skip:], piece_v.at[i]) for i, piece in enumerate((p0, p1, p2, p3))
    ] + [copies.start(wo, wo_v)]
    more = [copies.start(a, b) for a, b in ((qkv, qkv_v), (tt, tt_v), (ot, ot_v), (kv.at[0:2], kv_v))]
    rest = [copies.start(w, w_v)]
    copies.wait(*loads)
    for i, off in enumerate(offs):
        part[pl.ds(off, shard), :] = piece_v[i].astype(F32)
    da_v[...] = part[...].astype(BF16)
    copies.start(da_v, da.at[slot])
    grads = dot_nt(da_v[...], wo_v[...])
    do_v[...] = grads.astype(BF16)
    do_tall[...] = grads.astype(BF16).astype(F32).T
    copies.wait(*more)
    for kind in range(2):
        span = patches if kind else rows
        whole_keys = kv_v[0] if kind else qkv_v[1]
        k_tall[:, 0:span] = whole_keys.astype(F32).T.astype(BF16)
        dk_sum[...] = jnp.zeros_like(dk_sum)
        dv_sum[...] = jnp.zeros_like(dv_sum)
        for start, size in query_blocks(rows, CROSS_BACK if kind else SELF_BLOCK):
            seen = start + size if kind == 0 else patches
            block = slice(start, start + size)
            keys = kv_v[0] if kind else qkv_v[1, 0:seen, :]
            values = kv_v[1] if kind else qkv_v[2, 0:seen, :]
            for head in range(heads):
                at = head * HEAD_DIM
                own = slice(at, at + HEAD_DIM)
                out_own = slice(kind * width + at, kind * width + at + HEAD_DIM)
                query = qkv_v[3 if kind else 0, block, :] * head_mask(head, width, SCALE)
                grad = do_v[block, kind * width : (kind + 1) * width] * head_mask(head, width, 1.0)
                scores = dot_nt(keys, query)
                if kind == 0:
                    scores = causal(scores, start, last_key)
                weights = jnp.exp(scores - tt_v[kind * heads + head, :, block])
                pulled = dot_nt(values, grad)
                delta = jnp.sum(do_tall[out_own, block] * ot_v[out_own, block], axis=0, keepdims=True)
                score_grad = (weights * (pulled - delta)).astype(BF16)
                dv_sum[0:seen, :] += dot(weights.astype(BF16), grad)
                dk_sum[0:seen, :] += dot(score_grad, query)
                dq_tall[own, block] = dot(k_tall[own, 0:seen], score_grad) * SCALE
        if kind == 0:
            d_v[:, 0:width] = dq_tall[...].T.astype(BF16)
            d_v[:, width : 2 * width] = dk_sum[...].astype(BF16)
            d_v[:, 2 * width : 3 * width] = dv_sum[...].astype(BF16)
        else:
            d_v[:, 3 * width :] = dq_tall[...].T.astype(BF16)
            dkv_v[0] = dk_sum[0:patches, :].astype(BF16)
            dkv_v[1] = dv_sum[0:patches, :].astype(BF16)
    copies.start(dkv_v, dkv)
    copies.start(d_v, dd.at[slot])
    copies.wait(*rest)
    part[...] = dot_nt(d_v[...], w_v[...])
    for i, (off, piece) in enumerate(zip(offs, (r0, r1, r23.at[0], r23.at[1]))):
        piece_v[i] = part[pl.ds(off, shard), :].astype(BF16)
        copies.start(piece_v.at[i], piece.at[skip:])
    copies.finish()


def text_backward(tick, info, shard, micro, pieces, w, wo, kv, qkv, ot, tt, stacks):
    n, d = pieces[0].shape
    rows = 4 * shard
    patches, width = kv.shape[1:]
    heads = width // HEAD_DIM
    return run(
        functools.partial(text_backward_kernel, n - shard),
        "text_backward",
        cost(
            2 * rows * d * width * 6 + 10 * heads * rows * (rows * 0.6 + patches) * 256,
            2 * rows * d * 3 + 20 * rows * width + 12 * d * width,
            heads * rows * (rows * 0.6 + patches),
        ),
        (tick, info),
        (*pieces, w, wo, kv, qkv, ot, tt, *stacks),
        (
            shape_of((n, d), BF16),
            shape_of((n, d), BF16),
            shape_of((2, n, d), BF16),
            shape_of((2, patches, width), BF16),
            shape_of((micro + 1, rows, d), BF16),
            shape_of((micro + 1, rows, 4 * width), BF16),
        ),
        [
            pltpu.VMEM((rows, d), BF16),
            pltpu.VMEM(w.shape, BF16),
            pltpu.VMEM(wo.shape, BF16),
            pltpu.VMEM((2, patches, width), BF16),
            pltpu.VMEM((4, rows, width), BF16),
            pltpu.VMEM((2 * width, rows), F32),
            pltpu.VMEM((2 * heads, 1, rows), F32),
            pltpu.VMEM((rows, 2 * width), BF16),
            pltpu.VMEM((rows, 4 * width), BF16),
            pltpu.VMEM((2, patches, width), BF16),
            pltpu.VMEM((rows, d), F32),
            pltpu.VMEM((4, shard, d), BF16),
            pltpu.VMEM((width, rows), F32),
            pltpu.VMEM((width, rows), BF16),
            pltpu.VMEM((2 * width, rows), F32),
            pltpu.VMEM((rows, width), F32),
            pltpu.VMEM((rows, width), F32),
        ],
        18,
        ((10, 4), (11, 5)) if stacks else (),
    )


def attention_weights_kernel(h, dd, o, da, out, w_sum, wo_sum):
    step = pl.program_id(0)
    w_part = dot_tn(h[0], dd[0])
    wo_part = dot_tn(o[0], da[0])

    @pl.when(step == 0)
    def _():
        w_sum[...] = w_part
        wo_sum[...] = wo_part

    @pl.when(step > 0)
    def _():
        w_sum[...] += w_part
        wo_sum[...] += wo_part

    @pl.when(step == pl.num_programs(0) - 1)
    def _():
        chunks = out.shape[0]
        d, columns = w_sum.shape
        rows, wide = d // chunks, wo_sum.shape[1]
        at = rows
        for z in range(chunks):
            out[z, 0:rows, :] = w_sum[z * rows : (z + 1) * rows, :].astype(BF16)
        narrow = d // 4 // chunks
        for part in range(wo_sum.shape[0] // (d // 4)):
            for z in range(chunks):
                top = part * (d // 4) + z * narrow
                out[z, at : at + narrow, 0:wide] = wo_sum[top : top + narrow, :].astype(BF16)
                if columns > wide:
                    out[z, at : at + narrow, wide:] = jnp.zeros((narrow, columns - wide), BF16)
            at += narrow


def attention_weights(h, dd, o, da, chunks, name):
    slots, rows, d = h.shape
    columns, wide = dd.shape[2], o.shape[2]
    out = (chunks, (d + wide) // chunks, columns)
    slot = lambda a: pl.BlockSpec((1, *a.shape[1:]), lambda i: (i, 0, 0))
    return pl.pallas_call(
        attention_weights_kernel,
        grid=(slots - 1,),
        out_shape=shape_of(out, BF16),
        in_specs=[slot(a) for a in (h, dd, o, da)],
        out_specs=whole(*out),
        scratch_shapes=[pltpu.VMEM((d, columns), F32), pltpu.VMEM((wide, d), F32)],
        compiler_params=params(),
        cost_estimate=cost(
            2 * slots * rows * d * (columns + wide), 2 * slots * rows * (2 * d + columns + wide)
        ),
        name=name,
    )(h, dd, o, da)


def ff_forward_kernel(ni, tick, info, x, a, b, c, gain, bias, u0, u1, u2, u3, d0, d1, d2, d3, *refs):
    refs = refs[-(7 + 11) :]
    mid, gp, z, h2, g, image_out, text_out = refs[:7]
    x_v, abc, norm, up, down, mid_v, h2_v, g_v, gp_v, z_v, sems = refs[7:]
    copies = Copies(sems)
    n, d = x_v.shape
    hidden = up.shape[2]
    slot = info[AT_STACK + tick[0]]
    at_row = pl.multiple_of(slot * n, 8)
    loads = [
        copies.start(s, t)
        for s, t in (
            (x, x_v),
            (a, abc.at[0]),
            (b.at[0], abc.at[1]),
            (c, abc.at[2]),
            (gain, norm.at[0]),
            (bias, norm.at[1]),
        )
    ]
    weights = [
        (copies.start(u, up.at[i]), copies.start(w, down.at[i]))
        for i, (u, w) in enumerate(zip((u0, u1, u2, u3), (d0, d1, d2, d3)))
    ]
    copies.wait(*loads)
    values = x_v[...].astype(F32) + (
        abc[0].astype(F32) + abc[1].astype(F32) + abc[2].astype(F32)
    )
    mid_v[...] = values
    unit, _ = normalized(values)
    h2_v[...] = (unit * norm[0, 1:2, :] + norm[1, 1:2, :]).astype(BF16)
    copies.start(mid_v, mid)
    copies.start(h2_v, h2.at[pl.ds(at_row, n)])

    def ascend(i):
        copies.wait(weights[i][0])
        return dot(h2_v[...], up[i])

    def bend(i, u):
        square = u * u
        bent = jnp.tanh(u * (GELU_C + (GELU_C * GELU_A) * square))
        half = 0.5 * (1.0 + bent)
        g_v[i] = (u * half).astype(BF16)
        slope = half + (0.5 * u) * (1.0 - bent * bent) * (GELU_C + (3.0 * GELU_C * GELU_A) * square)
        gp_v[i] = slope.astype(BF16)
        columns = slice(i * hidden, (i + 1) * hidden)
        copies.start(g_v.at[i], g.at[pl.ds(at_row, n), columns])
        copies.start(gp_v.at[i], gp.at[:, columns])

    total = mid_v[...]
    u = ascend(0)
    for i in range(4):
        bend(i, u)
        copies.wait(weights[i][1])
        total = total + dot(g_v[i], down[i])
        u = ascend(i + 1) if i < 3 else None
    z_v[...] = total.astype(BF16)
    copies.start(z_v, z)
    copies.finish()

    @pl.when(info[AT_VALID + tick[0]] > 0)
    def _():
        image_copy = pltpu.make_async_copy(z_v.at[0:ni], image_out.at[slot], sems.at[0])
        text_copy = pltpu.make_async_copy(z_v.at[ni:], text_out.at[slot], sems.at[1])
        image_copy.start()
        text_copy.start()
        image_copy.wait()
        text_copy.wait()


def ff_forward(tick, info, ni, micro, x, parts, gain, bias, up, down, stacks):
    n, d = x.shape
    hidden = up[0].shape[1]
    return run(
        functools.partial(ff_forward_kernel, ni),
        "ff_forward",
        cost(16 * n * d * hidden, 16 * d * hidden + 16 * n * hidden + 16 * n * d, 4 * n * hidden),
        (tick, info),
        (x, *parts, gain, bias, *up, *down, *stacks),
        (
            shape_of((n, d), F32),
            shape_of((n, 4 * hidden), BF16),
            shape_of((n, d), BF16),
            shape_of(((micro + 1) * n, d), BF16),
            shape_of(((micro + 1) * n, 4 * hidden), BF16),
            shape_of((micro, ni, d), BF16),
            shape_of((micro, n - ni, d), BF16),
        ),
        [
            pltpu.VMEM((n, d), BF16),
            pltpu.VMEM((3, n, d), BF16),
            pltpu.VMEM((2, 2, d), F32),
            pltpu.VMEM((4, d, hidden), BF16),
            pltpu.VMEM((4, hidden, d), BF16),
            pltpu.VMEM((n, d), F32),
            pltpu.VMEM((n, d), BF16),
            pltpu.VMEM((4, n, hidden), BF16),
            pltpu.VMEM((4, n, hidden), BF16),
            pltpu.VMEM((n, d), BF16),
        ],
        26,
        ((14, 3), (15, 4), (16, 5), (17, 6)) if stacks else (),
    )


def ff_backward_kernel(
    source, tick, info, coti, cott, back, gp, mid, gain, u0, u1, u2, u3, d0, d1, d2, d3, *refs
):
    refs = refs[-(5 + 13) :]
    dmid, da, sums, dm, du = refs[:5]
    cot_v, back_v, gp_v, mid_v, norm, up, down, rows, dm_v, du_v, da_v, sums_v, sems = refs[5:]
    copies = Copies(sems)
    n, d = mid_v.shape
    ni = coti.shape[1]
    nt = n - ni
    hidden = up.shape[2]
    valid = info[AT_VALID + tick[0]].astype(F32)
    slot = info[AT_STACK + tick[0]]
    at_row = pl.multiple_of(slot * n, 8)
    loads = [
        copies.start(coti.at[source], cot_v.at[0:ni]),
        copies.start(cott.at[source], cot_v.at[ni:]),
        copies.start(back, back_v),
    ]
    weights = []
    for i, (u, w) in enumerate(zip((u0, u1, u2, u3), (d0, d1, d2, d3))):
        columns = slice(i * hidden, (i + 1) * hidden)
        weights.append(
            (
                copies.start(w, down.at[i]),
                copies.start(gp.at[:, columns], gp_v.at[i]),
                copies.start(u, up.at[i]),
            )
        )
    rest = [copies.start(mid, mid_v), copies.start(gain, norm)]
    copies.wait(*loads)
    first = info[AT_SECTION] == 0
    place = lax.broadcasted_iota(jnp.int32, (nt, 1), 0) + info[AT_MP] * nt
    kept = (place < info[AT_LENGTH + tick[0]]).astype(F32)
    rows[0:ni, :] = jnp.where(first, back_v[0:ni, :].astype(F32), cot_v[0:ni, :].astype(F32))
    rows[ni:, :] = jnp.where(first, back_v[ni:, :].astype(F32), cot_v[ni:, :].astype(F32) * kept)
    dm_v[...] = rows[...].astype(BF16)
    copies.start(dm_v, dm.at[pl.ds(at_row, n)])

    def descend(i):
        copies.wait(weights[i][0])
        return dot_nt(dm_v[...], down[i])

    total = None
    act_grad = descend(0)
    for i in range(4):
        later = descend(i + 1) if i < 3 else None
        copies.wait(weights[i][1], weights[i][2])
        du_v[i] = (gp_v[i].astype(F32) * act_grad).astype(BF16)
        copies.start(du_v.at[i], du.at[pl.ds(at_row, n), i * hidden : (i + 1) * hidden])
        part = dot_nt(du_v[i], up[i])
        total = part if total is None else total + part
        act_grad = later
    copies.wait(*rest)
    pulled, gain_sum, bias_sum = norm_pull(total, mid_v[...], norm[1:2, :])
    total = rows[...] + pulled
    rows[...] = total
    da_v[...] = total.astype(BF16)
    sums_v[0:1, :] = gain_sum * valid
    sums_v[1:2, :] = bias_sum * valid
    copies.start(da_v, da)
    copies.start(rows, dmid)
    copies.start(sums_v, sums)
    copies.finish()


def ff_backward(tick, info, source, micro, coti, cott, back, gp, mid, gain, up, down, stacks):
    n, d = mid.shape
    hidden = up[0].shape[1]
    return run(
        functools.partial(ff_backward_kernel, source),
        "ff_backward",
        cost(16 * n * d * hidden, 16 * d * hidden + 16 * n * hidden + 16 * n * d),
        (tick, info),
        (coti, cott, back, gp, mid, gain, *up, *down, *stacks),
        (
            shape_of((n, d), F32),
            shape_of((n, d), BF16),
            shape_of((2, d), F32),
            shape_of(((micro + 1) * n, d), BF16),
            shape_of(((micro + 1) * n, 4 * hidden), BF16),
        ),
        [
            pltpu.VMEM((n, d), BF16),
            pltpu.VMEM((n, d), BF16),
            pltpu.VMEM((4, n, hidden), BF16),
            pltpu.VMEM((n, d), F32),
            pltpu.VMEM((2, d), F32),
            pltpu.VMEM((4, d, hidden), BF16),
            pltpu.VMEM((4, hidden, d), BF16),
            pltpu.VMEM((n, d), F32),
            pltpu.VMEM((n, d), BF16),
            pltpu.VMEM((4, n, hidden), BF16),
            pltpu.VMEM((n, d), BF16),
            pltpu.VMEM((2, d), F32),
        ],
        26,
        ((14, 3), (15, 4)) if stacks else (),
    )


def ff_weights_kernel(h2, dm, du, g, one, two):
    piece = pl.program_id(0)
    up_part = dot_tn(h2[...], du[...]).astype(BF16)
    down_part = dot_tn(g[...], dm[...]).astype(BF16)
    for index, out in enumerate((one, two)):

        @pl.when(piece == index)
        def _():
            chunks, rows = out.shape[0], out.shape[1] // 2
            for z in range(chunks):
                span = slice(z * rows, (z + 1) * rows)
                out[z, 0:rows, :] = up_part[span, :]
                out[z, rows:, :] = down_part[span, :]


def ff_weights(pieces, samples, h2, dm, du, g, chunks):
    d = h2.shape[1]
    hidden = du.shape[1] // 4
    n = h2.shape[0] // (samples + 1) * samples
    one, two = pieces
    part = (chunks, 2 * d // chunks, hidden)
    column = lambda i: one + (two - one) * i
    return pl.pallas_call(
        ff_weights_kernel,
        grid=(2,),
        out_shape=(shape_of(part, BF16),) * 2,
        in_specs=[
            whole(n, d),
            whole(n, d),
            pl.BlockSpec((n, hidden), lambda i: (0, column(i))),
            pl.BlockSpec((n, hidden), lambda i: (0, column(i))),
        ],
        out_specs=(whole(*part), whole(*part)),
        compiler_params=params(),
        cost_estimate=cost(8 * n * d * hidden, 4 * n * d + 8 * n * hidden + 8 * d * hidden),
        name="ff_weights",
    )(h2, dm, du, g)


def close_kernel(ni, tick, info, x, a, b, c, dmid, gain, *refs):
    refs = refs[-(4 + 8) :]
    back, sums, image_grad, text_grad = refs[:4]
    x_v, abc, dmid_v, norm, total_v, back_v, sums_v, sems = refs[4:]
    copies = Copies(sems)
    n = x_v.shape[0]
    slot = info[AT_STACK + tick[0]]
    valid = info[AT_VALID + tick[0]]
    ready = copies.start(gain, norm)
    spans = (slice(0, ni), slice(ni, n))
    loads = [
        [
            copies.start(source.at[span], target.at[span])
            for source, target in (
                (a, abc.at[0]),
                (b.at[0], abc.at[1]),
                (c, abc.at[2]),
                (x, x_v),
                (dmid, dmid_v),
            )
        ]
        for span in spans
    ]
    copies.wait(ready)
    gain_total = bias_total = None
    for index, (span, load) in enumerate(zip(spans, loads)):
        copies.wait(*load)
        grad = abc[0, span, :].astype(F32) + abc[1, span, :].astype(F32) + abc[2, span, :].astype(F32)
        pulled, gain_sum, bias_sum = norm_pull(grad, x_v[span, :].astype(F32), norm[0:1, :])
        total = dmid_v[span, :] + pulled
        total_v[span, :] = total
        back_v[span, :] = total.astype(BF16)
        copies.start(back_v.at[span], back.at[span])
        out = (image_grad, text_grad)[index]
        copy = pltpu.make_async_copy(total_v.at[span], out.at[slot], sems.at[16 + index])

        @pl.when(valid > 0)
        def _():
            copy.start()

        gain_total = gain_sum if index == 0 else gain_total + gain_sum
        bias_total = bias_sum if index == 0 else bias_total + bias_sum
    sums_v[0:1, :] = gain_total * valid.astype(F32)
    sums_v[1:2, :] = bias_total * valid.astype(F32)
    copies.start(sums_v, sums)
    copies.finish()
    for index, (span, out) in enumerate(zip(spans, (image_grad, text_grad))):

        @pl.when(valid > 0)
        def _():
            pltpu.make_async_copy(total_v.at[span], out.at[slot], sems.at[16 + index]).wait()


def close(tick, info, ni, micro, x, parts, dmid, gain, stacks):
    n, d = x.shape
    return run(
        functools.partial(close_kernel, ni),
        "input_grad",
        cost(20 * n * d, 18 * n * d),
        (tick, info),
        (x, *parts, dmid, gain, *stacks),
        (
            shape_of((n, d), BF16),
            shape_of((2, d), F32),
            shape_of((micro, ni, d), F32),
            shape_of((micro, n - ni, d), F32),
        ),
        [
            pltpu.VMEM((n, d), BF16),
            pltpu.VMEM((3, n, d), BF16),
            pltpu.VMEM((n, d), F32),
            pltpu.VMEM((2, d), F32),
            pltpu.VMEM((n, d), F32),
            pltpu.VMEM((n, d), BF16),
            pltpu.VMEM((2, d), F32),
        ],
        18,
        ((6, 2), (7, 3)) if stacks else (),
    )


def over_y(array):
    return lax.ppermute(array, "mp", [(m, m ^ 2) for m in range(4)])


def over_core(array):
    return lax.ppermute(array, "mp", [(m, m ^ 1) for m in range(4)])


def gathered(own, across=None):
    across = over_y(own) if across is None else across
    return (own, across, over_core(own), over_core(across))


def for_y(r1, r23):
    other = over_core(r23)
    return other, (r1.astype(F32) + other[1].astype(F32)).astype(BF16)


def shifted(array, by):
    length = lax.axis_size("section")
    return lax.ppermute(array, "section", [(i, i + by) for i in range(length) if 0 <= i + by < length])


def over_everyone(sums):
    groups = lax.axis_size("dp")
    if groups & (groups - 1):
        return lax.psum_scatter(sums, ("dp", "mp"), scatter_dimension=2, tiled=True)
    for flip in (1, 2):
        sums = sums + lax.ppermute(sums, "mp", [(m, m ^ flip) for m in range(4)])
    flip = 1
    while flip < groups:
        sums = sums + lax.ppermute(sums, "dp", [(z, z ^ flip) for z in range(groups)])
        flip *= 2
    own = sums.shape[2] // (4 * groups)
    mine = lax.axis_index("dp") * 4 + lax.axis_index("mp")
    return lax.dynamic_slice_in_dim(sums, mine * own, own, axis=2)


def hold(values, *earlier):
    return lax.optimization_barrier((tuple(values), *earlier))[0]


def shards(
    image, text, lengths, image_cot, text_cot, qkv_image, out_image, qkv_text, out_text,
    query_cross, kv_cross, out_cross, up_proj, down_proj, norm_gain, norm_bias,
):
    section = lax.axis_index("section")
    me = lax.axis_index("mp")
    groups = lax.axis_size("dp")
    micro = image.shape[0]
    ticks = micro + SKEW
    ni, d = image.shape[1:]
    nt = text.shape[1]
    gain, bias = norm_gain[0], norm_bias[0]
    width = out_image.shape[1]
    w_image = jnp.concatenate(
        (kv_cross[0].reshape(d, 2 * width), qkv_image[0].reshape(d, 3 * width)), axis=1
    )
    w_text = jnp.concatenate((qkv_text[0].reshape(d, 3 * width), query_cross[0]), axis=1)
    wo_image = out_image[0]
    wo_text = jnp.concatenate((out_text[0], out_cross[0]), axis=0)

    flips = jnp.array(FLIPS, jnp.int32)
    turn = jnp.arange(ticks) - section * SKEW
    valid = (turn >= 0) & (turn < micro)
    gap = jnp.zeros((16 - ticks,), jnp.int32)
    info = jnp.concatenate(
        (
            ((me ^ flips) - section) % 4,
            me ^ flips,
            jnp.stack((section, me)).astype(jnp.int32),
            jnp.zeros((AT_LENGTH - 10,), jnp.int32),
            lengths[jnp.clip(turn, 0, micro - 1)],
            gap,
            valid.astype(jnp.int32),
            gap,
            jnp.where(valid, turn, micro).astype(jnp.int32),
        )
    ).astype(jnp.int32)
    place = jnp.arange(4 * ni)
    turned = (place % PATCH_COLS - section * SHIFT) % PATCH_COLS
    edge = PATCH_ROWS - section * SHIFT
    row_region = (place // PATCH_COLS >= PATCH_ROWS - WIN).astype(jnp.int32) + (
        place // PATCH_COLS >= edge
    ).astype(jnp.int32)
    col_region = (turned >= PATCH_COLS - WIN).astype(jnp.int32) + (turned >= edge).astype(jnp.int32)
    region = row_region * 3 + col_region
    gidc = region[:, None]
    gidr = region[None, :]

    tick_at = [jnp.full((1,), t, jnp.int32) for t in range(ticks)]
    nothing = jnp.zeros((ni + nt, d), BF16)
    up = down = None
    image_stacks = text_stacks = ff_stacks = ()
    state = {}
    relayed = {}
    ahead = {}

    def attend(t):
        nonlocal image_stacks, text_stacks, up, down
        got = relayed.get(t - SKEW, nothing)
        if t >= SKEW and t % SKEW == 0:
            got = hold((got,), ahead["out"])[0]
        elif t % SKEW > 0:
            got = hold((got,), ahead["h"])[0]
        x, h = entry(tick_at[t], info, min(t, micro - 1), image, text, got, gain, bias)
        ahead["h"] = h
        pieces = gathered(h)
        if up is None:
            up_own, down_own, _ = lax.optimization_barrier((up_proj[0], down_proj[0], pieces[1]))
            up = gathered(up_own)
            part = down_own.shape[0] // groups
            own_part = lax.dynamic_slice_in_dim(down_own, lax.axis_index("dp") * part, part, axis=0)
            part = over_y(own_part)
        second = t % SKEW > 0
        if second:
            pieces = hold(pieces, ahead["own"])
        r0, r1, r23, qkvi, oti, tti, hx, oi = image_forward(
            tick_at[t], info, ni, micro, pieces, w_image, wo_image, gidc, gidr, image_stacks
        )
        image_stacks = (hx, oi)
        if second and t > SKEW:
            r0, r1, r23 = hold((r0, r1, r23), ahead["across"])
        r0, r1, r23, qkvt, ott, ttt, hy, o = text_forward(
            tick_at[t], info, nt, micro, pieces, w_text, wo_text, qkvi, (r0, r1, r23), text_stacks
        )
        text_stacks = (hy, o)
        state[t] = [x, qkvi, oti, tti, qkvt, ott, ttt]
        other, across = for_y(r1, r23)
        ahead.update(own=r0, across=across)
        if down is None:
            part = lax.all_gather(hold((part,), r0)[0], "dp", axis=0, tiled=True)
            down = gathered(down_own, part)
        return (r0, other, over_y(across))

    def feed(t, parts):
        nonlocal ff_stacks
        x = hold((state[t][0],), ahead["out"])[0] if t % SKEW > 0 else state[t][0]
        mid, gp, z, *ff_stacks = ff_forward(
            tick_at[t], info, ni, micro, x, parts, gain, bias, up, down, ff_stacks
        )
        state[t] += [mid, gp]
        ahead["out"] = z
        if t + SKEW < ticks:
            relayed[t] = shifted(z, 1)

    for t in range(0, ticks, SKEW):
        sums = [attend(t + i) for i in range(SKEW)]
        for i in range(SKEW):
            feed(t + i, sums[i])
    h2, g, image_result, text_result = ff_stacks

    sums_one = sums_two = jnp.zeros((2, d), F32)
    relayed = {}
    ff_stacks = text_back = image_back = close_stacks = ()
    ahead = {}

    def descend(k):
        nonlocal ff_stacks, sums_two
        t = ticks - 1 - k
        mid, gp = state[t][7:9]
        back = relayed.get(k - SKEW, nothing)
        if k >= SKEW and k % SKEW == 0:
            back = hold((back,), ahead["out"])[0]
        elif k % SKEW > 0:
            back = hold((back,), ahead["da"])[0]
        dmid, da, sums, *ff_stacks = ff_backward(
            tick_at[t], info, max(t - SKEW, 0), micro, image_cot, text_cot, back, gp, mid, gain,
            up, down, ff_stacks,
        )
        sums_two = sums_two + sums
        ahead["da"] = da
        return dmid, da, over_y(da)

    def text_part(k, pieces):
        nonlocal text_back
        t = ticks - 1 - k
        qkvi, _, _, qkvt, ott, ttt = state[t][1:7]
        r0, r1, r23, dkv, *text_back = text_backward(
            tick_at[t], info, nt, micro, pieces, w_text, wo_text, qkvi, qkvt, ott, ttt, text_back
        )
        return (r0, r1, r23), dkv

    def image_part(k, pieces, parts, dkv):
        nonlocal image_back
        t = ticks - 1 - k
        qkvi, oti, tti = state[t][1:4]
        r0, r1, r23, *image_back = image_backward(
            tick_at[t], info, ni, micro, pieces, w_image, wo_image, gidc, gidr, qkvi, oti, tti, dkv,
            parts, image_back,
        )
        other, across = for_y(r1, r23)
        return r0, other, across

    def finish(k, parts, dmid):
        nonlocal close_stacks, sums_one
        t = ticks - 1 - k
        if k % SKEW > 0:
            dmid = hold((dmid,), ahead["out"])[0]
        back, sums, *close_stacks = close(
            tick_at[t], info, ni, micro, state[t][0], parts, dmid, gain, close_stacks
        )
        sums_one = sums_one + sums
        ahead["out"] = back
        if k + SKEW < ticks:
            relayed[k] = shifted(back, -1)

    final = ticks - SKEW
    fed = {}
    for k in range(final):
        second = k % SKEW > 0
        if not second:
            fed = {k + i: descend(k + i) for i in range(SKEW)}
        dmid, da, across = fed[k]
        across = hold((across,), ahead["text"] if second else ahead["da"])[0]
        pieces = gathered(da, across)
        if second:
            pieces = hold(pieces, ahead["own"])
        parts, dkv = text_part(k, pieces)
        ahead["text"] = parts[0]
        if second:
            parts = hold(parts, ahead["crossed"])
        r0, other, across = image_part(k, pieces, parts, dkv)
        crossed = over_y(across)
        ahead.update(own=r0, crossed=crossed)
        fed[k] = (k, (r0, other, crossed), dmid)
        if k % SKEW == SKEW - 1:
            for i in range(k - SKEW + 1, k + 1):
                finish(*fed[i])

    one, two = final, final + 1
    (dmid_one, da_one, a_one), (dmid_two, da_two, a_two) = descend(one), descend(two)
    pieces_one = gathered(da_one, *hold((a_one,), da_two))
    parts_one, dkv_one = text_part(one, pieces_one)
    pieces_two = hold(gathered(da_two, *hold((a_two,), parts_one[0])), parts_one[0])
    parts_two, dkv_two = text_part(two, pieces_two)
    dm, du = hold(ff_stacks, parts_two[0])
    far, y_part = ff_weights((3, 1), micro, h2, dm, du, g, groups)
    text_all = hold((*text_stacks, *text_back), far)
    text_w = attention_weights(
        text_all[0], text_all[3], text_all[1], text_all[2], groups, "text_weights"
    )
    parts_one = hold(parts_one, text_w)
    r0_one, other_one, across_one = image_part(one, pieces_one, parts_one, dkv_one)
    ff_across = (y_part.astype(F32) + over_core(far).astype(F32)).astype(BF16)
    parts_two = hold(parts_two, r0_one, ff_across)
    r0_two, other_two, across_two = image_part(two, pieces_two, parts_two, dkv_two)
    quarter = ff_across.shape[1] // 4
    crossed = [over_y(ff_across[:, i * quarter : (i + 1) * quarter]) for i in range(4)]
    image_stacks = hold((*image_stacks, *image_back), crossed[0], across_one)
    image_w = attention_weights(
        image_stacks[0], image_stacks[3], image_stacks[1], image_stacks[2], groups, "image_weights"
    )
    du = hold((du,), image_w, crossed[1], across_two)[0]
    near, core_part = ff_weights((0, 2), micro, h2, dm, du, g, groups)
    core_part = hold((core_part,), crossed[2])[0]
    dmid_one = hold((dmid_one,), near)[0]
    dmid_two = hold((dmid_two,), crossed[3])[0]
    finish(one, (r0_one, other_one, over_y(across_one)), dmid_one)
    finish(two, (r0_two, other_two, over_y(across_two)), dmid_two)
    ff_sum = (
        near.astype(F32) + over_core(core_part).astype(F32) + jnp.concatenate(crossed, axis=1).astype(F32)
    ).astype(BF16)

    def over_dp(array):
        return lax.psum_scatter(array, "dp", scatter_dimension=0, tiled=True)[0].astype(F32)

    ff_grad = over_dp(ff_sum)
    text_grad = over_dp(text_w)
    image_grad = over_dp(image_w)
    rows, wo_rows = d // groups, width // groups
    gain_grad, bias_grad = over_everyone(jnp.stack((sums_one, sums_two), axis=1))
    return (
        image_result[None],
        text_result[None],
        close_stacks[0][None],
        close_stacks[1][None],
        image_grad[:rows, 2 * width :].reshape(1, rows, 3, width),
        image_grad[rows:, :d][None],
        text_grad[:rows, : 3 * width].reshape(1, rows, 3, width),
        text_grad[rows : rows + wo_rows, :d][None],
        text_grad[:rows, 3 * width :][None],
        image_grad[:rows, : 2 * width].reshape(1, rows, 2, width),
        text_grad[rows + wo_rows :, :d][None],
        ff_grad[:rows][None],
        ff_grad[rows:][None],
        gain_grad[None],
        bias_grad[None],
    )


def solution(mesh):
    return jax.shard_map(
        shards,
        mesh=mesh,
        in_specs=(
            P("dp", "mp", None),
            P("dp", "mp", None),
            P("dp"),
            P("dp", "mp", None),
            P("dp", "mp", None),
            P("section", None, None, "mp"),
            P("section", "mp", None),
            P("section", None, None, "mp"),
            P("section", "mp", None),
            P("section", None, "mp"),
            P("section", None, None, "mp"),
            P("section", "mp", None),
            P("section", None, "mp"),
            P("section", "mp", None),
            P("section", None, None),
            P("section", None, None),
        ),
        out_specs=(
            P("section", "dp", "mp", None),
            P("section", "dp", "mp", None),
            P("section", "dp", "mp", None),
            P("section", "dp", "mp", None),
            P("section", "dp", None, "mp"),
            P("section", ("mp", "dp"), None),
            P("section", "dp", None, "mp"),
            P("section", ("mp", "dp"), None),
            P("section", "dp", "mp"),
            P("section", "dp", None, "mp"),
            P("section", ("mp", "dp"), None),
            P("section", "dp", "mp"),
            P("section", ("mp", "dp"), None),
            P("section", None, ("dp", "mp")),
            P("section", None, ("dp", "mp")),
        ),
        check_vma=False,
    )
```
